32 devices in a mesh: seq: 8 (over z, y), head: 4 (over x, core).
Axes of the slice: x: 2, y: 2, z: 4, core: 2. Of those that a mesh axis runs over, the one named last changes fastest.
Arguments:
- tokens: bfloat16 [2048, 4096], P('seq', 'head'), may hold values from -6 to 6
- light_input: bfloat16 [3, 4096, 1024], P(None, None, 'head'), may hold values from -14 to 14
- light_output: bfloat16 [1024, 4096], P('head'), may hold values from -0.75 to 0.75
- heavy_input: bfloat16 [3, 4096, 4096], P(None, 'seq', 'head'), may hold values from -14 to 14
- heavy_output: bfloat16 [4096, 4096], P('head', 'seq'), may hold values from -0.75 to 0.75
- query_tokens: int32 [8, 32], replicated, may hold values from -1 to 255, as said below
- context_tokens: int32 [8, 32], replicated, may hold values from -1 to 255, as said below
- query_gate: float32 [8, 32], P('seq'), may hold values from 0.25 to 2
Outputs:
- mixed: bfloat16 [2048, 4096], P('seq', 'head')
The draws below stay inside these ranges and needn't reach their ends.
Inputs may be any that keep to these rules, and one draw needn't show every extreme that they name: `query_tokens`: row s lists, in its first entries, distinct positions within sequence shard s of routed query tokens, and -1 after them; 64 positions are listed over all rows, at most 32 in a row, and exactly 32 in some row. `context_tokens`: row s lists, in its first entries, distinct positions within sequence shard s of routed key-value tokens, and -1 after them; 64 positions are listed over all rows, at most 32 in a row, and exactly 32 in some row.
All inputs are finite; a program needn't handle non-finite values.
Results may differ from the reference program's by a relative error of at most 0.012.
Values may be sent and summed in bfloat16 or wider, within the bound.
No kernel may reach another device: no remote copies, remote signals or barrier semaphores. Data moves between devices by JAX's collectives and lax.ppermute only.
A program may use at most 64 MiB of HBM per device.

```python
import math
import jax
import jax.numpy as jnp
from jax import lax

TOK_DEV = 256
D = 4096
HD = 128
LH = 8
HH = 32
LB = 128
LW = 1024
HW = 4096
CQ = 32
TOKENS = 2048
ROUTED = 64
N_SEQ = 8


def shard_places(subkey):
    return jax.random.permutation(subkey, TOK_DEV)[:CQ]


def route_table(key, salt):
    streams = jax.random.split(jax.random.fold_in(key, salt), 5)
    shard_total = TOKENS // TOK_DEV
    groups = shard_total // 4
    first_count = jax.random.randint(streams[0], (groups,), 0, CQ // 2 + 1)
    second_count = jax.random.randint(streams[1], (groups,), 0, (CQ - first_count) // 2 + 1)
    third_count = jax.random.randint(streams[2], (groups,), 0, (CQ - first_count - second_count) // 2 + 1)
    leading = jnp.arange(groups) == 0
    first_count = jnp.where(leading, 0, first_count)
    second_count = jnp.where(leading, 0, second_count)
    third_count = jnp.where(leading, 0, third_count)
    fourth_count = CQ - first_count - second_count - third_count
    counts = jnp.stack([first_count, second_count, third_count, fourth_count], axis=1).reshape(shard_total)
    counts = jnp.take(counts, jax.random.permutation(streams[3], shard_total))
    places = jax.vmap(shard_places)(jax.random.split(streams[4], shard_total))
    position = jnp.arange(CQ)[None, :]
    return jnp.where(position < counts[:, None], places, -1).astype(jnp.int32)


def drawn_weights(key, salt, width):
    streams = jax.random.split(jax.random.fold_in(key, salt), 1)
    fan_scale = 1.0 / math.sqrt(D)
    return jnp.clip(jax.random.normal(streams[0], (3, D, width), jnp.float32), -6.0, 6.0) * fan_scale


def draw_tokens(key, part):
    streams = jax.random.split(jax.random.fold_in(key, 5), 1)
    return jnp.clip(jax.random.normal(streams[0], (TOKENS, D), jnp.float32), -6.0, 6.0).astype(jnp.bfloat16)


def draw_light_input(key, part):
    return drawn_weights(key, 3, LH * HD).astype(jnp.bfloat16)


def draw_heavy_input(key, part):
    return drawn_weights(key, 4, HH * HD).astype(jnp.bfloat16)


def draw_query_tokens(key, part):
    return route_table(key, 11)


def draw_context_tokens(key, part):
    return route_table(key, 23)


def shard_levels(own_key, shape, shards, least, high):
    gain, own = 1.0, jax.random.fold_in(own_key, 6)
    for dim, parts in shards:
        draws = jnp.exp(jax.random.uniform(jax.random.fold_in(own, dim), (parts,), jnp.float32, least / len(shards), high / len(shards)))
        gain = gain * jnp.repeat(draws, shape[dim] // parts).reshape([-1 if axis == dim else 1 for axis in range(len(shape))])
    return gain


def normal_values(key, extent, deviation, reach, cuts=(), kind=jnp.bfloat16):
    entries = jax.random.normal(key, extent, jnp.float32) * deviation
    if len(cuts) > 0:
        entries = shard_levels(key, extent, cuts, -0.22, 0.18) * entries
    return jnp.clip(entries, min=-reach, max=reach).astype(kind)


def setup_inputs(seed: int = 0) -> dict:
    keys = jax.random.split(jax.random.key(seed), 9)
    return {
        "tokens": draw_tokens(jax.random.fold_in(keys[8], 71), 0),
        "light_input": draw_light_input(jax.random.fold_in(keys[8], 71), 0),
        "light_output": normal_values(keys[2], (LW, D), (LW // 16) ** -0.5, 0.75, ((0, 4),)),
        "heavy_input": draw_heavy_input(jax.random.fold_in(keys[8], 71), 0),
        "heavy_output": normal_values(keys[4], (HW, D), (HW // 64) ** -0.5, 0.75, ((0, 4), (1, 8))),
        "query_tokens": draw_query_tokens(jax.random.fold_in(keys[8], 71), 0),
        "context_tokens": draw_context_tokens(jax.random.fold_in(keys[8], 71), 0),
        "query_gate": jnp.clip(jnp.exp(math.log(2.0) - 2.0794415 * jax.random.uniform(keys[7], (N_SEQ, CQ), jnp.float32) ** shard_levels(keys[7], (N_SEQ, CQ), ((0, 8),), -0.2, 0.2)), 0.25, 2.0),
    }


def attend(queries, key_rows, value_rows):
    scores = jnp.einsum('bqhe,bkhe->bhqk', queries.astype(jnp.float32), key_rows.astype(jnp.float32)) / math.sqrt(queries.shape[-1])
    highest = lax.optimization_barrier(jnp.max(scores, axis=-1, keepdims=True))
    expanded = jnp.exp(scores - highest)
    totals = lax.optimization_barrier(jnp.sum(expanded, axis=-1))
    rounded = lax.optimization_barrier(expanded.astype(jnp.bfloat16))
    weighted = jnp.einsum('bhqk,bkhe->bqhe', rounded.astype(jnp.float32), value_rows.astype(jnp.float32))
    return (weighted / jnp.transpose(totals, (0, 2, 1))[..., None]).astype(jnp.bfloat16)

def routed_list(table):
    counts = lax.optimization_barrier(jnp.sum((table >= 0).astype(jnp.int32), axis=1))
    upper_end = jnp.cumsum(counts).astype(jnp.int32)
    lower_end = (upper_end - counts).astype(jnp.int32)
    compact_rows = jnp.arange(ROUTED, dtype=jnp.int32)
    source_shard = lax.optimization_barrier(jnp.sum((upper_end[None, :] <= compact_rows[:, None]).astype(jnp.int32), axis=1)).astype(jnp.int32)
    within = (compact_rows - lower_end[source_shard]).astype(jnp.int32)
    positions = (source_shard * TOK_DEV + table[source_shard, within]).astype(jnp.int32)
    return (source_shard, within, positions)

def reference(tokens, light_input, light_output, heavy_input, heavy_output, query_tokens, context_tokens, query_gate):
    light_mapped = jnp.stack([jnp.dot(tokens, light_input[c], preferred_element_type=jnp.float32).astype(jnp.bfloat16) for c in range(3)])
    light_blocks = light_mapped.reshape(3, TOKENS // LB, LB, LH, HD)
    light_heads = attend(light_blocks[0], light_blocks[1], light_blocks[2]).reshape(TOKENS, LH * HD)
    light_update = jnp.dot(light_heads, light_output, preferred_element_type=jnp.float32)
    query_shard, query_within, query_list = routed_list(query_tokens)
    context_list = routed_list(context_tokens)[2]
    query_rows = tokens[query_list]
    context_rows = tokens[context_list]
    heavy_queries = jnp.dot(query_rows, heavy_input[0], preferred_element_type=jnp.float32).astype(jnp.bfloat16)
    heavy_keys = jnp.dot(context_rows, heavy_input[1], preferred_element_type=jnp.float32).astype(jnp.bfloat16)
    heavy_values = jnp.dot(context_rows, heavy_input[2], preferred_element_type=jnp.float32).astype(jnp.bfloat16)
    heavy_heads = attend(heavy_queries.reshape(1, ROUTED, HH, HD), heavy_keys.reshape(1, ROUTED, HH, HD), heavy_values.reshape(1, ROUTED, HH, HD)).reshape(ROUTED, HH * HD)
    heavy_update = jnp.dot(heavy_heads, heavy_output, preferred_element_type=jnp.float32)
    gate_values = query_gate[query_shard, query_within]
    mixed = light_update.at[query_list].add(gate_values[:, None] * heavy_update)
    return mixed.astype(jnp.bfloat16)
```

```python
import math

import jax
import jax.numpy as jnp
from jax import lax
from jax.sharding import PartitionSpec as P

HD = 128
LB = 128
ROUTE = 32


def attend(queries, key_rows, value_rows):
    scores = jnp.einsum(
        "bqhe,bkhe->bhqk", queries, key_rows, preferred_element_type=jnp.float32
    ) / math.sqrt(queries.shape[-1])
    highest = jnp.max(scores, axis=-1, keepdims=True)
    expanded = jnp.exp(scores - highest)
    totals = jnp.sum(expanded, axis=-1)
    weighted = jnp.einsum(
        "bhqk,bkhe->bqhe",
        expanded.astype(jnp.bfloat16),
        value_rows,
        preferred_element_type=jnp.float32,
    )
    return (weighted / jnp.transpose(totals, (0, 2, 1))[..., None]).astype(jnp.bfloat16)


def routed_map(table, routed):
    counts = jnp.sum((table >= 0).astype(jnp.int32), axis=1)
    shard = jnp.arange(table.shape[0], dtype=jnp.int32)
    upper_end = jnp.sum(jnp.where(shard[None, :] <= shard[:, None], counts[None, :], 0), axis=1)
    lower_end = upper_end - counts
    compact_rows = jnp.arange(routed, dtype=jnp.int32)
    source_shard = jnp.sum((upper_end[None, :] <= compact_rows[:, None]).astype(jnp.int32), axis=1)
    onehot_shard = (
        source_shard[:, None] == jnp.arange(table.shape[0], dtype=jnp.int32)[None, :]
    ).astype(jnp.int32)
    within = compact_rows - jnp.sum(onehot_shard * lower_end[None, :], axis=1)
    return (source_shard * table.shape[1] + within, lower_end)


def project(query_part, source_part, weights):
    stacked = jnp.stack((query_part, source_part, source_part))
    return jnp.einsum("cmd,cdw->mcw", stacked, weights, preferred_element_type=jnp.float32)


def pick_rows(gathered, own_list):
    chosen = jnp.take(gathered, jnp.maximum(own_list, 0), axis=0)
    return jnp.where((own_list >= 0)[:, None], chosen, jnp.zeros_like(chosen))


def per_device(
    tokens,
    light_input,
    light_output,
    heavy_input,
    heavy_output,
    query_tokens,
    context_tokens,
    query_gate,
):
    gathered = lax.all_gather(tokens, "head", axis=1, tiled=True)
    tok_rows = gathered.shape[0]
    light_mapped = jnp.einsum(
        "td,cdw->ctw", gathered, light_input, preferred_element_type=jnp.float32
    ).astype(jnp.bfloat16)
    light_blocks = light_mapped.reshape(3, tok_rows // LB, LB, -1, HD)
    light_heads = attend(light_blocks[0], light_blocks[1], light_blocks[2]).reshape(tok_rows, -1)
    light_part = jnp.dot(light_heads, light_output, preferred_element_type=jnp.float32)
    seq_count = lax.axis_size("seq")
    routed = seq_count * tok_rows // ROUTE
    slot_count = query_tokens.shape[1]
    seq_index = lax.axis_index("seq")
    own_queries = lax.dynamic_index_in_dim(query_tokens, seq_index, 0, keepdims=False)
    own_sources = lax.dynamic_index_in_dim(context_tokens, seq_index, 0, keepdims=False)
    query_cols, source_cols = (
        lax.all_to_all(
            pick_rows(gathered, own_queries), "seq", split_axis=1, concat_axis=0, tiled=True
        ),
        lax.all_to_all(
            pick_rows(gathered, own_sources), "seq", split_axis=1, concat_axis=0, tiled=True
        ),
    )
    query_index, query_lower = routed_map(query_tokens, routed)
    source_index = routed_map(context_tokens, routed)[0]
    query_rows = jnp.take(query_cols, query_index, axis=0)
    source_rows = jnp.take(source_cols, source_index, axis=0)
    summed = lax.psum(project(query_rows, source_rows, heavy_input), "seq").astype(jnp.bfloat16)
    heavy_heads = attend(
        summed[:, 0].reshape(1, routed, -1, HD),
        summed[:, 1].reshape(1, routed, -1, HD),
        summed[:, 2].reshape(1, routed, -1, HD),
    ).reshape(routed, -1)
    heavy_part = jnp.dot(heavy_heads, heavy_output, preferred_element_type=jnp.float32)
    slot_live = query_tokens >= 0
    compact = query_lower[:, None] + jnp.arange(slot_count, dtype=jnp.int32)[None, :]
    outgoing = jnp.take(heavy_part, jnp.where(slot_live, compact, 0).reshape(-1), axis=0)
    outgoing = jnp.where(slot_live.reshape(-1)[:, None], outgoing, jnp.zeros_like(outgoing))
    returned = lax.all_to_all(
        outgoing.astype(jnp.bfloat16), "seq", split_axis=0, concat_axis=1, tiled=True
    ).astype(outgoing.dtype)
    scaled = returned * query_gate[0][:, None]
    targets = jnp.where(own_queries >= 0, own_queries, tok_rows)
    combined = light_part.at[targets].add(scaled, mode="drop")
    return lax.psum_scatter(combined.astype(jnp.bfloat16), "head", scatter_dimension=1, tiled=True)


def solution(mesh):
    placed = (
        P("seq", "head"),
        P(None, None, "head"),
        P("head", None),
        P(None, "seq", "head"),
        P("head", "seq"),
        P(),
        P(),
        P("seq", None),
    )
    return jax.shard_map(
        per_device, mesh=mesh, in_specs=placed, out_specs=P("seq", "head"), check_vma=False
    )
```

```python
import functools
import math

import jax
import jax.numpy as jnp
from jax import lax
from jax.experimental import pallas as pl
from jax.experimental.pallas import tpu as pltpu
from jax.sharding import PartitionSpec as P

HD = 128
LB = 128
ROUTE = 32
BF = jnp.bfloat16
F32 = jnp.float32
VMEM = pl.BlockSpec(memory_space=pltpu.VMEM)
FIRST = (((0,), (0,)), ((), ()))
LAST = (((1,), (1,)), ((), ()))


def attend(queries, key_rows, value_rows):
    scores = jnp.einsum(
        "bqhe,bkhe->bhqk", queries, key_rows, preferred_element_type=jnp.float32
    ) / math.sqrt(queries.shape[-1])
    highest = jnp.max(scores, axis=-1, keepdims=True)
    expanded = jnp.exp(scores - highest)
    totals = jnp.sum(expanded, axis=-1)
    weighted = jnp.einsum(
        "bhqk,bkhe->bqhe",
        expanded.astype(jnp.bfloat16),
        value_rows,
        preferred_element_type=jnp.float32,
    )
    return (weighted / jnp.transpose(totals, (0, 2, 1))[..., None]).astype(jnp.bfloat16)


def routed_map(table, routed):
    counts = jnp.sum((table >= 0).astype(jnp.int32), axis=1)
    shard = jnp.arange(table.shape[0], dtype=jnp.int32)
    upper_end = jnp.sum(jnp.where(shard[None, :] <= shard[:, None], counts[None, :], 0), axis=1)
    lower_end = upper_end - counts
    compact_rows = jnp.arange(routed, dtype=jnp.int32)
    source_shard = jnp.sum((upper_end[None, :] <= compact_rows[:, None]).astype(jnp.int32), axis=1)
    onehot_shard = (
        source_shard[:, None] == jnp.arange(table.shape[0], dtype=jnp.int32)[None, :]
    ).astype(jnp.int32)
    within = compact_rows - jnp.sum(onehot_shard * lower_end[None, :], axis=1)
    return (source_shard * table.shape[1] + within, lower_end)


def project(query_part, source_part, weights):
    stacked = jnp.stack((query_part, source_part, source_part))
    return jnp.einsum("cmd,cdw->mcw", stacked, weights, preferred_element_type=jnp.float32)


def pick_rows(gathered, own_list):
    chosen = jnp.take(gathered, jnp.maximum(own_list, 0), axis=0)
    return jnp.where((own_list >= 0)[:, None], chosen, jnp.zeros_like(chosen))


def general(
    tokens,
    light_input,
    light_output,
    heavy_input,
    heavy_output,
    query_tokens,
    context_tokens,
    query_gate,
):
    gathered = lax.all_gather(tokens, "head", axis=1, tiled=True)
    tok_rows = gathered.shape[0]
    light_mapped = jnp.einsum(
        "td,cdw->ctw", gathered, light_input, preferred_element_type=jnp.float32
    ).astype(jnp.bfloat16)
    light_blocks = light_mapped.reshape(3, tok_rows // LB, LB, -1, HD)
    light_heads = attend(light_blocks[0], light_blocks[1], light_blocks[2]).reshape(tok_rows, -1)
    light_part = jnp.dot(light_heads, light_output, preferred_element_type=jnp.float32)
    seq_count = lax.axis_size("seq")
    routed = seq_count * tok_rows // ROUTE
    slot_count = query_tokens.shape[1]
    seq_index = lax.axis_index("seq")
    own_queries = lax.dynamic_index_in_dim(query_tokens, seq_index, 0, keepdims=False)
    own_sources = lax.dynamic_index_in_dim(context_tokens, seq_index, 0, keepdims=False)
    query_cols, source_cols = (
        lax.all_to_all(
            pick_rows(gathered, own_queries), "seq", split_axis=1, concat_axis=0, tiled=True
        ),
        lax.all_to_all(
            pick_rows(gathered, own_sources), "seq", split_axis=1, concat_axis=0, tiled=True
        ),
    )
    query_index, query_lower = routed_map(query_tokens, routed)
    source_index = routed_map(context_tokens, routed)[0]
    query_rows = jnp.take(query_cols, query_index, axis=0)
    source_rows = jnp.take(source_cols, source_index, axis=0)
    summed = lax.psum(project(query_rows, source_rows, heavy_input), "seq").astype(jnp.bfloat16)
    heavy_heads = attend(
        summed[:, 0].reshape(1, routed, -1, HD),
        summed[:, 1].reshape(1, routed, -1, HD),
        summed[:, 2].reshape(1, routed, -1, HD),
    ).reshape(routed, -1)
    heavy_part = jnp.dot(heavy_heads, heavy_output, preferred_element_type=jnp.float32)
    slot_live = query_tokens >= 0
    compact = query_lower[:, None] + jnp.arange(slot_count, dtype=jnp.int32)[None, :]
    outgoing = jnp.take(heavy_part, jnp.where(slot_live, compact, 0).reshape(-1), axis=0)
    outgoing = jnp.where(slot_live.reshape(-1)[:, None], outgoing, jnp.zeros_like(outgoing))
    returned = lax.all_to_all(
        outgoing.astype(jnp.bfloat16), "seq", split_axis=0, concat_axis=1, tiled=True
    ).astype(outgoing.dtype)
    scaled = returned * query_gate[0][:, None]
    targets = jnp.where(own_queries >= 0, own_queries, tok_rows)
    combined = light_part.at[targets].add(scaled, mode="drop")
    return lax.psum_scatter(combined.astype(jnp.bfloat16), "head", scatter_dimension=1, tiled=True)


def own_row(table, index):
    rows = lax.broadcasted_iota(jnp.int32, table.shape, 0)
    return jnp.sum(jnp.where(rows == index, table, 0), axis=0, keepdims=True)


def compact_onehot(flat, routed):
    slots = flat.shape[1]
    live = flat >= 0
    before = lax.broadcasted_iota(jnp.int32, (slots, slots), 0) < lax.broadcasted_iota(
        jnp.int32, (slots, slots), 1
    )
    place = jnp.dot(
        live.astype(F32).astype(BF), before.astype(F32).astype(BF), preferred_element_type=F32
    ).astype(jnp.int32)
    row = lax.broadcasted_iota(jnp.int32, (routed, slots), 0)
    return ((row == place) & live).astype(F32).astype(BF)


def pick_kernel(where_ref, tok_ref, query_ref, source_ref, keep_ref, send_ref):
    seq_index, odd = where_ref[0], where_ref[1] % 2
    own_q = own_row(query_ref[...], seq_index)
    own_s = own_row(source_ref[...], seq_index)
    tok_rows = tok_ref.shape[0]
    spot = lax.broadcasted_iota(jnp.int32, (tok_rows, own_q.shape[1]), 0)
    for ref, wanted in ((keep_ref, 0), (send_ref, 1)):
        listed = jnp.where(odd == wanted, own_q, own_s)
        chosen = (spot == listed).astype(F32).astype(BF)
        ref[...] = lax.dot_general(
            chosen, tok_ref[...], FIRST, preferred_element_type=F32
        ).astype(BF)


def spread_kernel(where_ref, keep_ref, got_ref, out_ref):
    odd = where_ref[1] % 2
    keep, got = keep_ref[...], got_ref[...]
    width = out_ref.shape[2]
    per = keep.shape[1] // width
    for part, block in enumerate((jnp.where(odd == 0, keep, got), jnp.where(odd == 0, got, keep))):
        for j in range(per):
            for at in range(part * per + j, out_ref.shape[0], 2 * per):
                out_ref[at] = block[:, j * width : (j + 1) * width]


def compact_kernel(where_ref, slots_ref, query_ref, source_ref, out_ref):
    odd = where_ref[1] % 2
    flat = jnp.where(odd == 0, query_ref[...], source_ref[...])
    chosen = compact_onehot(flat, out_ref.shape[0])
    rows = slots_ref[...].reshape(-1, slots_ref.shape[2])
    out_ref[...] = jnp.dot(chosen, rows, preferred_element_type=F32).astype(BF)


def project_kernel(where_ref, mine_ref, other_ref, weight_ref, out_ref):
    odd = where_ref[1] % 2
    mine, other = mine_ref[...], other_ref[...]
    query = jnp.where(odd == 0, mine, other)
    source = jnp.where(odd == 0, other, mine)
    for c, rows in enumerate((query, source, source)):
        part = jnp.dot(rows, weight_ref[c], preferred_element_type=F32).astype(BF)
        for g in range(out_ref.shape[0]):
            out_ref[g, c] = part[:, g * HD : (g + 1) * HD]


def one_head(query, key, value):
    scores = lax.dot_general(query, key, LAST, preferred_element_type=F32) / math.sqrt(HD)
    expanded = jnp.exp(scores - jnp.max(scores, axis=-1, keepdims=True))
    totals = jnp.sum(expanded, axis=-1, keepdims=True)
    weighted = jnp.dot(expanded.astype(BF), value, preferred_element_type=F32)
    return (weighted / totals).astype(BF)


def heavy_attend_kernel(parts_ref, out_ref):
    total = parts_ref[0].astype(F32)
    for s in range(1, parts_ref.shape[0]):
        total = total + parts_ref[s].astype(F32)
    total = total.astype(BF)
    result = one_head(total[0], total[1], total[2])
    for s in range(out_ref.shape[0]):
        out_ref[s] = result


def heavy_output_kernel(heads_ref, weight_ref, query_ref, out_ref):
    routed = heads_ref.shape[1]
    part = jnp.zeros((routed, weight_ref.shape[1]), F32)
    rows = jnp.concatenate([heads_ref[g] for g in range(heads_ref.shape[0])], axis=1)
    part = jnp.dot(rows, weight_ref[...], preferred_element_type=F32).astype(BF)
    chosen = compact_onehot(query_ref[...], routed)
    spread = lax.dot_general(chosen, part, FIRST, preferred_element_type=F32).astype(BF)
    out_ref[...] = spread.reshape(out_ref.shape)


def finish_kernel(where_ref, light_ref, mine_ref, got_ref, last_ref, query_ref, gate_ref, out_ref):
    seq_index, head = where_ref[0], where_ref[1]
    per = last_ref.shape[0]
    own_q = own_row(query_ref[...], seq_index)
    slots = own_q.shape[1]
    at = pl.multiple_of(head * per, per)
    outer = pl.multiple_of((head // 2) * per, per)
    heavy = (
        mine_ref[pl.ds(at, per)].astype(F32)
        + got_ref[pl.ds(outer, per)].astype(F32)
        + last_ref[...].astype(F32)
    )
    diagonal = lax.broadcasted_iota(jnp.int32, (slots, slots), 0) == lax.broadcasted_iota(
        jnp.int32, (slots, slots), 1
    )
    gate = jnp.sum(jnp.where(diagonal, gate_ref[...], 0.0), axis=1, keepdims=True)
    tok_rows = light_ref.shape[0]
    spot = lax.broadcasted_iota(jnp.int32, (tok_rows, slots), 0)
    chosen = (spot == own_q).astype(F32).astype(BF)
    width = heavy.shape[2]
    for j in range(per):
        scaled = heavy[j] * gate
        coarse = scaled.astype(BF)
        fine = (scaled - coarse.astype(F32)).astype(BF)
        added = jnp.dot(chosen, coarse, preferred_element_type=F32) + jnp.dot(
            chosen, fine, preferred_element_type=F32
        )
        cols = slice(j * width, (j + 1) * width)
        out_ref[:, cols] = (light_ref[:, cols].astype(F32) + added).astype(BF)


def light_kernel(tok_ref, weight_ref, out_ref, acc_ref):
    step = pl.program_id(0)

    @pl.when(step == 0)
    def _():
        acc_ref[...] = jnp.zeros_like(acc_ref)

    for c in range(3):
        acc_ref[c] += jnp.dot(tok_ref[...], weight_ref[c], preferred_element_type=F32)

    @pl.when(step == pl.num_programs(0) - 1)
    def _():
        for b in range(out_ref.shape[0] // LB):
            for g in range(out_ref.shape[1] // HD):
                at = (slice(b * LB, (b + 1) * LB), slice(g * HD, (g + 1) * HD))
                out_ref[at] = one_head(*(acc_ref[(c, *at)].astype(BF) for c in range(3)))


def light_output_kernel(heads_ref, weight_ref, out_ref):
    out_ref[...] = jnp.dot(heads_ref[...], weight_ref[...], preferred_element_type=F32).astype(BF)


def cost(flops, moved):
    return pl.CostEstimate(flops=int(flops), bytes_accessed=int(moved), transcendentals=0)


SMEM = pl.BlockSpec(memory_space=pltpu.SMEM)


def one_head_a_device(
    tokens,
    light_input,
    light_output,
    heavy_input,
    heavy_output,
    query_tokens,
    context_tokens,
    query_gate,
):
    seq_count, head_count = lax.axis_size("seq"), lax.axis_size("head")
    seq_index, head_index = lax.axis_index("seq"), lax.axis_index("head")
    where = jnp.stack([seq_index, head_index]).astype(jnp.int32)
    tok_rows, own_width = tokens.shape
    slots = query_tokens.shape[1]
    routed = seq_count * tok_rows // ROUTE
    part_width = heavy_input.shape[1]
    head_cols = heavy_input.shape[2]
    out_cols = heavy_output.shape[1]
    flat_q = query_tokens.reshape(1, -1)
    flat_s = context_tokens.reshape(1, -1)
    pair = [(i, i ^ 1) for i in range(head_count)]
    across = [(i, i ^ 2) for i in range(head_count)]
    half = seq_count // (head_count // 2)

    gathered = lax.all_gather(tokens, "head", axis=1, tiled=True)
    full = gathered.shape[1]
    light_cols = light_input.shape[2]
    tile = part_width
    light_heads = pl.pallas_call(
        light_kernel,
        grid=(full // tile,),
        in_specs=[
            pl.BlockSpec((tok_rows, tile), lambda i: (0, i)),
            pl.BlockSpec((3, tile, light_cols), lambda i: (0, i, 0)),
        ],
        out_specs=pl.BlockSpec((tok_rows, light_cols), lambda i: (0, 0)),
        out_shape=jax.ShapeDtypeStruct((tok_rows, light_cols), BF),
        scratch_shapes=[pltpu.VMEM((3, tok_rows, light_cols), F32)],
        cost_estimate=cost(6 * tok_rows * full * light_cols, 2 * full * (3 * light_cols + tok_rows)),
    )(gathered, light_input)
    wide = light_output.shape[1]
    light_part = pl.pallas_call(
        light_output_kernel,
        grid=(wide // own_width,),
        in_specs=[
            pl.BlockSpec((tok_rows, light_cols), lambda i: (0, 0)),
            pl.BlockSpec((light_cols, own_width), lambda i: (0, i)),
        ],
        out_specs=pl.BlockSpec((tok_rows, own_width), lambda i: (0, i)),
        out_shape=jax.ShapeDtypeStruct((tok_rows, wide), BF),
        cost_estimate=cost(2 * tok_rows * light_cols * wide, 2 * wide * (light_cols + tok_rows)),
    )(light_heads, light_output)
    light = lax.psum_scatter(light_part, "head", scatter_dimension=1, tiled=True)

    keep, send = pl.pallas_call(
        pick_kernel,
        in_specs=[SMEM, VMEM, VMEM, VMEM],
        out_specs=[VMEM, VMEM],
        out_shape=[jax.ShapeDtypeStruct((slots, own_width), BF)] * 2,
        cost_estimate=cost(4 * slots * tok_rows * own_width, 2 * tok_rows * own_width),
    )(where, tokens, query_tokens, context_tokens)
    got = lax.ppermute(send, "head", pair)
    spread = pl.pallas_call(
        spread_kernel,
        in_specs=[SMEM, VMEM, VMEM],
        out_specs=VMEM,
        out_shape=jax.ShapeDtypeStruct((seq_count, slots, part_width), BF),
        cost_estimate=cost(0, 4 * seq_count * slots * part_width),
    )(where, keep, got)
    spread = lax.all_to_all(spread, "seq", split_axis=0, concat_axis=0, tiled=True)
    mine = pl.pallas_call(
        compact_kernel,
        in_specs=[SMEM, VMEM, VMEM, VMEM],
        out_specs=VMEM,
        out_shape=jax.ShapeDtypeStruct((routed, part_width), BF),
        cost_estimate=cost(0, 4 * seq_count * slots * part_width),
    )(where, spread, flat_q, flat_s)
    holds = [
        (s * head_count + h, s * head_count + (h ^ 2))
        for s in range(seq_count)
        for h in range(head_count)
        if s // half == h // 2
    ]
    crossed = lax.ppermute(mine, ("seq", "head"), holds)
    mine = jnp.where(seq_index // half == head_index // 2, mine, crossed)
    other = lax.ppermute(mine, "head", pair)
    group = 2
    parts = pl.pallas_call(
        project_kernel,
        grid=(head_cols // (group * HD),),
        in_specs=[
            SMEM,
            pl.BlockSpec((routed, part_width), lambda i: (0, 0)),
            pl.BlockSpec((routed, part_width), lambda i: (0, 0)),
            pl.BlockSpec((3, part_width, group * HD), lambda i: (0, 0, i)),
        ],
        out_specs=pl.BlockSpec((group, 3, routed, HD), lambda i: (i, 0, 0, 0)),
        out_shape=jax.ShapeDtypeStruct((seq_count, 3, routed, HD), BF),
        cost_estimate=cost(6 * routed * part_width * head_cols, 6 * part_width * head_cols),
    )(where, mine, other, heavy_input)
    parts = lax.all_to_all(parts, "seq", split_axis=0, concat_axis=0, tiled=True)
    heads = pl.pallas_call(
        heavy_attend_kernel,
        in_specs=[VMEM],
        out_specs=VMEM,
        out_shape=jax.ShapeDtypeStruct((seq_count, routed, HD), BF),
        cost_estimate=cost(0, 8 * seq_count * routed * HD),
    )(parts)
    heads = lax.all_to_all(heads, "seq", split_axis=0, concat_axis=0, tiled=True)
    outgoing = pl.pallas_call(
        heavy_output_kernel,
        in_specs=[VMEM, VMEM, VMEM],
        out_specs=VMEM,
        out_shape=jax.ShapeDtypeStruct((seq_count, slots, out_cols), BF),
        cost_estimate=cost(2 * routed * head_cols * out_cols, 2 * head_cols * out_cols),
    )(heads, heavy_output, flat_q)
    returned = lax.all_to_all(outgoing, "seq", split_axis=0, concat_axis=0, tiled=True)
    per = seq_count // head_count
    view = returned.reshape(head_count // 2, 2, per, slots, out_cols)
    odd = head_index % 2
    give = lax.dynamic_index_in_dim(view, 1 - odd, 1, keepdims=False)
    got_pair = lax.ppermute(give, "head", pair)
    far = 1 - head_index // 2
    give = (
        lax.dynamic_index_in_dim(
            lax.dynamic_index_in_dim(view, far, 0, keepdims=False), odd, 0, keepdims=False
        ).astype(F32)
        + lax.dynamic_index_in_dim(got_pair, far, 0, keepdims=False).astype(F32)
    ).astype(BF)
    last = lax.ppermute(give, "head", across)
    return pl.pallas_call(
        finish_kernel,
        in_specs=[SMEM] + [VMEM] * 6,
        out_specs=VMEM,
        out_shape=jax.ShapeDtypeStruct((tok_rows, own_width), BF),
        cost_estimate=cost(0, 4 * tok_rows * own_width),
    )(
        where,
        light,
        returned,
        got_pair.reshape(-1, slots, out_cols),
        last,
        query_tokens,
        query_gate,
    )


def solution(mesh):
    placed = (
        P("seq", "head"),
        P(None, None, "head"),
        P("head", None),
        P(None, "seq", "head"),
        P("head", "seq"),
        P(),
        P(),
        P("seq", None),
    )

    def per_device(*args):
        seq_count, head_count = mesh.shape["seq"], mesh.shape["head"]
        local_heads = args[3].shape[2] // HD
        fits = head_count // 2 == 2 and seq_count % head_count == 0 and local_heads == seq_count
        return (one_head_a_device if fits else general)(*args)

    return jax.shard_map(
        per_device, mesh=mesh, in_specs=placed, out_specs=P("seq", "head"), check_vma=False
    )
```

```python
import functools
import math

import jax
import jax.numpy as jnp
from jax import lax
from jax.experimental import pallas as pl
from jax.experimental.pallas import tpu as pltpu
from jax.sharding import PartitionSpec as P

HD = 128
LB = 128
ROUTE = 32
BF = jnp.bfloat16
F32 = jnp.float32
VMEM = pl.BlockSpec(memory_space=pltpu.VMEM)
FIRST = (((0,), (0,)), ((), ()))
LAST = (((1,), (1,)), ((), ()))


def attend(queries, key_rows, value_rows):
    scores = jnp.einsum(
        "bqhe,bkhe->bhqk", queries, key_rows, preferred_element_type=jnp.float32
    ) / math.sqrt(queries.shape[-1])
    highest = jnp.max(scores, axis=-1, keepdims=True)
    expanded = jnp.exp(scores - highest)
    totals = jnp.sum(expanded, axis=-1)
    weighted = jnp.einsum(
        "bhqk,bkhe->bqhe",
        expanded.astype(jnp.bfloat16),
        value_rows,
        preferred_element_type=jnp.float32,
    )
    return (weighted / jnp.transpose(totals, (0, 2, 1))[..., None]).astype(jnp.bfloat16)


def routed_map(table, routed):
    counts = jnp.sum((table >= 0).astype(jnp.int32), axis=1)
    shard = jnp.arange(table.shape[0], dtype=jnp.int32)
    upper_end = jnp.sum(jnp.where(shard[None, :] <= shard[:, None], counts[None, :], 0), axis=1)
    lower_end = upper_end - counts
    compact_rows = jnp.arange(routed, dtype=jnp.int32)
    source_shard = jnp.sum((upper_end[None, :] <= compact_rows[:, None]).astype(jnp.int32), axis=1)
    onehot_shard = (
        source_shard[:, None] == jnp.arange(table.shape[0], dtype=jnp.int32)[None, :]
    ).astype(jnp.int32)
    within = compact_rows - jnp.sum(onehot_shard * lower_end[None, :], axis=1)
    return (source_shard * table.shape[1] + within, lower_end)


def project(query_part, source_part, weights):
    stacked = jnp.stack((query_part, source_part, source_part))
    return jnp.einsum("cmd,cdw->mcw", stacked, weights, preferred_element_type=jnp.float32)


def pick_rows(gathered, own_list):
    chosen = jnp.take(gathered, jnp.maximum(own_list, 0), axis=0)
    return jnp.where((own_list >= 0)[:, None], chosen, jnp.zeros_like(chosen))


def general(
    tokens,
    light_input,
    light_output,
    heavy_input,
    heavy_output,
    query_tokens,
    context_tokens,
    query_gate,
):
    gathered = lax.all_gather(tokens, "head", axis=1, tiled=True)
    tok_rows = gathered.shape[0]
    light_mapped = jnp.einsum(
        "td,cdw->ctw", gathered, light_input, preferred_element_type=jnp.float32
    ).astype(jnp.bfloat16)
    light_blocks = light_mapped.reshape(3, tok_rows // LB, LB, -1, HD)
    light_heads = attend(light_blocks[0], light_blocks[1], light_blocks[2]).reshape(tok_rows, -1)
    light_part = jnp.dot(light_heads, light_output, preferred_element_type=jnp.float32)
    seq_count = lax.axis_size("seq")
    routed = seq_count * tok_rows // ROUTE
    slot_count = query_tokens.shape[1]
    seq_index = lax.axis_index("seq")
    own_queries = lax.dynamic_index_in_dim(query_tokens, seq_index, 0, keepdims=False)
    own_sources = lax.dynamic_index_in_dim(context_tokens, seq_index, 0, keepdims=False)
    query_cols, source_cols = (
        lax.all_to_all(
            pick_rows(gathered, own_queries), "seq", split_axis=1, concat_axis=0, tiled=True
        ),
        lax.all_to_all(
            pick_rows(gathered, own_sources), "seq", split_axis=1, concat_axis=0, tiled=True
        ),
    )
    query_index, query_lower = routed_map(query_tokens, routed)
    source_index = routed_map(context_tokens, routed)[0]
    query_rows = jnp.take(query_cols, query_index, axis=0)
    source_rows = jnp.take(source_cols, source_index, axis=0)
    summed = lax.psum(project(query_rows, source_rows, heavy_input), "seq").astype(jnp.bfloat16)
    heavy_heads = attend(
        summed[:, 0].reshape(1, routed, -1, HD),
        summed[:, 1].reshape(1, routed, -1, HD),
        summed[:, 2].reshape(1, routed, -1, HD),
    ).reshape(routed, -1)
    heavy_part = jnp.dot(heavy_heads, heavy_output, preferred_element_type=jnp.float32)
    slot_live = query_tokens >= 0
    compact = query_lower[:, None] + jnp.arange(slot_count, dtype=jnp.int32)[None, :]
    outgoing = jnp.take(heavy_part, jnp.where(slot_live, compact, 0).reshape(-1), axis=0)
    outgoing = jnp.where(slot_live.reshape(-1)[:, None], outgoing, jnp.zeros_like(outgoing))
    returned = lax.all_to_all(
        outgoing.astype(jnp.bfloat16), "seq", split_axis=0, concat_axis=1, tiled=True
    ).astype(outgoing.dtype)
    scaled = returned * query_gate[0][:, None]
    targets = jnp.where(own_queries >= 0, own_queries, tok_rows)
    combined = light_part.at[targets].add(scaled, mode="drop")
    return lax.psum_scatter(combined.astype(jnp.bfloat16), "head", scatter_dimension=1, tiled=True)


def own_row(table, index):
    rows = lax.broadcasted_iota(jnp.int32, table.shape, 0)
    return jnp.sum(jnp.where(rows == index, table, 0), axis=0, keepdims=True)


def compact_onehot(flat, routed):
    slots = flat.shape[1]
    live = flat >= 0
    before = lax.broadcasted_iota(jnp.int32, (slots, slots), 0) < lax.broadcasted_iota(
        jnp.int32, (slots, slots), 1
    )
    place = jnp.dot(
        live.astype(F32).astype(BF), before.astype(F32).astype(BF), preferred_element_type=F32
    ).astype(jnp.int32)
    row = lax.broadcasted_iota(jnp.int32, (routed, slots), 0)
    return ((row == place) & live).astype(F32).astype(BF)


def pick_kernel(where_ref, tok_ref, query_ref, source_ref, keep_ref, send_ref):
    seq_index, odd = where_ref[0], where_ref[1] % 2
    own_q = own_row(query_ref[...], seq_index)
    own_s = own_row(source_ref[...], seq_index)
    tok_rows = tok_ref.shape[0]
    spot = lax.broadcasted_iota(jnp.int32, (tok_rows, own_q.shape[1]), 0)
    for ref, wanted in ((keep_ref, 0), (send_ref, 1)):
        listed = jnp.where(odd == wanted, own_q, own_s)
        chosen = (spot == listed).astype(F32).astype(BF)
        ref[...] = lax.dot_general(
            chosen, tok_ref[...], FIRST, preferred_element_type=F32
        ).astype(BF)


def spread_kernel(where_ref, keep_ref, got_ref, out_ref):
    odd = where_ref[1] % 2
    keep, got = keep_ref[...], got_ref[...]
    width = out_ref.shape[2]
    per = keep.shape[1] // width
    for part, block in enumerate((jnp.where(odd == 0, keep, got), jnp.where(odd == 0, got, keep))):
        for j in range(per):
            for at in range(part * per + j, out_ref.shape[0], 2 * per):
                out_ref[at] = block[:, j * width : (j + 1) * width]


def compact_kernel(where_ref, slots_ref, query_ref, source_ref, out_ref):
    odd = where_ref[1] % 2
    flat = jnp.where(odd == 0, query_ref[...], source_ref[...])
    chosen = compact_onehot(flat, out_ref.shape[0])
    rows = slots_ref[...].reshape(-1, slots_ref.shape[2])
    out_ref[...] = jnp.dot(chosen, rows, preferred_element_type=F32).astype(BF)


def project_kernel(where_ref, mine_ref, other_ref, weight_ref, out_ref):
    odd = where_ref[1] % 2
    mine, other = mine_ref[...], other_ref[...]
    query = jnp.where(odd == 0, mine, other)
    source = jnp.where(odd == 0, other, mine)
    for c, rows in enumerate((query, source, source)):
        part = jnp.dot(rows, weight_ref[c], preferred_element_type=F32).astype(BF)
        for g in range(out_ref.shape[0]):
            out_ref[g, c] = part[:, g * HD : (g + 1) * HD]


def one_head(query, key, value):
    scores = lax.dot_general(query, key, LAST, preferred_element_type=F32) / math.sqrt(HD)
    expanded = jnp.exp(scores - jnp.max(scores, axis=-1, keepdims=True))
    totals = jnp.sum(expanded, axis=-1, keepdims=True)
    weighted = jnp.dot(expanded.astype(BF), value, preferred_element_type=F32)
    return (weighted / totals).astype(BF)


def heavy_attend_kernel(parts_ref, out_ref):
    total = parts_ref[0].astype(F32)
    for s in range(1, parts_ref.shape[0]):
        total = total + parts_ref[s].astype(F32)
    total = total.astype(BF)
    result = one_head(total[0], total[1], total[2])
    for s in range(out_ref.shape[0]):
        out_ref[s] = result


def heavy_output_kernel(heads_ref, weight_ref, query_ref, out_ref):
    routed = heads_ref.shape[1]
    part = jnp.zeros((routed, weight_ref.shape[1]), F32)
    rows = jnp.concatenate([heads_ref[g] for g in range(heads_ref.shape[0])], axis=1)
    part = jnp.dot(rows, weight_ref[...], preferred_element_type=F32).astype(BF)
    chosen = compact_onehot(query_ref[...], routed)
    spread = lax.dot_general(chosen, part, FIRST, preferred_element_type=F32).astype(BF)
    out_ref[...] = spread.reshape(out_ref.shape)


def finish_kernel(where_ref, light_ref, mine_ref, got_ref, last_ref, query_ref, gate_ref, out_ref):
    seq_index, head = where_ref[0], where_ref[1]
    per = last_ref.shape[0]
    own_q = own_row(query_ref[...], seq_index)
    slots = own_q.shape[1]
    at = pl.multiple_of(head * per, per)
    outer = pl.multiple_of((head // 2) * per, per)
    heavy = (
        mine_ref[pl.ds(at, per)].astype(F32)
        + got_ref[pl.ds(outer, per)].astype(F32)
        + last_ref[...].astype(F32)
    )
    diagonal = lax.broadcasted_iota(jnp.int32, (slots, slots), 0) == lax.broadcasted_iota(
        jnp.int32, (slots, slots), 1
    )
    gate = jnp.sum(jnp.where(diagonal, gate_ref[...], 0.0), axis=1, keepdims=True)
    tok_rows = light_ref.shape[0]
    spot = lax.broadcasted_iota(jnp.int32, (tok_rows, slots), 0)
    chosen = (spot == own_q).astype(F32).astype(BF)
    width = heavy.shape[2]
    for j in range(per):
        scaled = heavy[j] * gate
        coarse = scaled.astype(BF)
        fine = (scaled - coarse.astype(F32)).astype(BF)
        added = jnp.dot(chosen, coarse, preferred_element_type=F32) + jnp.dot(
            chosen, fine, preferred_element_type=F32
        )
        cols = slice(j * width, (j + 1) * width)
        out_ref[:, cols] = (light_ref[:, cols].astype(F32) + added).astype(BF)


def light_kernel(tok_ref, weight_ref, out_ref, acc_ref):
    step = pl.program_id(0)

    @pl.when(step == 0)
    def _():
        acc_ref[...] = jnp.zeros_like(acc_ref)

    for c in range(3):
        acc_ref[c] += jnp.dot(tok_ref[...], weight_ref[c], preferred_element_type=F32)

    @pl.when(step == pl.num_programs(0) - 1)
    def _():
        for b in range(out_ref.shape[0] // LB):
            for g in range(out_ref.shape[1] // HD):
                at = (slice(b * LB, (b + 1) * LB), slice(g * HD, (g + 1) * HD))
                out_ref[at] = one_head(*(acc_ref[(c, *at)].astype(BF) for c in range(3)))


def light_output_kernel(heads_ref, weight_ref, out_ref):
    out_ref[...] = jnp.dot(heads_ref[...], weight_ref[...], preferred_element_type=F32).astype(BF)


def cost(flops, moved):
    return pl.CostEstimate(flops=int(flops), bytes_accessed=int(moved), transcendentals=0)


SMEM = pl.BlockSpec(memory_space=pltpu.SMEM)


def one_head_a_device(
    tokens,
    light_input,
    light_output,
    heavy_input,
    heavy_output,
    query_tokens,
    context_tokens,
    query_gate,
):
    seq_count, head_count = lax.axis_size("seq"), lax.axis_size("head")
    seq_index, head_index = lax.axis_index("seq"), lax.axis_index("head")
    where = jnp.stack([seq_index, head_index]).astype(jnp.int32)
    tok_rows, own_width = tokens.shape
    slots = query_tokens.shape[1]
    routed = seq_count * tok_rows // ROUTE
    part_width = heavy_input.shape[1]
    head_cols = heavy_input.shape[2]
    out_cols = heavy_output.shape[1]
    flat_q = query_tokens.reshape(1, -1)
    flat_s = context_tokens.reshape(1, -1)
    pair = [(i, i ^ 1) for i in range(head_count)]
    across = [(i, i ^ 2) for i in range(head_count)]
    half = seq_count // (head_count // 2)

    gathered = lax.all_gather(tokens, "head", axis=1, tiled=True)

    keep, send = pl.pallas_call(
        pick_kernel,
        in_specs=[SMEM, VMEM, VMEM, VMEM],
        out_specs=[VMEM, VMEM],
        out_shape=[jax.ShapeDtypeStruct((slots, own_width), BF)] * 2,
        cost_estimate=cost(4 * slots * tok_rows * own_width, 2 * tok_rows * own_width),
    )(where, tokens, query_tokens, context_tokens)
    got = lax.ppermute(send, "head", pair)
    spread = pl.pallas_call(
        spread_kernel,
        in_specs=[SMEM, VMEM, VMEM],
        out_specs=VMEM,
        out_shape=jax.ShapeDtypeStruct((seq_count, slots, part_width), BF),
        cost_estimate=cost(0, 4 * seq_count * slots * part_width),
    )(where, keep, got)
    spread = lax.all_to_all(spread, "seq", split_axis=0, concat_axis=0, tiled=True)
    mine = pl.pallas_call(
        compact_kernel,
        in_specs=[SMEM, VMEM, VMEM, VMEM],
        out_specs=VMEM,
        out_shape=jax.ShapeDtypeStruct((routed, part_width), BF),
        cost_estimate=cost(0, 4 * seq_count * slots * part_width),
    )(where, spread, flat_q, flat_s)
    holds = [
        (s * head_count + h, s * head_count + (h ^ 2))
        for s in range(seq_count)
        for h in range(head_count)
        if s // half == h // 2
    ]
    crossed = lax.ppermute(mine, ("seq", "head"), holds)
    mine = jnp.where(seq_index // half == head_index // 2, mine, crossed)
    other = lax.ppermute(mine, "head", pair)
    group = 2
    parts = pl.pallas_call(
        project_kernel,
        grid=(head_cols // (group * HD),),
        in_specs=[
            SMEM,
            pl.BlockSpec((routed, part_width), lambda i: (0, 0)),
            pl.BlockSpec((routed, part_width), lambda i: (0, 0)),
            pl.BlockSpec((3, part_width, group * HD), lambda i: (0, 0, i)),
        ],
        out_specs=pl.BlockSpec((group, 3, routed, HD), lambda i: (i, 0, 0, 0)),
        out_shape=jax.ShapeDtypeStruct((seq_count, 3, routed, HD), BF),
        cost_estimate=cost(6 * routed * part_width * head_cols, 6 * part_width * head_cols),
    )(where, mine, other, heavy_input)
    gathered, parts = lax.optimization_barrier((gathered, parts))
    full = gathered.shape[1]
    light_cols = light_input.shape[2]
    tile = part_width
    light_heads = pl.pallas_call(
        light_kernel,
        grid=(full // tile,),
        in_specs=[
            pl.BlockSpec((tok_rows, tile), lambda i: (0, i)),
            pl.BlockSpec((3, tile, light_cols), lambda i: (0, i, 0)),
        ],
        out_specs=pl.BlockSpec((tok_rows, light_cols), lambda i: (0, 0)),
        out_shape=jax.ShapeDtypeStruct((tok_rows, light_cols), BF),
        scratch_shapes=[pltpu.VMEM((3, tok_rows, light_cols), F32)],
        cost_estimate=cost(6 * tok_rows * full * light_cols, 2 * full * (3 * light_cols + tok_rows)),
    )(gathered, light_input)
    wide = light_output.shape[1]
    light_part = pl.pallas_call(
        light_output_kernel,
        grid=(wide // own_width,),
        in_specs=[
            pl.BlockSpec((tok_rows, light_cols), lambda i: (0, 0)),
            pl.BlockSpec((light_cols, own_width), lambda i: (0, i)),
        ],
        out_specs=pl.BlockSpec((tok_rows, own_width), lambda i: (0, i)),
        out_shape=jax.ShapeDtypeStruct((tok_rows, wide), BF),
        cost_estimate=cost(2 * tok_rows * light_cols * wide, 2 * wide * (light_cols + tok_rows)),
    )(light_heads, light_output)

    parts = lax.all_to_all(parts, "seq", split_axis=0, concat_axis=0, tiled=True)
    parts, light_part = lax.optimization_barrier((parts, light_part))
    light = lax.psum_scatter(light_part, "head", scatter_dimension=1, tiled=True)
    heads = pl.pallas_call(
        heavy_attend_kernel,
        in_specs=[VMEM],
        out_specs=VMEM,
        out_shape=jax.ShapeDtypeStruct((seq_count, routed, HD), BF),
        cost_estimate=cost(0, 8 * seq_count * routed * HD),
    )(parts)
    heads = lax.all_to_all(heads, "seq", split_axis=0, concat_axis=0, tiled=True)
    outgoing = pl.pallas_call(
        heavy_output_kernel,
        in_specs=[VMEM, VMEM, VMEM],
        out_specs=VMEM,
        out_shape=jax.ShapeDtypeStruct((seq_count, slots, out_cols), BF),
        cost_estimate=cost(2 * routed * head_cols * out_cols, 2 * head_cols * out_cols),
    )(heads, heavy_output, flat_q)
    returned = lax.all_to_all(outgoing, "seq", split_axis=0, concat_axis=0, tiled=True)
    per = seq_count // head_count
    view = returned.reshape(head_count // 2, 2, per, slots, out_cols)
    odd = head_index % 2
    give = lax.dynamic_index_in_dim(view, 1 - odd, 1, keepdims=False)
    got_pair = lax.ppermute(give, "head", pair)
    far = 1 - head_index // 2
    give = (
        lax.dynamic_index_in_dim(
            lax.dynamic_index_in_dim(view, far, 0, keepdims=False), odd, 0, keepdims=False
        ).astype(F32)
        + lax.dynamic_index_in_dim(got_pair, far, 0, keepdims=False).astype(F32)
    ).astype(BF)
    last = lax.ppermute(give, "head", across)
    return pl.pallas_call(
        finish_kernel,
        in_specs=[SMEM] + [VMEM] * 6,
        out_specs=VMEM,
        out_shape=jax.ShapeDtypeStruct((tok_rows, own_width), BF),
        cost_estimate=cost(0, 4 * tok_rows * own_width),
    )(
        where,
        light,
        returned,
        got_pair.reshape(-1, slots, out_cols),
        last,
        query_tokens,
        query_gate,
    )


def solution(mesh):
    placed = (
        P("seq", "head"),
        P(None, None, "head"),
        P("head", None),
        P(None, "seq", "head"),
        P("head", "seq"),
        P(),
        P(),
        P("seq", None),
    )

    def per_device(*args):
        seq_count, head_count = mesh.shape["seq"], mesh.shape["head"]
        local_heads = args[3].shape[2] // HD
        fits = head_count // 2 == 2 and seq_count % head_count == 0 and local_heads == seq_count
        return (one_head_a_device if fits else general)(*args)

    return jax.shard_map(
        per_device, mesh=mesh, in_specs=placed, out_specs=P("seq", "head"), check_vma=False
    )
```

```python
import math

import jax
import jax.numpy as jnp
from jax import lax
from jax.experimental import pallas as pl
from jax.experimental.pallas import tpu as pltpu
from jax.sharding import PartitionSpec as P

HD = 128
LB = 128
ROUTE = 32
BF = jnp.bfloat16
F32 = jnp.float32
VMEM = pl.BlockSpec(memory_space=pltpu.VMEM)
FIRST = (((0,), (0,)), ((), ()))
LAST = (((1,), (1,)), ((), ()))


def attend(queries, key_rows, value_rows):
    scores = jnp.einsum(
        "bqhe,bkhe->bhqk", queries, key_rows, preferred_element_type=jnp.float32
    ) / math.sqrt(queries.shape[-1])
    highest = jnp.max(scores, axis=-1, keepdims=True)
    expanded = jnp.exp(scores - highest)
    totals = jnp.sum(expanded, axis=-1)
    weighted = jnp.einsum(
        "bhqk,bkhe->bqhe",
        expanded.astype(jnp.bfloat16),
        value_rows,
        preferred_element_type=jnp.float32,
    )
    return (weighted / jnp.transpose(totals, (0, 2, 1))[..., None]).astype(jnp.bfloat16)


def routed_map(table, routed):
    counts = jnp.sum((table >= 0).astype(jnp.int32), axis=1)
    shard = jnp.arange(table.shape[0], dtype=jnp.int32)
    upper_end = jnp.sum(jnp.where(shard[None, :] <= shard[:, None], counts[None, :], 0), axis=1)
    lower_end = upper_end - counts
    compact_rows = jnp.arange(routed, dtype=jnp.int32)
    source_shard = jnp.sum((upper_end[None, :] <= compact_rows[:, None]).astype(jnp.int32), axis=1)
    onehot_shard = (
        source_shard[:, None] == jnp.arange(table.shape[0], dtype=jnp.int32)[None, :]
    ).astype(jnp.int32)
    within = compact_rows - jnp.sum(onehot_shard * lower_end[None, :], axis=1)
    return (source_shard * table.shape[1] + within, lower_end)


def project(query_part, source_part, weights):
    stacked = jnp.stack((query_part, source_part, source_part))
    return jnp.einsum("cmd,cdw->mcw", stacked, weights, preferred_element_type=jnp.float32)


def pick_rows(gathered, own_list):
    chosen = jnp.take(gathered, jnp.maximum(own_list, 0), axis=0)
    return jnp.where((own_list >= 0)[:, None], chosen, jnp.zeros_like(chosen))


def general(
    tokens,
    light_input,
    light_output,
    heavy_input,
    heavy_output,
    query_tokens,
    context_tokens,
    query_gate,
):
    gathered = lax.all_gather(tokens, "head", axis=1, tiled=True)
    tok_rows = gathered.shape[0]
    light_mapped = jnp.einsum(
        "td,cdw->ctw", gathered, light_input, preferred_element_type=jnp.float32
    ).astype(jnp.bfloat16)
    light_blocks = light_mapped.reshape(3, tok_rows // LB, LB, -1, HD)
    light_heads = attend(light_blocks[0], light_blocks[1], light_blocks[2]).reshape(tok_rows, -1)
    light_part = jnp.dot(light_heads, light_output, preferred_element_type=jnp.float32)
    seq_count = lax.axis_size("seq")
    routed = seq_count * tok_rows // ROUTE
    slot_count = query_tokens.shape[1]
    seq_index = lax.axis_index("seq")
    own_queries = lax.dynamic_index_in_dim(query_tokens, seq_index, 0, keepdims=False)
    own_sources = lax.dynamic_index_in_dim(context_tokens, seq_index, 0, keepdims=False)
    query_cols, source_cols = (
        lax.all_to_all(
            pick_rows(gathered, own_queries), "seq", split_axis=1, concat_axis=0, tiled=True
        ),
        lax.all_to_all(
            pick_rows(gathered, own_sources), "seq", split_axis=1, concat_axis=0, tiled=True
        ),
    )
    query_index, query_lower = routed_map(query_tokens, routed)
    source_index = routed_map(context_tokens, routed)[0]
    query_rows = jnp.take(query_cols, query_index, axis=0)
    source_rows = jnp.take(source_cols, source_index, axis=0)
    summed = lax.psum(project(query_rows, source_rows, heavy_input), "seq").astype(jnp.bfloat16)
    heavy_heads = attend(
        summed[:, 0].reshape(1, routed, -1, HD),
        summed[:, 1].reshape(1, routed, -1, HD),
        summed[:, 2].reshape(1, routed, -1, HD),
    ).reshape(routed, -1)
    heavy_part = jnp.dot(heavy_heads, heavy_output, preferred_element_type=jnp.float32)
    slot_live = query_tokens >= 0
    compact = query_lower[:, None] + jnp.arange(slot_count, dtype=jnp.int32)[None, :]
    outgoing = jnp.take(heavy_part, jnp.where(slot_live, compact, 0).reshape(-1), axis=0)
    outgoing = jnp.where(slot_live.reshape(-1)[:, None], outgoing, jnp.zeros_like(outgoing))
    returned = lax.all_to_all(
        outgoing.astype(jnp.bfloat16), "seq", split_axis=0, concat_axis=1, tiled=True
    ).astype(outgoing.dtype)
    scaled = returned * query_gate[0][:, None]
    targets = jnp.where(own_queries >= 0, own_queries, tok_rows)
    combined = light_part.at[targets].add(scaled, mode="drop")
    return lax.psum_scatter(combined.astype(jnp.bfloat16), "head", scatter_dimension=1, tiled=True)


def in_vmem(*arrays):
    return tuple(pltpu.with_memory_space_constraint(a, pltpu.VMEM) for a in arrays)


def on_chip(kernel, outs, *arrays, hbm=(), scratch=(), flops=0, moved=0, off=False):
    made = [(jax.ShapeDtypeStruct if off else pltpu.VMEM)(*o) for o in outs]
    result = pl.pallas_call(
        kernel,
        in_specs=[pl.BlockSpec(memory_space=pl.ANY)] * len(hbm) + [VMEM] * len(arrays),
        scratch_shapes=list(scratch),
        out_specs=[VMEM] * len(made),
        out_shape=made,
        compiler_params=pltpu.CompilerParams(vmem_limit_bytes=(60 if hbm else 8) << 20),
        cost_estimate=pl.CostEstimate(
            flops=int(flops), bytes_accessed=int(moved), transcendentals=0
        ),
    )(*hbm, *in_vmem(*arrays))
    return result if len(outs) > 1 else result[0]


def own_row(table, index):
    rows = lax.broadcasted_iota(jnp.int32, table.shape, 0)
    return jnp.sum(jnp.where(rows == index, table, 0), axis=0, keepdims=True)


def onehot(flags):
    return flags.astype(F32).astype(BF)


def compact_onehot(table, out_ref):
    shards, slots = table.shape
    live = (table >= 0).astype(jnp.int32)
    counts = jnp.sum(live, axis=1, keepdims=True)
    row = lax.broadcasted_iota(jnp.int32, (out_ref.shape[0], slots), 0)
    place = lax.broadcasted_iota(jnp.int32, (1, slots), 1)
    for s in range(shards):
        here = (row == place) & (table[s : s + 1] >= 0)
        out_ref[:, s * slots : (s + 1) * slots] = onehot(here)
        place = place + counts[s : s + 1]


def pick_kernel(
    tok_hbm, query_hbm, source_hbm, keep_ref, send_ref, tok_ref, query_ref, source_ref, sems
):
    copies = [
        pltpu.make_async_copy(*ends, sems.at[i])
        for i, ends in enumerate(
            ((query_hbm, query_ref), (source_hbm, source_ref), (tok_hbm, tok_ref))
        )
    ]
    for copy in copies:
        copy.start()
    seq_index, odd = lax.axis_index("seq"), lax.axis_index("head") % 2
    copies[0].wait()
    copies[1].wait()
    own_q = own_row(query_ref[...], seq_index)
    own_s = own_row(source_ref[...], seq_index)
    spot = lax.broadcasted_iota(jnp.int32, (tok_ref.shape[0], own_q.shape[1]), 0)
    chosen = [onehot(spot == jnp.where(odd == k, own_q, own_s)) for k in range(2)]
    copies[2].wait()
    for ref, rows in zip((keep_ref, send_ref), chosen):
        ref[...] = lax.dot_general(rows, tok_ref[...], FIRST, preferred_element_type=F32).astype(
            BF
        )


def prepare_kernel(
    query_ref, source_ref, gate_ref, mine_ref, query_map_ref, own_map_ref, gate_map_ref
):
    odd = lax.axis_index("head") % 2
    query, source = query_ref[...], source_ref[...]
    compact_onehot(query, query_map_ref)
    compact_onehot(jnp.where(odd == 0, query, source), mine_ref)
    own_q = own_row(query, lax.axis_index("seq"))
    spot = lax.broadcasted_iota(jnp.int32, own_map_ref.shape, 0)
    own_map_ref[...] = onehot(spot == own_q)
    slots = own_q.shape[1]
    diagonal = lax.broadcasted_iota(jnp.int32, (slots, slots), 0) == lax.broadcasted_iota(
        jnp.int32, (slots, slots), 1
    )
    gate = jnp.sum(jnp.where(diagonal, gate_ref[...], 0.0), axis=1, keepdims=True)
    gate_map_ref[...] = jnp.broadcast_to(gate, gate_map_ref.shape)


def spread_kernel(*refs):
    *pieces, out_ref = refs
    head = lax.axis_index("head")
    width = out_ref.shape[2]
    per = out_ref.shape[0] // len(pieces)
    for j, piece in enumerate(pieces):
        owner = head ^ j
        for i in range(per):
            out_ref[owner * per + i] = piece[:, i * width : (i + 1) * width]


def compact_kernel(slots_ref, chosen_ref, out_ref):
    rows = slots_ref[...].reshape(-1, slots_ref.shape[2])
    out_ref[...] = jnp.dot(chosen_ref[...], rows, preferred_element_type=F32).astype(BF)


def project_kernel(mine_ref, other_ref, weight_ref, out_ref):
    odd = lax.axis_index("head") % 2
    mine, other = mine_ref[...], other_ref[...]
    query = jnp.where(odd == 0, mine, other)
    source = jnp.where(odd == 0, other, mine)
    for c, rows in enumerate((query, source, source)):
        part = jnp.dot(rows, weight_ref[c], preferred_element_type=F32).astype(BF)
        for g in range(out_ref.shape[0]):
            out_ref[g, c] = part[:, g * HD : (g + 1) * HD]


def one_head(query, key, value):
    scores = lax.dot_general(query, key, LAST, preferred_element_type=F32) / math.sqrt(HD)
    expanded = jnp.exp(scores - jnp.max(scores, axis=-1, keepdims=True))
    totals = jnp.sum(expanded, axis=-1, keepdims=True)
    weighted = jnp.dot(expanded.astype(BF), value, preferred_element_type=F32)
    return (weighted / totals).astype(BF)


def heavy_attend_kernel(parts_ref, out_ref):
    total = parts_ref[0].astype(F32)
    for s in range(1, parts_ref.shape[0]):
        total = total + parts_ref[s].astype(F32)
    total = total.astype(BF)
    result = one_head(total[0], total[1], total[2])
    for s in range(out_ref.shape[0]):
        out_ref[s] = result


def heavy_output_kernel(heads_ref, weight_ref, chosen_ref, out_ref):
    rows = jnp.concatenate([heads_ref[g] for g in range(heads_ref.shape[0])], axis=1)
    part = jnp.dot(rows, weight_ref[...], preferred_element_type=F32).astype(BF)
    spread = lax.dot_general(chosen_ref[...], part, FIRST, preferred_element_type=F32).astype(BF)
    out_ref[...] = spread.reshape(out_ref.shape)


def give_kernel(back_ref, out_ref):
    head = lax.axis_index("head")
    per = out_ref.shape[1]
    for i, j in enumerate((1, 3)):
        out_ref[i] = back_ref[pl.ds((head ^ j) * per, per)]


def far_kernel(back_ref, got_ref, out_ref):
    per = out_ref.shape[0]
    far = lax.axis_index("head") ^ 2
    out_ref[...] = (
        back_ref[pl.ds(far * per, per)].astype(F32) + got_ref[1].astype(F32)
    ).astype(BF)


def finish_kernel(
    light_ref, light_far_ref, back_ref, got_ref, last_ref, own_map_ref, gate_ref, out_ref
):
    head = lax.axis_index("head")
    per = last_ref.shape[0]
    heavy = (
        back_ref[pl.ds(head * per, per)].astype(F32)
        + got_ref[0].astype(F32)
        + last_ref[...].astype(F32)
    )
    chosen, gate = own_map_ref[...], gate_ref[:, :1]
    width = heavy.shape[2]
    for j in range(per):
        scaled = heavy[j] * gate
        coarse = scaled.astype(BF)
        fine = (scaled - coarse.astype(F32)).astype(BF)
        added = jnp.dot(chosen, coarse, preferred_element_type=F32) + jnp.dot(
            chosen, fine, preferred_element_type=F32
        )
        cols = slice(j * width, (j + 1) * width)
        light = light_ref[:, cols] + light_far_ref[:, cols].astype(F32)
        out_ref[:, cols] = (light + added).astype(BF)


def light_kernel(*refs):
    count = len(refs) - 9
    pieces, (w_in, w_out, heads_ref, give_ref, *held) = refs[:count], refs[count:]
    tok_ref, in_ref, out_ref, sems, gave_sems = held
    head = lax.axis_index("head")
    depth = pieces[0].shape[1]
    width = give_ref.shape[2]

    def rows(j):
        return pl.ds(pl.multiple_of((head ^ j) * depth, depth), depth)

    def cols(j):
        return pl.ds(pl.multiple_of((head ^ j) * width, width), width)

    copies = []
    for j, piece in enumerate(pieces):
        copies.append(pltpu.make_async_copy(piece, tok_ref.at[j], sems.at[0, j]))
        for c in range(3):
            copies.append(
                pltpu.make_async_copy(
                    w_in.at[c, rows(j), :], in_ref.at[c, j], sems.at[1 + c, j]
                )
            )
    late = [
        pltpu.make_async_copy(w_out.at[:, cols(j)], out_ref.at[i], gave_sems.at[i])
        for i, j in enumerate((1, 3))
    ]
    for copy in copies + late:
        copy.start()
    total = [None] * 3
    for j in range(count):
        copies[4 * j].wait()
        for c in range(3):
            copies[4 * j + 1 + c].wait()
            part = jnp.dot(tok_ref[j], in_ref[c, j], preferred_element_type=F32)
            total[c] = part if j == 0 else total[c] + part
    mapped = [t.astype(BF) for t in total]
    for b in range(heads_ref.shape[0] // LB):
        for g in range(heads_ref.shape[1] // HD):
            at = (slice(b * LB, (b + 1) * LB), slice(g * HD, (g + 1) * HD))
            heads_ref[at] = one_head(*(m[at] for m in mapped))
    for i in range(2):
        late[i].wait()
        give_ref[i] = jnp.dot(
            heads_ref[...], out_ref[i], preferred_element_type=F32
        ).astype(BF)


def light_own_kernel(w_out, got, heads_ref, own_ref, far_ref, out_ref, got_ref, sems):
    head = lax.axis_index("head")
    width = own_ref.shape[1]
    copies = []
    for i, j in enumerate((0, 2)):
        cols = pl.ds(pl.multiple_of((head ^ j) * width, width), width)
        copies.append(pltpu.make_async_copy(w_out.at[:, cols], out_ref.at[i], sems.at[0, i]))
        copies.append(pltpu.make_async_copy(got.at[i], got_ref.at[i], sems.at[1, i]))
    for copy in copies:
        copy.start()
    for i, ref in enumerate((own_ref, far_ref)):
        copies[2 * i].wait()
        copies[2 * i + 1].wait()
        block = jnp.dot(heads_ref[...], out_ref[i], preferred_element_type=F32)
        ref[...] = (block + got_ref[i].astype(F32)).astype(ref.dtype)


def one_head_a_device(
    tokens,
    light_input,
    light_output,
    heavy_input,
    heavy_output,
    query_tokens,
    context_tokens,
    query_gate,
):
    seq_count, head_count = lax.axis_size("seq"), lax.axis_size("head")
    tok_rows, own_width = tokens.shape
    slots = query_tokens.shape[1]
    routed = seq_count * tok_rows // ROUTE
    part_width, head_cols = heavy_input.shape[1:]
    out_cols = heavy_output.shape[1]
    light_cols = light_input.shape[2]
    per = seq_count // head_count
    pair, across, diagonal = (
        [(i, i ^ j) for i in range(head_count)] for j in (1, 2, 3)
    )

    def swap(x):
        return lax.all_to_all(x, "seq", split_axis=0, concat_axis=0, tiled=True)

    keep, send, tokens = on_chip(
        pick_kernel,
        [((slots, own_width), BF)] * 2 + [(tokens.shape, BF)],
        hbm=(tokens, query_tokens, context_tokens),
        scratch=[pltpu.VMEM(query_tokens.shape, jnp.int32)] * 2 + [pltpu.SemaphoreType.DMA((3,))],
    )
    pieces = (
        keep,
        lax.ppermute(send, "head", pair),
        lax.ppermute(keep, "head", across),
        lax.ppermute(send, "head", diagonal),
    )
    spread = on_chip(spread_kernel, [((seq_count, slots, part_width), BF)], *pieces)
    tables = (query_tokens, context_tokens, query_gate)
    spread, tables, tokens = lax.optimization_barrier((spread, tables, tokens))
    mine_map, query_map, own_map, gate_map = on_chip(
        prepare_kernel,
        [((routed, seq_count * slots), BF)] * 2 + [((tok_rows, slots), BF), ((slots, HD), F32)],
        *tables,
    )
    token_far = lax.ppermute(tokens, "head", across)
    token_pair = lax.ppermute(tokens, "head", pair)
    token_last = lax.ppermute(token_far, "head", pair)
    spread = swap(spread)
    spread, mine_map = lax.optimization_barrier((spread, mine_map))
    mine = on_chip(compact_kernel, [((routed, part_width), BF)], spread, mine_map)
    other = lax.ppermute(mine, "head", pair)
    parts = on_chip(
        project_kernel, [((seq_count, 3, routed, HD), BF)], mine, other, heavy_input
    )

    parts, token_pieces = lax.optimization_barrier(
        (parts, (tokens, token_pair, token_far, token_last))
    )
    light_heads, light_give = on_chip(
        light_kernel,
        [((tok_rows, light_cols), BF), ((2, tok_rows, own_width), BF)],
        hbm=(*token_pieces, light_input, light_output),
        scratch=[
            pltpu.VMEM((head_count, tok_rows, own_width), BF),
            pltpu.VMEM((3, head_count, own_width, light_cols), BF),
            pltpu.VMEM((2, light_cols, own_width), BF),
            pltpu.SemaphoreType.DMA((4, head_count)),
            pltpu.SemaphoreType.DMA((2,)),
        ],
        flops=6 * tok_rows * light_cols * own_width * head_count,
        off=True,
    )
    parts = swap(parts)
    parts, light_heads, light_give = lax.optimization_barrier((parts, light_heads, light_give))
    heads = on_chip(heavy_attend_kernel, [((seq_count, routed, HD), BF)], parts)
    light_got = lax.ppermute(light_give, "head", pair)
    light_own, light_far = on_chip(
        light_own_kernel,
        [((tok_rows, own_width), F32), ((tok_rows, own_width), BF)],
        light_heads,
        hbm=(light_output, light_got),
        scratch=[
            pltpu.VMEM((2, light_cols, own_width), BF),
            pltpu.VMEM((2, tok_rows, own_width), BF),
            pltpu.SemaphoreType.DMA((2, 2)),
        ],
        flops=4 * tok_rows * light_cols * own_width,
        off=True,
    )
    heads = swap(heads)
    heads, light_own, light_far = lax.optimization_barrier((heads, light_own, light_far))
    light_far = lax.ppermute(light_far, "head", across)

    back = swap(
        on_chip(
            heavy_output_kernel,
            [((seq_count, slots, out_cols), BF)],
            heads,
            heavy_output,
            query_map,
        )
    )
    give = on_chip(give_kernel, [((2, per, slots, out_cols), BF)], back)
    got = lax.ppermute(give, "head", pair)
    far = on_chip(far_kernel, [((per, slots, out_cols), BF)], back, got)
    last = lax.ppermute(far, "head", across)
    return on_chip(
        finish_kernel,
        [((tok_rows, own_width), BF)],
        light_own,
        light_far,
        back,
        got,
        last,
        own_map,
        gate_map,
        off=True,
    )


def solution(mesh):
    placed = (
        P("seq", "head"),
        P(None, None, "head"),
        P("head", None),
        P(None, "seq", "head"),
        P("head", "seq"),
        P(),
        P(),
        P("seq", None),
    )

    def per_device(*args):
        seq_count, head_count = mesh.shape["seq"], mesh.shape["head"]
        local_heads = args[3].shape[2] // HD
        fits = head_count // 2 == 2 and seq_count % head_count == 0 and local_heads == seq_count
        return (one_head_a_device if fits else general)(*args)

    return jax.shard_map(
        per_device, mesh=mesh, in_specs=placed, out_specs=P("seq", "head"), check_vma=False
    )
```

```python
import functools
import math

import jax
import jax.numpy as jnp
from jax import lax
from jax.experimental import pallas as pl
from jax.experimental.pallas import tpu as pltpu
from jax.sharding import PartitionSpec as P

HD = 128
LB = 128
ROUTE = 32
BF = jnp.bfloat16
F32 = jnp.float32
VMEM = pl.BlockSpec(memory_space=pltpu.VMEM)
FIRST = (((0,), (0,)), ((), ()))
LAST = (((1,), (1,)), ((), ()))


def attend(queries, key_rows, value_rows):
    scores = jnp.einsum(
        "bqhe,bkhe->bhqk", queries, key_rows, preferred_element_type=jnp.float32
    ) / math.sqrt(queries.shape[-1])
    highest = jnp.max(scores, axis=-1, keepdims=True)
    expanded = jnp.exp(scores - highest)
    totals = jnp.sum(expanded, axis=-1)
    weighted = jnp.einsum(
        "bhqk,bkhe->bqhe",
        expanded.astype(jnp.bfloat16),
        value_rows,
        preferred_element_type=jnp.float32,
    )
    return (weighted / jnp.transpose(totals, (0, 2, 1))[..., None]).astype(jnp.bfloat16)


def routed_map(table, routed):
    counts = jnp.sum((table >= 0).astype(jnp.int32), axis=1)
    shard = jnp.arange(table.shape[0], dtype=jnp.int32)
    upper_end = jnp.sum(jnp.where(shard[None, :] <= shard[:, None], counts[None, :], 0), axis=1)
    lower_end = upper_end - counts
    compact_rows = jnp.arange(routed, dtype=jnp.int32)
    source_shard = jnp.sum((upper_end[None, :] <= compact_rows[:, None]).astype(jnp.int32), axis=1)
    onehot_shard = (
        source_shard[:, None] == jnp.arange(table.shape[0], dtype=jnp.int32)[None, :]
    ).astype(jnp.int32)
    within = compact_rows - jnp.sum(onehot_shard * lower_end[None, :], axis=1)
    return (source_shard * table.shape[1] + within, lower_end)


def project(query_part, source_part, weights):
    stacked = jnp.stack((query_part, source_part, source_part))
    return jnp.einsum("cmd,cdw->mcw", stacked, weights, preferred_element_type=jnp.float32)


def pick_rows(gathered, own_list):
    chosen = jnp.take(gathered, jnp.maximum(own_list, 0), axis=0)
    return jnp.where((own_list >= 0)[:, None], chosen, jnp.zeros_like(chosen))


def general(
    tokens,
    light_input,
    light_output,
    heavy_input,
    heavy_output,
    query_tokens,
    context_tokens,
    query_gate,
):
    gathered = lax.all_gather(tokens, "head", axis=1, tiled=True)
    tok_rows = gathered.shape[0]
    light_mapped = jnp.einsum(
        "td,cdw->ctw", gathered, light_input, preferred_element_type=jnp.float32
    ).astype(jnp.bfloat16)
    light_blocks = light_mapped.reshape(3, tok_rows // LB, LB, -1, HD)
    light_heads = attend(light_blocks[0], light_blocks[1], light_blocks[2]).reshape(tok_rows, -1)
    light_part = jnp.dot(light_heads, light_output, preferred_element_type=jnp.float32)
    seq_count = lax.axis_size("seq")
    routed = seq_count * tok_rows // ROUTE
    slot_count = query_tokens.shape[1]
    seq_index = lax.axis_index("seq")
    own_queries = lax.dynamic_index_in_dim(query_tokens, seq_index, 0, keepdims=False)
    own_sources = lax.dynamic_index_in_dim(context_tokens, seq_index, 0, keepdims=False)
    query_cols, source_cols = (
        lax.all_to_all(
            pick_rows(gathered, own_queries), "seq", split_axis=1, concat_axis=0, tiled=True
        ),
        lax.all_to_all(
            pick_rows(gathered, own_sources), "seq", split_axis=1, concat_axis=0, tiled=True
        ),
    )
    query_index, query_lower = routed_map(query_tokens, routed)
    source_index = routed_map(context_tokens, routed)[0]
    query_rows = jnp.take(query_cols, query_index, axis=0)
    source_rows = jnp.take(source_cols, source_index, axis=0)
    summed = lax.psum(project(query_rows, source_rows, heavy_input), "seq").astype(jnp.bfloat16)
    heavy_heads = attend(
        summed[:, 0].reshape(1, routed, -1, HD),
        summed[:, 1].reshape(1, routed, -1, HD),
        summed[:, 2].reshape(1, routed, -1, HD),
    ).reshape(routed, -1)
    heavy_part = jnp.dot(heavy_heads, heavy_output, preferred_element_type=jnp.float32)
    slot_live = query_tokens >= 0
    compact = query_lower[:, None] + jnp.arange(slot_count, dtype=jnp.int32)[None, :]
    outgoing = jnp.take(heavy_part, jnp.where(slot_live, compact, 0).reshape(-1), axis=0)
    outgoing = jnp.where(slot_live.reshape(-1)[:, None], outgoing, jnp.zeros_like(outgoing))
    returned = lax.all_to_all(
        outgoing.astype(jnp.bfloat16), "seq", split_axis=0, concat_axis=1, tiled=True
    ).astype(outgoing.dtype)
    scaled = returned * query_gate[0][:, None]
    targets = jnp.where(own_queries >= 0, own_queries, tok_rows)
    combined = light_part.at[targets].add(scaled, mode="drop")
    return lax.psum_scatter(combined.astype(jnp.bfloat16), "head", scatter_dimension=1, tiled=True)


def in_vmem(*arrays):
    return tuple(pltpu.with_memory_space_constraint(a, pltpu.VMEM) for a in arrays)


def on_chip(kernel, outs, *arrays, hbm=(), scratch=(), flops=0, moved=0, off=False):
    made = [(jax.ShapeDtypeStruct if off else pltpu.VMEM)(*o) for o in outs]
    result = pl.pallas_call(
        kernel,
        in_specs=[pl.BlockSpec(memory_space=pl.ANY)] * len(hbm) + [VMEM] * len(arrays),
        scratch_shapes=list(scratch),
        out_specs=[VMEM] * len(made),
        out_shape=made,
        compiler_params=pltpu.CompilerParams(vmem_limit_bytes=(60 if hbm else 8) << 20),
        cost_estimate=pl.CostEstimate(
            flops=int(flops), bytes_accessed=int(moved), transcendentals=0
        ),
    )(*hbm, *in_vmem(*arrays))
    return result if len(outs) > 1 else result[0]


def own_row(table, index):
    rows = lax.broadcasted_iota(jnp.int32, table.shape, 0)
    return jnp.sum(jnp.where(rows == index, table, 0), axis=0, keepdims=True)


def onehot(flags):
    return flags.astype(F32).astype(BF)


def compact_onehot(table, out_ref):
    shards, slots = table.shape
    live = (table >= 0).astype(jnp.int32)
    counts = jnp.sum(live, axis=1, keepdims=True)
    row = lax.broadcasted_iota(jnp.int32, (out_ref.shape[0], slots), 0)
    place = lax.broadcasted_iota(jnp.int32, (1, slots), 1)
    for s in range(shards):
        here = (row == place) & (table[s : s + 1] >= 0)
        out_ref[:, s * slots : (s + 1) * slots] = onehot(here)
        place = place + counts[s : s + 1]


def pick_kernel(
    tok_hbm,
    query_hbm,
    source_hbm,
    gate_hbm,
    keep_ref,
    send_ref,
    mine_ref,
    query_map_ref,
    own_map_ref,
    gate_map_ref,
    tok_ref,
    query_ref,
    source_ref,
    gate_ref,
    sems,
):
    ends = (
        (query_hbm, query_ref),
        (source_hbm, source_ref),
        (gate_hbm, gate_ref),
        (tok_hbm, tok_ref),
    )
    copies = [pltpu.make_async_copy(*e, sems.at[i]) for i, e in enumerate(ends)]
    for copy in copies:
        copy.start()
    odd = lax.axis_index("head") % 2
    for copy in copies[:3]:
        copy.wait()
    query, source = query_ref[...], source_ref[...]
    own_q = own_row(query, lax.axis_index("seq"))
    own_s = own_row(source, lax.axis_index("seq"))
    spot = lax.broadcasted_iota(jnp.int32, own_map_ref.shape, 0)
    chosen = [onehot(spot == jnp.where(odd == k, own_q, own_s)) for k in range(2)]
    own_map_ref[...] = onehot(spot == own_q)
    compact_onehot(query, query_map_ref)
    compact_onehot(jnp.where(odd == 0, query, source), mine_ref)
    slots = own_q.shape[1]
    diagonal = lax.broadcasted_iota(jnp.int32, (slots, slots), 0) == lax.broadcasted_iota(
        jnp.int32, (slots, slots), 1
    )
    gate = jnp.sum(jnp.where(diagonal, gate_ref[...], 0.0), axis=1, keepdims=True)
    gate_map_ref[...] = jnp.broadcast_to(gate, gate_map_ref.shape)
    copies[3].wait()
    for ref, rows in zip((keep_ref, send_ref), chosen):
        ref[...] = lax.dot_general(rows, tok_ref[...], FIRST, preferred_element_type=F32).astype(
            BF
        )


def spread_kernel(keep_ref, got_ref, out_ref):
    odd = lax.axis_index("head") % 2
    keep, got = keep_ref[...], got_ref[...]
    width = out_ref.shape[2]
    per = keep.shape[1] // width
    for part, block in enumerate((jnp.where(odd == 0, keep, got), jnp.where(odd == 0, got, keep))):
        for i in range(per):
            for at in range(part * per + i, out_ref.shape[0], 2 * per):
                out_ref[at] = block[:, i * width : (i + 1) * width]


def compact_kernel(slots_ref, chosen_ref, out_ref):
    rows = slots_ref[...].reshape(-1, slots_ref.shape[2])
    out_ref[...] = jnp.dot(chosen_ref[...], rows, preferred_element_type=F32).astype(BF)


def choose_kernel(mine_ref, crossed_ref, out_ref):
    pairs = lax.axis_size("head") // 2
    holder = lax.axis_index("seq") * pairs // lax.axis_size("seq")
    out_ref[...] = jnp.where(holder == lax.axis_index("head") // 2, mine_ref[...], crossed_ref[...])


def project_kernel(mine_ref, other_ref, weight_ref, out_ref):
    odd = lax.axis_index("head") % 2
    mine, other = mine_ref[...], other_ref[...]
    query = jnp.where(odd == 0, mine, other)
    source = jnp.where(odd == 0, other, mine)
    for c, rows in enumerate((query, source, source)):
        part = jnp.dot(rows, weight_ref[c], preferred_element_type=F32).astype(BF)
        for g in range(out_ref.shape[0]):
            out_ref[g, c] = part[:, g * HD : (g + 1) * HD]


def one_head(query, key, value):
    scores = lax.dot_general(query, key, LAST, preferred_element_type=F32) / math.sqrt(HD)
    expanded = jnp.exp(scores - jnp.max(scores, axis=-1, keepdims=True))
    totals = jnp.sum(expanded, axis=-1, keepdims=True)
    weighted = jnp.dot(expanded.astype(BF), value, preferred_element_type=F32)
    return (weighted / totals).astype(BF)


def heavy_attend_kernel(parts_ref, out_ref):
    total = parts_ref[0].astype(F32)
    for s in range(1, parts_ref.shape[0]):
        total = total + parts_ref[s].astype(F32)
    total = total.astype(BF)
    result = one_head(total[0], total[1], total[2])
    for s in range(out_ref.shape[0]):
        out_ref[s] = result


def heavy_output_kernel(heads_ref, weight_ref, chosen_ref, out_ref):
    rows = jnp.concatenate([heads_ref[g] for g in range(heads_ref.shape[0])], axis=1)
    part = jnp.dot(rows, weight_ref[...], preferred_element_type=F32).astype(BF)
    spread = lax.dot_general(chosen_ref[...], part, FIRST, preferred_element_type=F32).astype(BF)
    out_ref[...] = spread.reshape(out_ref.shape)


def give_kernel(back_ref, out_ref):
    head = lax.axis_index("head")
    per = out_ref.shape[1]
    for i, j in enumerate((1, 3)):
        out_ref[i] = back_ref[pl.ds((head ^ j) * per, per)]


def far_kernel(back_ref, got_ref, out_ref):
    per = out_ref.shape[0]
    far = lax.axis_index("head") ^ 2
    out_ref[...] = (
        back_ref[pl.ds(far * per, per)].astype(F32) + got_ref[1].astype(F32)
    ).astype(BF)


def finish_kernel(
    light_ref, light_far_ref, back_ref, got_ref, last_ref, own_map_ref, gate_ref, out_ref
):
    head = lax.axis_index("head")
    per = last_ref.shape[0]
    heavy = (
        back_ref[pl.ds(head * per, per)].astype(F32)
        + got_ref[0].astype(F32)
        + last_ref[...].astype(F32)
    )
    chosen, gate = own_map_ref[...], gate_ref[:, :1]
    width = heavy.shape[2]
    for j in range(per):
        scaled = heavy[j] * gate
        coarse = scaled.astype(BF)
        fine = (scaled - coarse.astype(F32)).astype(BF)
        added = jnp.dot(chosen, coarse, preferred_element_type=F32) + jnp.dot(
            chosen, fine, preferred_element_type=F32
        )
        cols = slice(j * width, (j + 1) * width)
        light = light_ref[:, cols] + light_far_ref[:, cols].astype(F32)
        out_ref[:, cols] = (light + added).astype(BF)


def light_kernel(flips, last, *refs):
    count = len(flips)
    pieces, (w_in, *refs) = refs[:count], refs[count:]
    if last:
        before, w_out, heads_ref, give_ref, before_ref, out_ref, *refs = refs
    else:
        sum_ref, *refs = refs
    tok_ref, in_ref, sems = refs[:3]
    head = lax.axis_index("head")
    depth = pieces[0].shape[1]
    copies = []
    for i, (j, piece) in enumerate(zip(flips, pieces)):
        rows = pl.ds(pl.multiple_of((head ^ j) * depth, depth), depth)
        copies.append(pltpu.make_async_copy(piece, tok_ref.at[i], sems.at[0, i]))
        for c in range(3):
            copies.append(
                pltpu.make_async_copy(w_in.at[c, rows, :], in_ref.at[c, i], sems.at[1 + c, i])
            )
    late = []
    if last:
        late_sems = refs[3]
        width = give_ref.shape[2]
        late.append(pltpu.make_async_copy(before, before_ref, late_sems.at[2]))
        for i, j in enumerate((1, 3)):
            cols = pl.ds(pl.multiple_of((head ^ j) * width, width), width)
            late.append(pltpu.make_async_copy(w_out.at[:, cols], out_ref.at[i], late_sems.at[i]))
    for copy in copies + late:
        copy.start()
    total = [None] * 3
    for i in range(count):
        copies[4 * i].wait()
        for c in range(3):
            copies[4 * i + 1 + c].wait()
            part = jnp.dot(tok_ref[i], in_ref[c, i], preferred_element_type=F32)
            total[c] = part if i == 0 else total[c] + part
    if not last:
        for c in range(3):
            sum_ref[c] = total[c]
        return
    late[0].wait()
    mapped = [(before_ref[c] + total[c]).astype(BF) for c in range(3)]
    for b in range(heads_ref.shape[0] // LB):
        for g in range(heads_ref.shape[1] // HD):
            at = (slice(b * LB, (b + 1) * LB), slice(g * HD, (g + 1) * HD))
            heads_ref[at] = one_head(*(m[at] for m in mapped))
    for i in range(2):
        late[1 + i].wait()
        give_ref[i] = jnp.dot(heads_ref[...], out_ref[i], preferred_element_type=F32).astype(BF)


def light_own_kernel(w_out, got_ref, heads_ref, own_ref, far_ref, out_ref, sems):
    head = lax.axis_index("head")
    width = own_ref.shape[1]
    copies = []
    for i, j in enumerate((0, 2)):
        cols = pl.ds(pl.multiple_of((head ^ j) * width, width), width)
        copies.append(pltpu.make_async_copy(w_out.at[:, cols], out_ref.at[i], sems.at[i]))
    for copy in copies:
        copy.start()
    for i, ref in enumerate((own_ref, far_ref)):
        copies[i].wait()
        block = jnp.dot(heads_ref[...], out_ref[i], preferred_element_type=F32)
        ref[...] = (block + got_ref[i].astype(F32)).astype(ref.dtype)


def light_call(flips, last, outs, pieces, *arrays, scratch=()):
    count = len(flips)
    rows, width = pieces[0].shape
    return on_chip(
        functools.partial(light_kernel, flips, last),
        outs,
        hbm=(*pieces, *arrays),
        scratch=[
            *scratch,
            pltpu.VMEM((count, rows, width), BF),
            pltpu.VMEM((3, count, width, arrays[0].shape[2]), BF),
            pltpu.SemaphoreType.DMA((4, count)),
            pltpu.SemaphoreType.DMA((3,)),
        ],
        flops=6 * count * rows * width * arrays[0].shape[2],
        off=True,
    )


def one_head_a_device(
    tokens,
    light_input,
    light_output,
    heavy_input,
    heavy_output,
    query_tokens,
    context_tokens,
    query_gate,
):
    seq_count, head_count = lax.axis_size("seq"), lax.axis_size("head")
    tok_rows, own_width = tokens.shape
    slots = query_tokens.shape[1]
    routed = seq_count * tok_rows // ROUTE
    part_width, head_cols = heavy_input.shape[1:]
    out_cols = heavy_output.shape[1]
    light_cols = light_input.shape[2]
    per = seq_count // head_count
    pair, across = ([(i, i ^ j) for i in range(head_count)] for j in (1, 2))

    def swap(x):
        return lax.all_to_all(x, "seq", split_axis=0, concat_axis=0, tiled=True)

    routes = (routed, seq_count * slots)
    keep, send, mine_map, query_map, own_map, gate_map = on_chip(
        pick_kernel,
        [((slots, own_width), BF)] * 2
        + [(routes, BF)] * 2
        + [((tok_rows, slots), BF), ((slots, HD), F32)],
        hbm=(tokens, query_tokens, context_tokens, query_gate),
        scratch=[
            pltpu.VMEM(tokens.shape, BF),
            pltpu.VMEM(query_tokens.shape, jnp.int32),
            pltpu.VMEM(context_tokens.shape, jnp.int32),
            pltpu.VMEM(query_gate.shape, F32),
            pltpu.SemaphoreType.DMA((4,)),
        ],
    )
    got = lax.ppermute(send, "head", pair)
    spread = on_chip(spread_kernel, [((seq_count, slots, part_width), BF)], keep, got)
    spread, tokens = lax.optimization_barrier((spread, tokens))
    token_far = lax.ppermute(tokens, "head", across)
    token_pair = lax.ppermute(tokens, "head", pair)
    light_sum = light_call(
        (0, 1),
        False,
        [((3, tok_rows, light_cols), F32)],
        (tokens, token_pair),
        light_input,
    )
    spread = swap(spread)
    spread, token_far, light_sum = lax.optimization_barrier((spread, token_far, light_sum))
    token_last = lax.ppermute(token_far, "head", pair)
    mine = on_chip(compact_kernel, [((routed, part_width), BF)], spread, mine_map, moved=20 << 20)
    half = seq_count * 2 // head_count
    holds = [
        (s * head_count + h, s * head_count + (h ^ 2))
        for s in range(seq_count)
        for h in range(head_count)
        if s // half == h // 2
    ]
    crossed = lax.ppermute(mine, ("seq", "head"), holds)
    mine = on_chip(choose_kernel, [((routed, part_width), BF)], mine, crossed)
    other = lax.ppermute(mine, "head", pair)
    parts = on_chip(
        project_kernel, [((seq_count, 3, routed, HD), BF)], mine, other, heavy_input
    )

    parts, light_sum, token_far, token_last = lax.optimization_barrier(
        (parts, light_sum, token_far, token_last)
    )
    light_heads, light_give = light_call(
        (2, 3),
        True,
        [((tok_rows, light_cols), BF), ((2, tok_rows, own_width), BF)],
        (token_far, token_last),
        light_input,
        light_sum,
        light_output,
        scratch=[
            pltpu.VMEM((3, tok_rows, light_cols), F32),
            pltpu.VMEM((2, light_cols, own_width), BF),
        ],
    )
    parts = swap(parts)
    parts, light_heads, light_give = lax.optimization_barrier((parts, light_heads, light_give))
    light_got = lax.ppermute(light_give, "head", pair)
    heads = on_chip(heavy_attend_kernel, [((seq_count, routed, HD), BF)], parts)
    light_own, light_far = on_chip(
        light_own_kernel,
        [((tok_rows, own_width), F32), ((tok_rows, own_width), BF)],
        light_got,
        light_heads,
        hbm=(light_output,),
        scratch=[pltpu.VMEM((2, light_cols, own_width), BF), pltpu.SemaphoreType.DMA((2,))],
        flops=4 * tok_rows * light_cols * own_width,
        off=True,
    )
    heads = swap(heads)
    heads, light_own, light_far = lax.optimization_barrier((heads, light_own, light_far))
    light_far = lax.ppermute(light_far, "head", across)

    back = on_chip(
        heavy_output_kernel,
        [((seq_count, slots, out_cols), BF)],
        heads,
        heavy_output,
        query_map,
    )
    back = swap(back)
    back, light_far = lax.optimization_barrier((back, light_far))
    give = on_chip(give_kernel, [((2, per, slots, out_cols), BF)], back)
    got = lax.ppermute(give, "head", pair)
    far = on_chip(far_kernel, [((per, slots, out_cols), BF)], back, got)
    last = lax.ppermute(far, "head", across)
    return on_chip(
        finish_kernel,
        [((tok_rows, own_width), BF)],
        light_own,
        light_far,
        back,
        got,
        last,
        own_map,
        gate_map,
        off=True,
    )


def solution(mesh):
    placed = (
        P("seq", "head"),
        P(None, None, "head"),
        P("head", None),
        P(None, "seq", "head"),
        P("head", "seq"),
        P(),
        P(),
        P("seq", None),
    )

    def per_device(*args):
        seq_count, head_count = mesh.shape["seq"], mesh.shape["head"]
        local_heads = args[3].shape[2] // HD
        fits = head_count // 2 == 2 and seq_count % head_count == 0 and local_heads == seq_count
        return (one_head_a_device if fits else general)(*args)

    return jax.shard_map(
        per_device, mesh=mesh, in_specs=placed, out_specs=P("seq", "head"), check_vma=False
    )
```

```python
import functools
import math

import jax
import jax.numpy as jnp
from jax import lax
from jax.experimental import pallas as pl
from jax.experimental.pallas import tpu as pltpu
from jax.sharding import PartitionSpec as P

HD = 128
LB = 128
ROUTE = 32
BF = jnp.bfloat16
F32 = jnp.float32
VMEM = pl.BlockSpec(memory_space=pltpu.VMEM)
FIRST = (((0,), (0,)), ((), ()))
LAST = (((1,), (1,)), ((), ()))


def attend(queries, key_rows, value_rows):
    scores = jnp.einsum(
        "bqhe,bkhe->bhqk", queries, key_rows, preferred_element_type=jnp.float32
    ) / math.sqrt(queries.shape[-1])
    highest = jnp.max(scores, axis=-1, keepdims=True)
    expanded = jnp.exp(scores - highest)
    totals = jnp.sum(expanded, axis=-1)
    weighted = jnp.einsum(
        "bhqk,bkhe->bqhe",
        expanded.astype(jnp.bfloat16),
        value_rows,
        preferred_element_type=jnp.float32,
    )
    return (weighted / jnp.transpose(totals, (0, 2, 1))[..., None]).astype(jnp.bfloat16)


def routed_map(table, routed):
    counts = jnp.sum((table >= 0).astype(jnp.int32), axis=1)
    shard = jnp.arange(table.shape[0], dtype=jnp.int32)
    upper_end = jnp.sum(jnp.where(shard[None, :] <= shard[:, None], counts[None, :], 0), axis=1)
    lower_end = upper_end - counts
    compact_rows = jnp.arange(routed, dtype=jnp.int32)
    source_shard = jnp.sum((upper_end[None, :] <= compact_rows[:, None]).astype(jnp.int32), axis=1)
    onehot_shard = (
        source_shard[:, None] == jnp.arange(table.shape[0], dtype=jnp.int32)[None, :]
    ).astype(jnp.int32)
    within = compact_rows - jnp.sum(onehot_shard * lower_end[None, :], axis=1)
    return (source_shard * table.shape[1] + within, lower_end)


def project(query_part, source_part, weights):
    stacked = jnp.stack((query_part, source_part, source_part))
    return jnp.einsum("cmd,cdw->mcw", stacked, weights, preferred_element_type=jnp.float32)


def pick_rows(gathered, own_list):
    chosen = jnp.take(gathered, jnp.maximum(own_list, 0), axis=0)
    return jnp.where((own_list >= 0)[:, None], chosen, jnp.zeros_like(chosen))


def general(
    tokens,
    light_input,
    light_output,
    heavy_input,
    heavy_output,
    query_tokens,
    context_tokens,
    query_gate,
):
    gathered = lax.all_gather(tokens, "head", axis=1, tiled=True)
    tok_rows = gathered.shape[0]
    light_mapped = jnp.einsum(
        "td,cdw->ctw", gathered, light_input, preferred_element_type=jnp.float32
    ).astype(jnp.bfloat16)
    light_blocks = light_mapped.reshape(3, tok_rows // LB, LB, -1, HD)
    light_heads = attend(light_blocks[0], light_blocks[1], light_blocks[2]).reshape(tok_rows, -1)
    light_part = jnp.dot(light_heads, light_output, preferred_element_type=jnp.float32)
    seq_count = lax.axis_size("seq")
    routed = seq_count * tok_rows // ROUTE
    slot_count = query_tokens.shape[1]
    seq_index = lax.axis_index("seq")
    own_queries = lax.dynamic_index_in_dim(query_tokens, seq_index, 0, keepdims=False)
    own_sources = lax.dynamic_index_in_dim(context_tokens, seq_index, 0, keepdims=False)
    query_cols, source_cols = (
        lax.all_to_all(
            pick_rows(gathered, own_queries), "seq", split_axis=1, concat_axis=0, tiled=True
        ),
        lax.all_to_all(
            pick_rows(gathered, own_sources), "seq", split_axis=1, concat_axis=0, tiled=True
        ),
    )
    query_index, query_lower = routed_map(query_tokens, routed)
    source_index = routed_map(context_tokens, routed)[0]
    query_rows = jnp.take(query_cols, query_index, axis=0)
    source_rows = jnp.take(source_cols, source_index, axis=0)
    summed = lax.psum(project(query_rows, source_rows, heavy_input), "seq").astype(jnp.bfloat16)
    heavy_heads = attend(
        summed[:, 0].reshape(1, routed, -1, HD),
        summed[:, 1].reshape(1, routed, -1, HD),
        summed[:, 2].reshape(1, routed, -1, HD),
    ).reshape(routed, -1)
    heavy_part = jnp.dot(heavy_heads, heavy_output, preferred_element_type=jnp.float32)
    slot_live = query_tokens >= 0
    compact = query_lower[:, None] + jnp.arange(slot_count, dtype=jnp.int32)[None, :]
    outgoing = jnp.take(heavy_part, jnp.where(slot_live, compact, 0).reshape(-1), axis=0)
    outgoing = jnp.where(slot_live.reshape(-1)[:, None], outgoing, jnp.zeros_like(outgoing))
    returned = lax.all_to_all(
        outgoing.astype(jnp.bfloat16), "seq", split_axis=0, concat_axis=1, tiled=True
    ).astype(outgoing.dtype)
    scaled = returned * query_gate[0][:, None]
    targets = jnp.where(own_queries >= 0, own_queries, tok_rows)
    combined = light_part.at[targets].add(scaled, mode="drop")
    return lax.psum_scatter(combined.astype(jnp.bfloat16), "head", scatter_dimension=1, tiled=True)


def in_vmem(*arrays):
    return tuple(pltpu.with_memory_space_constraint(a, pltpu.VMEM) for a in arrays)


def on_chip(kernel, outs, *arrays, hbm=(), scratch=(), flops=0, moved=0, off=False):
    made = [(jax.ShapeDtypeStruct if off else pltpu.VMEM)(*o) for o in outs]
    result = pl.pallas_call(
        kernel,
        in_specs=[pl.BlockSpec(memory_space=pl.ANY)] * len(hbm) + [VMEM] * len(arrays),
        scratch_shapes=list(scratch),
        out_specs=[VMEM] * len(made),
        out_shape=made,
        compiler_params=pltpu.CompilerParams(vmem_limit_bytes=(60 if hbm else 8) << 20),
        cost_estimate=pl.CostEstimate(
            flops=int(flops), bytes_accessed=int(moved), transcendentals=0
        ),
    )(*hbm, *in_vmem(*arrays))
    return result if len(outs) > 1 else result[0]


def listed(count):
    inner = sorted(range(count), key=lambda i: 2 * abs(2 * i + 1 - count) // count)
    return [i ^ 1 for i in inner]


def spots(count):
    order = listed(count)
    return [order.index(i) for i in range(count)]


def look_up(values, index):
    found = jnp.int32(values[0])
    for i, value in enumerate(values[1:], 1):
        found = jnp.where(index == i, value, found)
    return found


def own_row(table, index):
    rows = lax.broadcasted_iota(jnp.int32, table.shape, 0)
    return jnp.sum(jnp.where(rows == index, table, 0), axis=0, keepdims=True)


def onehot(flags):
    return flags.astype(F32).astype(BF)


def compact_onehot(table, out_ref):
    shards, slots = table.shape
    spot = spots(shards)
    live = (table >= 0).astype(jnp.int32)
    counts = jnp.sum(live, axis=1, keepdims=True)
    row = lax.broadcasted_iota(jnp.int32, (out_ref.shape[0], slots), 0)
    place = lax.broadcasted_iota(jnp.int32, (1, slots), 1)
    for s in range(shards):
        here = (row == place) & (table[s : s + 1] >= 0)
        out_ref[:, spot[s] * slots : (spot[s] + 1) * slots] = onehot(here)
        place = place + counts[s : s + 1]


def pick_kernel(
    tok_hbm,
    query_hbm,
    source_hbm,
    gate_hbm,
    keep_ref,
    send_ref,
    mine_ref,
    query_map_ref,
    own_map_ref,
    gate_map_ref,
    tok_ref,
    query_ref,
    source_ref,
    gate_ref,
    sems,
):
    ends = (
        (query_hbm, query_ref),
        (source_hbm, source_ref),
        (gate_hbm, gate_ref),
        (tok_hbm, tok_ref),
    )
    copies = [pltpu.make_async_copy(*e, sems.at[i]) for i, e in enumerate(ends)]
    for copy in copies:
        copy.start()
    odd = lax.axis_index("head") % 2
    for copy in copies[:3]:
        copy.wait()
    query, source = query_ref[...], source_ref[...]
    own_q = own_row(query, lax.axis_index("seq"))
    own_s = own_row(source, lax.axis_index("seq"))
    spot = lax.broadcasted_iota(jnp.int32, own_map_ref.shape, 0)
    chosen = [onehot(spot == jnp.where(odd == k, own_q, own_s)) for k in range(2)]
    own_map_ref[...] = onehot(spot == own_q)
    compact_onehot(query, query_map_ref)
    compact_onehot(jnp.where(odd == 0, query, source), mine_ref)
    slots = own_q.shape[1]
    diagonal = lax.broadcasted_iota(jnp.int32, (slots, slots), 0) == lax.broadcasted_iota(
        jnp.int32, (slots, slots), 1
    )
    gate = jnp.sum(jnp.where(diagonal, gate_ref[...], 0.0), axis=1, keepdims=True)
    gate_map_ref[...] = jnp.broadcast_to(gate, gate_map_ref.shape)
    copies[3].wait()
    for ref, rows in zip((keep_ref, send_ref), chosen):
        ref[...] = lax.dot_general(rows, tok_ref[...], FIRST, preferred_element_type=F32).astype(
            BF
        )


def spread_kernel(keep_ref, got_ref, out_ref):
    odd = lax.axis_index("head") % 2
    keep, got = keep_ref[...], got_ref[...]
    width = out_ref.shape[2]
    per = keep.shape[1] // width
    spot = spots(out_ref.shape[0])
    for part, block in enumerate((jnp.where(odd == 0, keep, got), jnp.where(odd == 0, got, keep))):
        for i in range(per):
            for at in range(part * per + i, out_ref.shape[0], 2 * per):
                out_ref[spot[at]] = block[:, i * width : (i + 1) * width]


def compact_kernel(slots_ref, chosen_ref, out_ref):
    rows = slots_ref[...].reshape(-1, slots_ref.shape[2])
    out_ref[...] = jnp.dot(chosen_ref[...], rows, preferred_element_type=F32).astype(BF)


def choose_kernel(mine_ref, crossed_ref, out_ref):
    pairs = lax.axis_size("head") // 2
    holder = lax.axis_index("seq") * pairs // lax.axis_size("seq")
    out_ref[...] = jnp.where(holder == lax.axis_index("head") // 2, mine_ref[...], crossed_ref[...])


def project_kernel(mine_ref, other_ref, weight_ref, out_ref):
    odd = lax.axis_index("head") % 2
    mine, other = mine_ref[...], other_ref[...]
    query = jnp.where(odd == 0, mine, other)
    source = jnp.where(odd == 0, other, mine)
    spot = spots(out_ref.shape[0])
    for c, rows in enumerate((query, source, source)):
        part = jnp.dot(rows, weight_ref[c], preferred_element_type=F32).astype(BF)
        for g in range(out_ref.shape[0]):
            out_ref[spot[g], c] = part[:, g * HD : (g + 1) * HD]


def one_head(query, key, value):
    scores = lax.dot_general(query, key, LAST, preferred_element_type=F32) / math.sqrt(HD)
    expanded = jnp.exp(scores - jnp.max(scores, axis=-1, keepdims=True))
    totals = jnp.sum(expanded, axis=-1, keepdims=True)
    weighted = jnp.dot(expanded.astype(BF), value, preferred_element_type=F32)
    return (weighted / totals).astype(BF)


def heavy_attend_kernel(parts_ref, out_ref):
    total = parts_ref[0].astype(F32)
    for s in range(1, parts_ref.shape[0]):
        total = total + parts_ref[s].astype(F32)
    total = total.astype(BF)
    result = one_head(total[0], total[1], total[2])
    for s in range(out_ref.shape[0]):
        out_ref[s] = result


def heavy_output_kernel(heads_ref, weight_ref, chosen_ref, out_ref):
    rows = jnp.concatenate([heads_ref[i] for i in spots(heads_ref.shape[0])], axis=1)
    part = jnp.dot(rows, weight_ref[...], preferred_element_type=F32).astype(BF)
    spread = lax.dot_general(chosen_ref[...], part, FIRST, preferred_element_type=F32).astype(BF)
    out_ref[...] = spread.reshape(out_ref.shape)


def block_of(back_ref, head, per, i):
    spot = spots(back_ref.shape[0])
    return back_ref[look_up(spot[i::per], head)]


def give_kernel(back_ref, out_ref):
    head = lax.axis_index("head")
    per = out_ref.shape[1]
    for k, j in enumerate((1, 3)):
        for i in range(per):
            out_ref[k, i] = block_of(back_ref, head ^ j, per, i)


def far_kernel(back_ref, got_ref, out_ref):
    per = out_ref.shape[0]
    head = lax.axis_index("head")
    for i in range(per):
        mine = block_of(back_ref, head ^ 2, per, i).astype(F32)
        out_ref[i] = (mine + got_ref[1, i].astype(F32)).astype(BF)


def finish_kernel(
    light_ref, light_far_ref, back_ref, got_ref, last_ref, own_map_ref, gate_ref, out_ref
):
    head = lax.axis_index("head")
    per = last_ref.shape[0]
    chosen, gate = own_map_ref[...], gate_ref[:, :1]
    width = last_ref.shape[2]
    for j in range(per):
        mine = block_of(back_ref, head, per, j).astype(F32)
        scaled = (mine + got_ref[0, j].astype(F32) + last_ref[j].astype(F32)) * gate
        coarse = scaled.astype(BF)
        fine = (scaled - coarse.astype(F32)).astype(BF)
        added = jnp.dot(chosen, coarse, preferred_element_type=F32) + jnp.dot(
            chosen, fine, preferred_element_type=F32
        )
        cols = slice(j * width, (j + 1) * width)
        light = light_ref[:, cols] + light_far_ref[:, cols].astype(F32)
        out_ref[:, cols] = (light + added).astype(BF)


def light_kernel(flips, last, *refs):
    count = len(flips)
    pieces, (w_in, *refs) = refs[:count], refs[count:]
    if last:
        before, w_out, heads_ref, give_ref, before_ref, out_ref, *refs = refs
    else:
        sum_ref, *refs = refs
    tok_ref, in_ref, sems = refs[:3]
    head = lax.axis_index("head")
    depth = pieces[0].shape[1]
    copies = []
    for i, (j, piece) in enumerate(zip(flips, pieces)):
        rows = pl.ds(pl.multiple_of((head ^ j) * depth, depth), depth)
        copies.append(pltpu.make_async_copy(piece, tok_ref.at[i], sems.at[0, i]))
        for c in range(3):
            copies.append(
                pltpu.make_async_copy(w_in.at[c, rows, :], in_ref.at[c, i], sems.at[1 + c, i])
            )
    late = []
    if last:
        late_sems = refs[3]
        width = give_ref.shape[2]
        late.append(pltpu.make_async_copy(before, before_ref, late_sems.at[2]))
        for i, j in enumerate((1, 3)):
            cols = pl.ds(pl.multiple_of((head ^ j) * width, width), width)
            late.append(pltpu.make_async_copy(w_out.at[:, cols], out_ref.at[i], late_sems.at[i]))
    for copy in copies + late:
        copy.start()
    total = [None] * 3
    for i in range(count):
        copies[4 * i].wait()
        for c in range(3):
            copies[4 * i + 1 + c].wait()
            part = jnp.dot(tok_ref[i], in_ref[c, i], preferred_element_type=F32)
            total[c] = part if i == 0 else total[c] + part
    if not last:
        for c in range(3):
            sum_ref[c] = total[c]
        return
    late[0].wait()
    mapped = [(before_ref[c] + total[c]).astype(BF) for c in range(3)]
    for b in range(heads_ref.shape[0] // LB):
        for g in range(heads_ref.shape[1] // HD):
            at = (slice(b * LB, (b + 1) * LB), slice(g * HD, (g + 1) * HD))
            heads_ref[at] = one_head(*(m[at] for m in mapped))
    for i in range(2):
        late[1 + i].wait()
        give_ref[i] = jnp.dot(heads_ref[...], out_ref[i], preferred_element_type=F32).astype(BF)


def light_own_kernel(w_out, got_ref, heads_ref, own_ref, far_ref, out_ref, sems):
    head = lax.axis_index("head")
    width = own_ref.shape[1]
    copies = []
    for i, j in enumerate((0, 2)):
        cols = pl.ds(pl.multiple_of((head ^ j) * width, width), width)
        copies.append(pltpu.make_async_copy(w_out.at[:, cols], out_ref.at[i], sems.at[i]))
    for copy in copies:
        copy.start()
    for i, ref in enumerate((own_ref, far_ref)):
        copies[i].wait()
        block = jnp.dot(heads_ref[...], out_ref[i], preferred_element_type=F32)
        ref[...] = (block + got_ref[i].astype(F32)).astype(ref.dtype)


def light_call(flips, last, outs, pieces, *arrays, scratch=()):
    count = len(flips)
    rows, width = pieces[0].shape
    return on_chip(
        functools.partial(light_kernel, flips, last),
        outs,
        hbm=(*pieces, *arrays),
        scratch=[
            *scratch,
            pltpu.VMEM((count, rows, width), BF),
            pltpu.VMEM((3, count, width, arrays[0].shape[2]), BF),
            pltpu.SemaphoreType.DMA((4, count)),
            pltpu.SemaphoreType.DMA((3,)),
        ],
        flops=6 * count * rows * width * arrays[0].shape[2],
        off=True,
    )


def one_head_a_device(
    tokens,
    light_input,
    light_output,
    heavy_input,
    heavy_output,
    query_tokens,
    context_tokens,
    query_gate,
):
    seq_count, head_count = lax.axis_size("seq"), lax.axis_size("head")
    tok_rows, own_width = tokens.shape
    slots = query_tokens.shape[1]
    routed = seq_count * tok_rows // ROUTE
    part_width, head_cols = heavy_input.shape[1:]
    out_cols = heavy_output.shape[1]
    light_cols = light_input.shape[2]
    per = seq_count // head_count
    pair, across = ([(i, i ^ j) for i in range(head_count)] for j in (1, 2))

    def swap(x):
        return lax.all_to_all(
            x,
            "seq",
            split_axis=0,
            concat_axis=0,
            tiled=True,
            axis_index_groups=[listed(seq_count)],
        )

    routes = (routed, seq_count * slots)
    keep, send, mine_map, query_map, own_map, gate_map = on_chip(
        pick_kernel,
        [((slots, own_width), BF)] * 2
        + [(routes, BF)] * 2
        + [((tok_rows, slots), BF), ((slots, HD), F32)],
        hbm=(tokens, query_tokens, context_tokens, query_gate),
        scratch=[
            pltpu.VMEM(tokens.shape, BF),
            pltpu.VMEM(query_tokens.shape, jnp.int32),
            pltpu.VMEM(context_tokens.shape, jnp.int32),
            pltpu.VMEM(query_gate.shape, F32),
            pltpu.SemaphoreType.DMA((4,)),
        ],
    )
    got = lax.ppermute(send, "head", pair)
    spread = on_chip(spread_kernel, [((seq_count, slots, part_width), BF)], keep, got)
    token_far = lax.ppermute(tokens, "head", across)
    token_pair = lax.ppermute(tokens, "head", pair)
    spread, tokens, token_pair = lax.optimization_barrier((spread, tokens, token_pair))
    light_sum = light_call(
        (0, 1),
        False,
        [((3, tok_rows, light_cols), F32)],
        (tokens, token_pair),
        light_input,
    )
    spread = swap(spread)
    spread, token_far, light_sum = lax.optimization_barrier((spread, token_far, light_sum))
    token_last = lax.ppermute(token_far, "head", pair)
    mine = on_chip(compact_kernel, [((routed, part_width), BF)], spread, mine_map, moved=20 << 20)
    half = seq_count * 2 // head_count
    holds = [
        (s * head_count + h, s * head_count + (h ^ 2))
        for s in range(seq_count)
        for h in range(head_count)
        if s // half == h // 2
    ]
    crossed = lax.ppermute(mine, ("seq", "head"), holds)
    mine = on_chip(choose_kernel, [((routed, part_width), BF)], mine, crossed)
    other = lax.ppermute(mine, "head", pair)
    parts = on_chip(
        project_kernel, [((seq_count, 3, routed, HD), BF)], mine, other, heavy_input
    )

    parts, light_sum, token_far, token_last = lax.optimization_barrier(
        (parts, light_sum, token_far, token_last)
    )
    light_heads, light_give = light_call(
        (2, 3),
        True,
        [((tok_rows, light_cols), BF), ((2, tok_rows, own_width), BF)],
        (token_far, token_last),
        light_input,
        light_sum,
        light_output,
        scratch=[
            pltpu.VMEM((3, tok_rows, light_cols), F32),
            pltpu.VMEM((2, light_cols, own_width), BF),
        ],
    )
    parts = swap(parts)
    parts, light_heads, light_give = lax.optimization_barrier((parts, light_heads, light_give))
    light_got = lax.ppermute(light_give, "head", pair)
    heads = on_chip(heavy_attend_kernel, [((seq_count, routed, HD), BF)], parts)
    light_own, light_far = on_chip(
        light_own_kernel,
        [((tok_rows, own_width), F32), ((tok_rows, own_width), BF)],
        light_got,
        light_heads,
        hbm=(light_output,),
        scratch=[pltpu.VMEM((2, light_cols, own_width), BF), pltpu.SemaphoreType.DMA((2,))],
        flops=4 * tok_rows * light_cols * own_width,
        off=True,
    )
    heads = swap(heads)
    heads, light_own, light_far = lax.optimization_barrier((heads, light_own, light_far))
    light_far = lax.ppermute(light_far, "head", across)

    back = on_chip(
        heavy_output_kernel,
        [((seq_count, slots, out_cols), BF)],
        heads,
        heavy_output,
        query_map,
    )
    back = swap(back)
    give = on_chip(give_kernel, [((2, per, slots, out_cols), BF)], back)
    got = lax.ppermute(give, "head", pair)
    far = on_chip(far_kernel, [((per, slots, out_cols), BF)], back, got)
    far, light_far = lax.optimization_barrier((far, light_far))
    last = lax.ppermute(far, "head", across)
    return on_chip(
        finish_kernel,
        [((tok_rows, own_width), BF)],
        light_own,
        light_far,
        back,
        got,
        last,
        own_map,
        gate_map,
        off=True,
    )


def solution(mesh):
    placed = (
        P("seq", "head"),
        P(None, None, "head"),
        P("head", None),
        P(None, "seq", "head"),
        P("head", "seq"),
        P(),
        P(),
        P("seq", None),
    )

    def per_device(*args):
        seq_count, head_count = mesh.shape["seq"], mesh.shape["head"]
        local_heads = args[3].shape[2] // HD
        fits = head_count // 2 == 2 and seq_count % head_count == 0 and local_heads == seq_count
        return (one_head_a_device if fits else general)(*args)

    return jax.shard_map(
        per_device, mesh=mesh, in_specs=placed, out_specs=P("seq", "head"), check_vma=False
    )
```

```python
import functools
import math

import jax
import jax.numpy as jnp
from jax import lax
from jax.experimental import pallas as pl
from jax.experimental.pallas import tpu as pltpu
from jax.sharding import PartitionSpec as P

HD = 128
LB = 128
ROUTE = 32
BF = jnp.bfloat16
F32 = jnp.float32
VMEM = pl.BlockSpec(memory_space=pltpu.VMEM)
FIRST = (((0,), (0,)), ((), ()))
LAST = (((1,), (1,)), ((), ()))


def attend(queries, key_rows, value_rows):
    scores = jnp.einsum(
        "bqhe,bkhe->bhqk", queries, key_rows, preferred_element_type=jnp.float32
    ) / math.sqrt(queries.shape[-1])
    highest = jnp.max(scores, axis=-1, keepdims=True)
    expanded = jnp.exp(scores - highest)
    totals = jnp.sum(expanded, axis=-1)
    weighted = jnp.einsum(
        "bhqk,bkhe->bqhe",
        expanded.astype(jnp.bfloat16),
        value_rows,
        preferred_element_type=jnp.float32,
    )
    return (weighted / jnp.transpose(totals, (0, 2, 1))[..., None]).astype(jnp.bfloat16)


def routed_map(table, routed):
    counts = jnp.sum((table >= 0).astype(jnp.int32), axis=1)
    shard = jnp.arange(table.shape[0], dtype=jnp.int32)
    upper_end = jnp.sum(jnp.where(shard[None, :] <= shard[:, None], counts[None, :], 0), axis=1)
    lower_end = upper_end - counts
    compact_rows = jnp.arange(routed, dtype=jnp.int32)
    source_shard = jnp.sum((upper_end[None, :] <= compact_rows[:, None]).astype(jnp.int32), axis=1)
    onehot_shard = (
        source_shard[:, None] == jnp.arange(table.shape[0], dtype=jnp.int32)[None, :]
    ).astype(jnp.int32)
    within = compact_rows - jnp.sum(onehot_shard * lower_end[None, :], axis=1)
    return (source_shard * table.shape[1] + within, lower_end)


def project(query_part, source_part, weights):
    stacked = jnp.stack((query_part, source_part, source_part))
    return jnp.einsum("cmd,cdw->mcw", stacked, weights, preferred_element_type=jnp.float32)


def pick_rows(gathered, own_list):
    chosen = jnp.take(gathered, jnp.maximum(own_list, 0), axis=0)
    return jnp.where((own_list >= 0)[:, None], chosen, jnp.zeros_like(chosen))


def general(
    tokens,
    light_input,
    light_output,
    heavy_input,
    heavy_output,
    query_tokens,
    context_tokens,
    query_gate,
):
    gathered = lax.all_gather(tokens, "head", axis=1, tiled=True)
    tok_rows = gathered.shape[0]
    light_mapped = jnp.einsum(
        "td,cdw->ctw", gathered, light_input, preferred_element_type=jnp.float32
    ).astype(jnp.bfloat16)
    light_blocks = light_mapped.reshape(3, tok_rows // LB, LB, -1, HD)
    light_heads = attend(light_blocks[0], light_blocks[1], light_blocks[2]).reshape(tok_rows, -1)
    light_part = jnp.dot(light_heads, light_output, preferred_element_type=jnp.float32)
    seq_count = lax.axis_size("seq")
    routed = seq_count * tok_rows // ROUTE
    slot_count = query_tokens.shape[1]
    seq_index = lax.axis_index("seq")
    own_queries = lax.dynamic_index_in_dim(query_tokens, seq_index, 0, keepdims=False)
    own_sources = lax.dynamic_index_in_dim(context_tokens, seq_index, 0, keepdims=False)
    query_cols, source_cols = (
        lax.all_to_all(
            pick_rows(gathered, own_queries), "seq", split_axis=1, concat_axis=0, tiled=True
        ),
        lax.all_to_all(
            pick_rows(gathered, own_sources), "seq", split_axis=1, concat_axis=0, tiled=True
        ),
    )
    query_index, query_lower = routed_map(query_tokens, routed)
    source_index = routed_map(context_tokens, routed)[0]
    query_rows = jnp.take(query_cols, query_index, axis=0)
    source_rows = jnp.take(source_cols, source_index, axis=0)
    summed = lax.psum(project(query_rows, source_rows, heavy_input), "seq").astype(jnp.bfloat16)
    heavy_heads = attend(
        summed[:, 0].reshape(1, routed, -1, HD),
        summed[:, 1].reshape(1, routed, -1, HD),
        summed[:, 2].reshape(1, routed, -1, HD),
    ).reshape(routed, -1)
    heavy_part = jnp.dot(heavy_heads, heavy_output, preferred_element_type=jnp.float32)
    slot_live = query_tokens >= 0
    compact = query_lower[:, None] + jnp.arange(slot_count, dtype=jnp.int32)[None, :]
    outgoing = jnp.take(heavy_part, jnp.where(slot_live, compact, 0).reshape(-1), axis=0)
    outgoing = jnp.where(slot_live.reshape(-1)[:, None], outgoing, jnp.zeros_like(outgoing))
    returned = lax.all_to_all(
        outgoing.astype(jnp.bfloat16), "seq", split_axis=0, concat_axis=1, tiled=True
    ).astype(outgoing.dtype)
    scaled = returned * query_gate[0][:, None]
    targets = jnp.where(own_queries >= 0, own_queries, tok_rows)
    combined = light_part.at[targets].add(scaled, mode="drop")
    return lax.psum_scatter(combined.astype(jnp.bfloat16), "head", scatter_dimension=1, tiled=True)


def in_vmem(*arrays):
    return tuple(pltpu.with_memory_space_constraint(a, pltpu.VMEM) for a in arrays)


def on_chip(kernel, outs, *arrays, hbm=(), scratch=(), flops=0, moved=0, off=False):
    made = [(jax.ShapeDtypeStruct if off else pltpu.VMEM)(*o) for o in outs]
    result = pl.pallas_call(
        kernel,
        in_specs=[pl.BlockSpec(memory_space=pl.ANY)] * len(hbm) + [VMEM] * len(arrays),
        scratch_shapes=list(scratch),
        out_specs=[VMEM] * len(made),
        out_shape=made,
        compiler_params=pltpu.CompilerParams(vmem_limit_bytes=(60 if hbm else 8) << 20),
        cost_estimate=pl.CostEstimate(
            flops=int(flops), bytes_accessed=int(moved), transcendentals=0
        ),
    )(*hbm, *in_vmem(*arrays))
    return result if len(outs) > 1 else result[0]


def listed(count):
    inner = sorted(range(count), key=lambda i: 2 * abs(2 * i + 1 - count) // count)
    return [i ^ 1 for i in inner]


def spots(count):
    order = listed(count)
    return [order.index(i) for i in range(count)]


def look_up(values, index):
    found = jnp.int32(values[0])
    for i, value in enumerate(values[1:], 1):
        found = jnp.where(index == i, value, found)
    return found


def own_row(table, index):
    rows = lax.broadcasted_iota(jnp.int32, table.shape, 0)
    return jnp.sum(jnp.where(rows == index, table, 0), axis=0, keepdims=True)


def onehot(flags):
    return flags.astype(F32).astype(BF)


def compact_onehot(table, out_ref):
    shards, slots = table.shape
    spot = spots(shards)
    live = (table >= 0).astype(jnp.int32)
    counts = jnp.sum(live, axis=1, keepdims=True)
    row = lax.broadcasted_iota(jnp.int32, (out_ref.shape[0], slots), 0)
    place = lax.broadcasted_iota(jnp.int32, (1, slots), 1)
    for s in range(shards):
        here = (row == place) & (table[s : s + 1] >= 0)
        out_ref[:, spot[s] * slots : (spot[s] + 1) * slots] = onehot(here)
        place = place + counts[s : s + 1]


def pick_kernel(
    tok_hbm,
    query_hbm,
    source_hbm,
    gate_hbm,
    keep_ref,
    send_ref,
    mine_ref,
    query_map_ref,
    own_map_ref,
    gate_map_ref,
    tok_ref,
    query_ref,
    source_ref,
    gate_ref,
    sems,
):
    ends = (
        (query_hbm, query_ref),
        (source_hbm, source_ref),
        (gate_hbm, gate_ref),
        (tok_hbm, tok_ref),
    )
    copies = [pltpu.make_async_copy(*e, sems.at[i]) for i, e in enumerate(ends)]
    for copy in copies:
        copy.start()
    odd = lax.axis_index("head") % 2
    for copy in copies[:3]:
        copy.wait()
    query, source = query_ref[...], source_ref[...]
    own_q = own_row(query, lax.axis_index("seq"))
    own_s = own_row(source, lax.axis_index("seq"))
    spot = lax.broadcasted_iota(jnp.int32, own_map_ref.shape, 0)
    chosen = [onehot(spot == jnp.where(odd == k, own_q, own_s)) for k in range(2)]
    own_map_ref[...] = onehot(spot == own_q)
    compact_onehot(query, query_map_ref)
    compact_onehot(jnp.where(odd == 0, query, source), mine_ref)
    slots = own_q.shape[1]
    diagonal = lax.broadcasted_iota(jnp.int32, (slots, slots), 0) == lax.broadcasted_iota(
        jnp.int32, (slots, slots), 1
    )
    gate = jnp.sum(jnp.where(diagonal, gate_ref[...], 0.0), axis=1, keepdims=True)
    gate_map_ref[...] = jnp.broadcast_to(gate, gate_map_ref.shape)
    copies[3].wait()
    for ref, rows in zip((keep_ref, send_ref), chosen):
        ref[...] = lax.dot_general(rows, tok_ref[...], FIRST, preferred_element_type=F32).astype(
            BF
        )


def spread_kernel(keep_ref, got_ref, out_ref):
    odd = lax.axis_index("head") % 2
    keep, got = keep_ref[...], got_ref[...]
    width = out_ref.shape[2]
    per = keep.shape[1] // width
    spot = spots(out_ref.shape[0])
    for part, block in enumerate((jnp.where(odd == 0, keep, got), jnp.where(odd == 0, got, keep))):
        for i in range(per):
            for at in range(part * per + i, out_ref.shape[0], 2 * per):
                out_ref[spot[at]] = block[:, i * width : (i + 1) * width]


def compact_kernel(slots_ref, chosen_ref, out_ref):
    rows = slots_ref[...].reshape(-1, slots_ref.shape[2])
    out_ref[...] = jnp.dot(chosen_ref[...], rows, preferred_element_type=F32).astype(BF)


def choose_kernel(mine_ref, crossed_ref, out_ref):
    pairs = lax.axis_size("head") // 2
    holder = lax.axis_index("seq") * pairs // lax.axis_size("seq")
    out_ref[...] = jnp.where(holder == lax.axis_index("head") // 2, mine_ref[...], crossed_ref[...])


def project_kernel(mine_ref, other_ref, weight_ref, out_ref):
    odd = lax.axis_index("head") % 2
    mine, other = mine_ref[...], other_ref[...]
    query = jnp.where(odd == 0, mine, other)
    source = jnp.where(odd == 0, other, mine)
    spot = spots(out_ref.shape[0])
    for c, rows in enumerate((query, source, source)):
        part = jnp.dot(rows, weight_ref[c], preferred_element_type=F32).astype(BF)
        for g in range(out_ref.shape[0]):
            out_ref[spot[g], c] = part[:, g * HD : (g + 1) * HD]


def one_head(query, key, value):
    scores = lax.dot_general(query, key, LAST, preferred_element_type=F32) / math.sqrt(HD)
    expanded = jnp.exp(scores - jnp.max(scores, axis=-1, keepdims=True))
    totals = jnp.sum(expanded, axis=-1, keepdims=True)
    weighted = jnp.dot(expanded.astype(BF), value, preferred_element_type=F32)
    return (weighted / totals).astype(BF)


def heavy_attend_kernel(parts_ref, out_ref):
    total = parts_ref[0].astype(F32)
    for s in range(1, parts_ref.shape[0]):
        total = total + parts_ref[s].astype(F32)
    total = total.astype(BF)
    result = one_head(total[0], total[1], total[2])
    for s in range(out_ref.shape[0]):
        out_ref[s] = result


def heavy_output_kernel(heads_ref, weight_ref, chosen_ref, out_ref):
    rows = jnp.concatenate([heads_ref[i] for i in spots(heads_ref.shape[0])], axis=1)
    part = jnp.dot(rows, weight_ref[...], preferred_element_type=F32).astype(BF)
    spread = lax.dot_general(chosen_ref[...], part, FIRST, preferred_element_type=F32).astype(BF)
    out_ref[...] = spread.reshape(out_ref.shape)


def block_of(back_ref, head, per, i):
    spot = spots(back_ref.shape[0])
    return back_ref[look_up(spot[i::per], head)]


def give_kernel(back_ref, out_ref):
    head = lax.axis_index("head")
    per = out_ref.shape[1]
    for k, j in enumerate((1, 3)):
        for i in range(per):
            out_ref[k, i] = block_of(back_ref, head ^ j, per, i)


def far_kernel(back_ref, got_ref, out_ref):
    per = out_ref.shape[0]
    head = lax.axis_index("head")
    for i in range(per):
        mine = block_of(back_ref, head ^ 2, per, i).astype(F32)
        out_ref[i] = (mine + got_ref[1, i].astype(F32)).astype(BF)


def finish_kernel(
    light_ref, light_far_ref, back_ref, got_ref, last_ref, own_map_ref, gate_ref, out_ref
):
    head = lax.axis_index("head")
    per = last_ref.shape[0]
    chosen, gate = own_map_ref[...], gate_ref[:, :1]
    width = last_ref.shape[2]
    for j in range(per):
        mine = block_of(back_ref, head, per, j).astype(F32)
        scaled = (mine + got_ref[0, j].astype(F32) + last_ref[j].astype(F32)) * gate
        coarse = scaled.astype(BF)
        fine = (scaled - coarse.astype(F32)).astype(BF)
        added = jnp.dot(chosen, coarse, preferred_element_type=F32) + jnp.dot(
            chosen, fine, preferred_element_type=F32
        )
        cols = slice(j * width, (j + 1) * width)
        light = light_ref[:, cols] + light_far_ref[:, cols].astype(F32)
        out_ref[:, cols] = (light + added).astype(BF)


def light_kernel(flips, last, *refs):
    count = len(flips)
    pieces, (w_in, *refs) = refs[:count], refs[count:]
    if last:
        before, w_out, heads_ref, give_ref, before_ref, out_ref, *refs = refs
    else:
        sum_ref, *refs = refs
    tok_ref, in_ref, sems = refs[:3]
    head = lax.axis_index("head")
    depth = pieces[0].shape[1]
    copies = []
    for i, (j, piece) in enumerate(zip(flips, pieces)):
        rows = pl.ds(pl.multiple_of((head ^ j) * depth, depth), depth)
        copies.append(pltpu.make_async_copy(piece, tok_ref.at[i], sems.at[0, i]))
        for c in range(3):
            copies.append(
                pltpu.make_async_copy(w_in.at[c, rows, :], in_ref.at[c, i], sems.at[1 + c, i])
            )
    late = []
    if last:
        late_sems = refs[3]
        width = give_ref.shape[2]
        late.append(pltpu.make_async_copy(before, before_ref, late_sems.at[2]))
        for i, j in enumerate((1, 3)):
            cols = pl.ds(pl.multiple_of((head ^ j) * width, width), width)
            late.append(pltpu.make_async_copy(w_out.at[:, cols], out_ref.at[i], late_sems.at[i]))
    for copy in copies + late:
        copy.start()
    total = [None] * 3
    for i in range(count):
        copies[4 * i].wait()
        for c in range(3):
            copies[4 * i + 1 + c].wait()
            part = jnp.dot(tok_ref[i], in_ref[c, i], preferred_element_type=F32)
            total[c] = part if i == 0 else total[c] + part
    if not last:
        for c in range(3):
            sum_ref[c] = total[c]
        return
    late[0].wait()
    mapped = [(before_ref[c] + total[c]).astype(BF) for c in range(3)]
    for b in range(heads_ref.shape[0] // LB):
        for g in range(heads_ref.shape[1] // HD):
            at = (slice(b * LB, (b + 1) * LB), slice(g * HD, (g + 1) * HD))
            heads_ref[at] = one_head(*(m[at] for m in mapped))
    for i in range(2):
        late[1 + i].wait()
        give_ref[i] = jnp.dot(heads_ref[...], out_ref[i], preferred_element_type=F32).astype(BF)


def light_own_kernel(w_out, got_ref, heads_ref, own_ref, far_ref, out_ref, sems):
    head = lax.axis_index("head")
    width = own_ref.shape[1]
    copies = []
    for i, j in enumerate((0, 2)):
        cols = pl.ds(pl.multiple_of((head ^ j) * width, width), width)
        copies.append(pltpu.make_async_copy(w_out.at[:, cols], out_ref.at[i], sems.at[i]))
    for copy in copies:
        copy.start()
    for i, ref in enumerate((own_ref, far_ref)):
        copies[i].wait()
        block = jnp.dot(heads_ref[...], out_ref[i], preferred_element_type=F32)
        ref[...] = (block + got_ref[i].astype(F32)).astype(ref.dtype)


def light_call(flips, last, outs, pieces, *arrays, scratch=()):
    count = len(flips)
    rows, width = pieces[0].shape
    return on_chip(
        functools.partial(light_kernel, flips, last),
        outs,
        hbm=(*pieces, *arrays),
        scratch=[
            *scratch,
            pltpu.VMEM((count, rows, width), BF),
            pltpu.VMEM((3, count, width, arrays[0].shape[2]), BF),
            pltpu.SemaphoreType.DMA((4, count)),
            pltpu.SemaphoreType.DMA((3,)),
        ],
        flops=6 * count * rows * width * arrays[0].shape[2],
        off=True,
    )


def one_head_a_device(
    tokens,
    light_input,
    light_output,
    heavy_input,
    heavy_output,
    query_tokens,
    context_tokens,
    query_gate,
):
    seq_count, head_count = lax.axis_size("seq"), lax.axis_size("head")
    tok_rows, own_width = tokens.shape
    slots = query_tokens.shape[1]
    routed = seq_count * tok_rows // ROUTE
    part_width, head_cols = heavy_input.shape[1:]
    out_cols = heavy_output.shape[1]
    light_cols = light_input.shape[2]
    per = seq_count // head_count
    pair, across = ([(i, i ^ j) for i in range(head_count)] for j in (1, 2))

    def swap(x):
        return lax.all_to_all(
            x,
            "seq",
            split_axis=0,
            concat_axis=0,
            tiled=True,
            axis_index_groups=[listed(seq_count)],
        )

    routes = (routed, seq_count * slots)
    keep, send, mine_map, query_map, own_map, gate_map = on_chip(
        pick_kernel,
        [((slots, own_width), BF)] * 2
        + [(routes, BF)] * 2
        + [((tok_rows, slots), BF), ((slots, HD), F32)],
        hbm=(tokens, query_tokens, context_tokens, query_gate),
        scratch=[
            pltpu.VMEM(tokens.shape, BF),
            pltpu.VMEM(query_tokens.shape, jnp.int32),
            pltpu.VMEM(context_tokens.shape, jnp.int32),
            pltpu.VMEM(query_gate.shape, F32),
            pltpu.SemaphoreType.DMA((4,)),
        ],
    )
    got = lax.ppermute(send, "head", pair)
    spread = on_chip(spread_kernel, [((seq_count, slots, part_width), BF)], keep, got)
    token_far = lax.ppermute(tokens, "head", across)
    token_pair = lax.ppermute(tokens, "head", pair)
    spread, tokens, token_pair = lax.optimization_barrier((spread, tokens, token_pair))
    light_sum = light_call(
        (0, 1),
        False,
        [((3, tok_rows, light_cols), F32)],
        (tokens, token_pair),
        light_input,
    )
    spread = swap(spread)
    spread, token_far, light_sum = lax.optimization_barrier((spread, token_far, light_sum))
    token_last = lax.ppermute(token_far, "head", pair)
    mine = on_chip(compact_kernel, [((routed, part_width), BF)], spread, mine_map, moved=20 << 20)
    half = seq_count * 2 // head_count
    holds = [
        (s * head_count + h, s * head_count + (h ^ 2))
        for s in range(seq_count)
        for h in range(head_count)
        if s // half == h // 2
    ]
    crossed = lax.ppermute(mine, ("seq", "head"), holds)
    mine = on_chip(choose_kernel, [((routed, part_width), BF)], mine, crossed)
    other = lax.ppermute(mine, "head", pair)
    parts = on_chip(
        project_kernel, [((seq_count, 3, routed, HD), BF)], mine, other, heavy_input
    )

    parts, light_sum, token_far, token_last = lax.optimization_barrier(
        (parts, light_sum, token_far, token_last)
    )
    light_heads, light_give = light_call(
        (2, 3),
        True,
        [((tok_rows, light_cols), BF), ((2, tok_rows, own_width), BF)],
        (token_far, token_last),
        light_input,
        light_sum,
        light_output,
        scratch=[
            pltpu.VMEM((3, tok_rows, light_cols), F32),
            pltpu.VMEM((2, light_cols, own_width), BF),
        ],
    )
    parts = swap(parts)
    parts, light_heads, light_give = lax.optimization_barrier((parts, light_heads, light_give))
    light_got = lax.ppermute(light_give, "head", pair)
    heads = on_chip(heavy_attend_kernel, [((seq_count, routed, HD), BF)], parts)
    light_own, light_far = on_chip(
        light_own_kernel,
        [((tok_rows, own_width), F32), ((tok_rows, own_width), BF)],
        light_got,
        light_heads,
        hbm=(light_output,),
        scratch=[pltpu.VMEM((2, light_cols, own_width), BF), pltpu.SemaphoreType.DMA((2,))],
        flops=4 * tok_rows * light_cols * own_width,
        off=True,
    )
    heads = swap(heads)
    heads, light_own, light_far = lax.optimization_barrier((heads, light_own, light_far))
    light_far = lax.ppermute(light_far, "head", across)

    back = on_chip(
        heavy_output_kernel,
        [((seq_count, slots, out_cols), BF)],
        heads,
        heavy_output,
        query_map,
    )
    back = swap(back)
    back, light_far = lax.optimization_barrier((back, light_far))
    give = on_chip(give_kernel, [((2, per, slots, out_cols), BF)], back)
    got = lax.ppermute(give, "head", pair)
    far = on_chip(far_kernel, [((per, slots, out_cols), BF)], back, got)
    last = lax.ppermute(far, "head", across)
    return on_chip(
        finish_kernel,
        [((tok_rows, own_width), BF)],
        light_own,
        light_far,
        back,
        got,
        last,
        own_map,
        gate_map,
        off=True,
    )


def solution(mesh):
    placed = (
        P("seq", "head"),
        P(None, None, "head"),
        P("head", None),
        P(None, "seq", "head"),
        P("head", "seq"),
        P(),
        P(),
        P("seq", None),
    )

    def per_device(*args):
        seq_count, head_count = mesh.shape["seq"], mesh.shape["head"]
        local_heads = args[3].shape[2] // HD
        fits = head_count // 2 == 2 and seq_count % head_count == 0 and local_heads == seq_count
        return (one_head_a_device if fits else general)(*args)

    return jax.shard_map(
        per_device, mesh=mesh, in_specs=placed, out_specs=P("seq", "head"), check_vma=False
    )
```

```python
import functools
import math

import jax
import jax.numpy as jnp
from jax import lax
from jax.experimental import pallas as pl
from jax.experimental.pallas import tpu as pltpu
from jax.sharding import PartitionSpec as P

HD = 128
LB = 128
ROUTE = 32
BF = jnp.bfloat16
F32 = jnp.float32
VMEM = pl.BlockSpec(memory_space=pltpu.VMEM)
FIRST = (((0,), (0,)), ((), ()))
LAST = (((1,), (1,)), ((), ()))


def attend(queries, key_rows, value_rows):
    scores = jnp.einsum(
        "bqhe,bkhe->bhqk", queries, key_rows, preferred_element_type=jnp.float32
    ) / math.sqrt(queries.shape[-1])
    highest = jnp.max(scores, axis=-1, keepdims=True)
    expanded = jnp.exp(scores - highest)
    totals = jnp.sum(expanded, axis=-1)
    weighted = jnp.einsum(
        "bhqk,bkhe->bqhe",
        expanded.astype(jnp.bfloat16),
        value_rows,
        preferred_element_type=jnp.float32,
    )
    return (weighted / jnp.transpose(totals, (0, 2, 1))[..., None]).astype(jnp.bfloat16)


def routed_map(table, routed):
    counts = jnp.sum((table >= 0).astype(jnp.int32), axis=1)
    shard = jnp.arange(table.shape[0], dtype=jnp.int32)
    upper_end = jnp.sum(jnp.where(shard[None, :] <= shard[:, None], counts[None, :], 0), axis=1)
    lower_end = upper_end - counts
    compact_rows = jnp.arange(routed, dtype=jnp.int32)
    source_shard = jnp.sum((upper_end[None, :] <= compact_rows[:, None]).astype(jnp.int32), axis=1)
    onehot_shard = (
        source_shard[:, None] == jnp.arange(table.shape[0], dtype=jnp.int32)[None, :]
    ).astype(jnp.int32)
    within = compact_rows - jnp.sum(onehot_shard * lower_end[None, :], axis=1)
    return (source_shard * table.shape[1] + within, lower_end)


def project(query_part, source_part, weights):
    stacked = jnp.stack((query_part, source_part, source_part))
    return jnp.einsum("cmd,cdw->mcw", stacked, weights, preferred_element_type=jnp.float32)


def pick_rows(gathered, own_list):
    chosen = jnp.take(gathered, jnp.maximum(own_list, 0), axis=0)
    return jnp.where((own_list >= 0)[:, None], chosen, jnp.zeros_like(chosen))


def general(
    tokens,
    light_input,
    light_output,
    heavy_input,
    heavy_output,
    query_tokens,
    context_tokens,
    query_gate,
):
    gathered = lax.all_gather(tokens, "head", axis=1, tiled=True)
    tok_rows = gathered.shape[0]
    light_mapped = jnp.einsum(
        "td,cdw->ctw", gathered, light_input, preferred_element_type=jnp.float32
    ).astype(jnp.bfloat16)
    light_blocks = light_mapped.reshape(3, tok_rows // LB, LB, -1, HD)
    light_heads = attend(light_blocks[0], light_blocks[1], light_blocks[2]).reshape(tok_rows, -1)
    light_part = jnp.dot(light_heads, light_output, preferred_element_type=jnp.float32)
    seq_count = lax.axis_size("seq")
    routed = seq_count * tok_rows // ROUTE
    slot_count = query_tokens.shape[1]
    seq_index = lax.axis_index("seq")
    own_queries = lax.dynamic_index_in_dim(query_tokens, seq_index, 0, keepdims=False)
    own_sources = lax.dynamic_index_in_dim(context_tokens, seq_index, 0, keepdims=False)
    query_cols, source_cols = (
        lax.all_to_all(
            pick_rows(gathered, own_queries), "seq", split_axis=1, concat_axis=0, tiled=True
        ),
        lax.all_to_all(
            pick_rows(gathered, own_sources), "seq", split_axis=1, concat_axis=0, tiled=True
        ),
    )
    query_index, query_lower = routed_map(query_tokens, routed)
    source_index = routed_map(context_tokens, routed)[0]
    query_rows = jnp.take(query_cols, query_index, axis=0)
    source_rows = jnp.take(source_cols, source_index, axis=0)
    summed = lax.psum(project(query_rows, source_rows, heavy_input), "seq").astype(jnp.bfloat16)
    heavy_heads = attend(
        summed[:, 0].reshape(1, routed, -1, HD),
        summed[:, 1].reshape(1, routed, -1, HD),
        summed[:, 2].reshape(1, routed, -1, HD),
    ).reshape(routed, -1)
    heavy_part = jnp.dot(heavy_heads, heavy_output, preferred_element_type=jnp.float32)
    slot_live = query_tokens >= 0
    compact = query_lower[:, None] + jnp.arange(slot_count, dtype=jnp.int32)[None, :]
    outgoing = jnp.take(heavy_part, jnp.where(slot_live, compact, 0).reshape(-1), axis=0)
    outgoing = jnp.where(slot_live.reshape(-1)[:, None], outgoing, jnp.zeros_like(outgoing))
    returned = lax.all_to_all(
        outgoing.astype(jnp.bfloat16), "seq", split_axis=0, concat_axis=1, tiled=True
    ).astype(outgoing.dtype)
    scaled = returned * query_gate[0][:, None]
    targets = jnp.where(own_queries >= 0, own_queries, tok_rows)
    combined = light_part.at[targets].add(scaled, mode="drop")
    return lax.psum_scatter(combined.astype(jnp.bfloat16), "head", scatter_dimension=1, tiled=True)


def in_vmem(*arrays):
    return tuple(pltpu.with_memory_space_constraint(a, pltpu.VMEM) for a in arrays)


def on_chip(kernel, outs, *arrays, hbm=(), scratch=(), flops=0, moved=0, off=False):
    made = [(jax.ShapeDtypeStruct if off else pltpu.VMEM)(*o) for o in outs]
    result = pl.pallas_call(
        kernel,
        in_specs=[pl.BlockSpec(memory_space=pl.ANY)] * len(hbm) + [VMEM] * len(arrays),
        scratch_shapes=list(scratch),
        out_specs=[VMEM] * len(made),
        out_shape=made,
        compiler_params=pltpu.CompilerParams(vmem_limit_bytes=(60 if hbm else 8) << 20),
        cost_estimate=pl.CostEstimate(
            flops=int(flops), bytes_accessed=int(moved), transcendentals=0
        ),
    )(*hbm, *in_vmem(*arrays))
    return result if len(outs) > 1 else result[0]


def listed(count):
    inner = sorted(range(count), key=lambda i: 2 * abs(2 * i + 1 - count) // count)
    return [i ^ 1 for i in inner]


def spots(count):
    order = listed(count)
    return [order.index(i) for i in range(count)]


def look_up(values, index):
    found = jnp.int32(values[0])
    for i, value in enumerate(values[1:], 1):
        found = jnp.where(index == i, value, found)
    return found


def own_row(table, index):
    rows = lax.broadcasted_iota(jnp.int32, table.shape, 0)
    return jnp.sum(jnp.where(rows == index, table, 0), axis=0, keepdims=True)


def onehot(flags):
    return flags.astype(F32).astype(BF)


def compact_onehot(table, out_ref):
    shards, slots = table.shape
    spot = spots(shards)
    live = (table >= 0).astype(jnp.int32)
    counts = jnp.sum(live, axis=1, keepdims=True)
    row = lax.broadcasted_iota(jnp.int32, (out_ref.shape[0], slots), 0)
    place = lax.broadcasted_iota(jnp.int32, (1, slots), 1)
    for s in range(shards):
        here = (row == place) & (table[s : s + 1] >= 0)
        out_ref[:, spot[s] * slots : (spot[s] + 1) * slots] = onehot(here)
        place = place + counts[s : s + 1]


def pick_kernel(
    tok_hbm,
    query_hbm,
    source_hbm,
    gate_hbm,
    keep_ref,
    send_ref,
    mine_ref,
    query_map_ref,
    own_map_ref,
    gate_map_ref,
    tok_ref,
    query_ref,
    source_ref,
    gate_ref,
    sems,
):
    ends = (
        (query_hbm, query_ref),
        (source_hbm, source_ref),
        (gate_hbm, gate_ref),
        (tok_hbm, tok_ref),
    )
    copies = [pltpu.make_async_copy(*e, sems.at[i]) for i, e in enumerate(ends)]
    for copy in copies:
        copy.start()
    odd = lax.axis_index("head") % 2
    for copy in copies[:3]:
        copy.wait()
    query, source = query_ref[...], source_ref[...]
    own_q = own_row(query, lax.axis_index("seq"))
    own_s = own_row(source, lax.axis_index("seq"))
    spot = lax.broadcasted_iota(jnp.int32, own_map_ref.shape, 0)
    chosen = [onehot(spot == jnp.where(odd == k, own_q, own_s)) for k in range(2)]
    own_map_ref[...] = onehot(spot == own_q)
    compact_onehot(query, query_map_ref)
    compact_onehot(jnp.where(odd == 0, query, source), mine_ref)
    slots = own_q.shape[1]
    diagonal = lax.broadcasted_iota(jnp.int32, (slots, slots), 0) == lax.broadcasted_iota(
        jnp.int32, (slots, slots), 1
    )
    gate = jnp.sum(jnp.where(diagonal, gate_ref[...], 0.0), axis=1, keepdims=True)
    gate_map_ref[...] = jnp.broadcast_to(gate, gate_map_ref.shape)
    copies[3].wait()
    for ref, rows in zip((keep_ref, send_ref), chosen):
        ref[...] = lax.dot_general(rows, tok_ref[...], FIRST, preferred_element_type=F32).astype(
            BF
        )


def spread_kernel(keep_ref, got_ref, out_ref):
    odd = lax.axis_index("head") % 2
    keep, got = keep_ref[...], got_ref[...]
    width = out_ref.shape[2]
    per = keep.shape[1] // width
    spot = spots(out_ref.shape[0])
    for part, block in enumerate((jnp.where(odd == 0, keep, got), jnp.where(odd == 0, got, keep))):
        for i in range(per):
            for at in range(part * per + i, out_ref.shape[0], 2 * per):
                out_ref[spot[at]] = block[:, i * width : (i + 1) * width]


def compact_kernel(slots_ref, chosen_ref, out_ref):
    rows = slots_ref[...].reshape(-1, slots_ref.shape[2])
    out_ref[...] = jnp.dot(chosen_ref[...], rows, preferred_element_type=F32).astype(BF)


def choose_kernel(mine_ref, crossed_ref, out_ref):
    pairs = lax.axis_size("head") // 2
    holder = lax.axis_index("seq") * pairs // lax.axis_size("seq")
    out_ref[...] = jnp.where(holder == lax.axis_index("head") // 2, mine_ref[...], crossed_ref[...])


def project_kernel(mine_ref, other_ref, weight_ref, out_ref):
    odd = lax.axis_index("head") % 2
    mine, other = mine_ref[...], other_ref[...]
    query = jnp.where(odd == 0, mine, other)
    source = jnp.where(odd == 0, other, mine)
    spot = spots(out_ref.shape[0])
    for c, rows in enumerate((query, source, source)):
        part = jnp.dot(rows, weight_ref[c], preferred_element_type=F32).astype(BF)
        for g in range(out_ref.shape[0]):
            out_ref[spot[g], c] = part[:, g * HD : (g + 1) * HD]


def one_head(query, key, value):
    scores = lax.dot_general(query, key, LAST, preferred_element_type=F32) / math.sqrt(HD)
    expanded = jnp.exp(scores - jnp.max(scores, axis=-1, keepdims=True))
    totals = jnp.sum(expanded, axis=-1, keepdims=True)
    weighted = jnp.dot(expanded.astype(BF), value, preferred_element_type=F32)
    return (weighted / totals).astype(BF)


def heavy_attend_kernel(parts_ref, out_ref):
    total = parts_ref[0].astype(F32)
    for s in range(1, parts_ref.shape[0]):
        total = total + parts_ref[s].astype(F32)
    total = total.astype(BF)
    result = one_head(total[0], total[1], total[2])
    for s in range(out_ref.shape[0]):
        out_ref[s] = result


def heavy_output_kernel(heads_ref, weight_ref, keep_ref, give_ref):
    odd = lax.axis_index("head") % 2
    rows = jnp.concatenate([heads_ref[i] for i in spots(heads_ref.shape[0])], axis=1)
    part = jnp.dot(rows, weight_ref[...], preferred_element_type=F32)
    width = keep_ref.shape[1]
    low, high = part[:, :width], part[:, width:]
    keep_ref[...] = jnp.where(odd == 0, low, high)
    give_ref[...] = jnp.where(odd == 0, high, low).astype(BF)


def return_kernel(keep_ref, got_ref, chosen_ref, out_ref):
    rows = (keep_ref[...] + got_ref[...].astype(F32)).astype(BF)
    spread = lax.dot_general(chosen_ref[...], rows, FIRST, preferred_element_type=F32).astype(BF)
    shards, pairs, slots = out_ref.shape[:3]
    for s in range(shards):
        for k in range(pairs):
            out_ref[s, k] = spread[s * slots : (s + 1) * slots]


def block_of(back_ref, head, per, i):
    at = look_up(spots(back_ref.shape[0])[i::per], head)
    total = back_ref[at, 0].astype(F32)
    for k in range(1, back_ref.shape[1]):
        total = total + back_ref[at, k].astype(F32)
    return total


def give_kernel(back_ref, out_ref):
    head = lax.axis_index("head")
    per = out_ref.shape[0]
    for i in range(per):
        out_ref[i] = block_of(back_ref, head ^ 1, per, i).astype(BF)


def merge_kernel(own, far, out_ref, far_ref, sems):
    copies = [
        pltpu.make_async_copy(own, out_ref, sems.at[0]),
        pltpu.make_async_copy(far, far_ref, sems.at[1]),
    ]
    for copy in copies:
        copy.start()
    for copy in copies:
        copy.wait()
    out_ref[...] = out_ref[...] + far_ref[...].astype(F32)


def finish_kernel(light_ref, back_ref, got_ref, own_map_ref, gate_ref, out_ref):
    head = lax.axis_index("head")
    per, _, width = got_ref.shape
    chosen, gate = own_map_ref[...], gate_ref[:, :1]
    for i in range(per):
        for half, heavy in (
            (head % 2, block_of(back_ref, head, per, i)),
            (1 - head % 2, got_ref[i].astype(F32)),
        ):
            scaled = heavy * gate
            coarse = scaled.astype(BF)
            fine = (scaled - coarse.astype(F32)).astype(BF)
            added = jnp.dot(chosen, coarse, preferred_element_type=F32) + jnp.dot(
                chosen, fine, preferred_element_type=F32
            )
            cols = pl.ds(pl.multiple_of((2 * i + half) * width, width), width)
            out_ref[:, cols] = (light_ref[:, cols] + added).astype(BF)


def light_kernel(flips, last, *refs):
    count = len(flips)
    pieces, (w_in, *refs) = refs[:count], refs[count:]
    if last:
        before, w_out, heads_ref, give_ref, before_ref, out_ref, *refs = refs
    else:
        sum_ref, *refs = refs
    tok_ref, in_ref, sems = refs[:3]
    head = lax.axis_index("head")
    depth = pieces[0].shape[1]
    copies = []
    for i, (j, piece) in enumerate(zip(flips, pieces)):
        rows = pl.ds(pl.multiple_of((head ^ j) * depth, depth), depth)
        copies.append(pltpu.make_async_copy(piece, tok_ref.at[i], sems.at[0, i]))
        for c in range(3):
            copies.append(
                pltpu.make_async_copy(w_in.at[c, rows, :], in_ref.at[c, i], sems.at[1 + c, i])
            )
    late = []
    if last:
        late_sems = refs[3]
        width = give_ref.shape[2]
        late.append(pltpu.make_async_copy(before, before_ref, late_sems.at[2]))
        for i, j in enumerate((1, 3)):
            cols = pl.ds(pl.multiple_of((head ^ j) * width, width), width)
            late.append(pltpu.make_async_copy(w_out.at[:, cols], out_ref.at[i], late_sems.at[i]))
    for copy in copies + late:
        copy.start()
    total = [None] * 3
    for i in range(count):
        copies[4 * i].wait()
        for c in range(3):
            copies[4 * i + 1 + c].wait()
            part = jnp.dot(tok_ref[i], in_ref[c, i], preferred_element_type=F32)
            total[c] = part if i == 0 else total[c] + part
    if not last:
        for c in range(3):
            sum_ref[c] = total[c]
        return
    late[0].wait()
    mapped = [(before_ref[c] + total[c]).astype(BF) for c in range(3)]
    for b in range(heads_ref.shape[0] // LB):
        for g in range(heads_ref.shape[1] // HD):
            at = (slice(b * LB, (b + 1) * LB), slice(g * HD, (g + 1) * HD))
            heads_ref[at] = one_head(*(m[at] for m in mapped))
    for i in range(2):
        late[1 + i].wait()
        give_ref[i] = jnp.dot(heads_ref[...], out_ref[i], preferred_element_type=F32).astype(BF)


def light_own_kernel(w_out, got_ref, heads_ref, own_ref, far_ref, out_ref, sems):
    head = lax.axis_index("head")
    width = own_ref.shape[1]
    copies = []
    for i, j in enumerate((0, 2)):
        cols = pl.ds(pl.multiple_of((head ^ j) * width, width), width)
        copies.append(pltpu.make_async_copy(w_out.at[:, cols], out_ref.at[i], sems.at[i]))
    for copy in copies:
        copy.start()
    for i, ref in enumerate((own_ref, far_ref)):
        copies[i].wait()
        block = jnp.dot(heads_ref[...], out_ref[i], preferred_element_type=F32)
        ref[...] = (block + got_ref[i].astype(F32)).astype(ref.dtype)


def light_call(flips, last, outs, pieces, *arrays, scratch=()):
    count = len(flips)
    rows, width = pieces[0].shape
    return on_chip(
        functools.partial(light_kernel, flips, last),
        outs,
        hbm=(*pieces, *arrays),
        scratch=[
            *scratch,
            pltpu.VMEM((count, rows, width), BF),
            pltpu.VMEM((3, count, width, arrays[0].shape[2]), BF),
            pltpu.SemaphoreType.DMA((4, count)),
            pltpu.SemaphoreType.DMA((3,)),
        ],
        flops=6 * count * rows * width * arrays[0].shape[2],
        off=True,
    )


def one_head_a_device(
    tokens,
    light_input,
    light_output,
    heavy_input,
    heavy_output,
    query_tokens,
    context_tokens,
    query_gate,
):
    seq_count, head_count = lax.axis_size("seq"), lax.axis_size("head")
    tok_rows, own_width = tokens.shape
    slots = query_tokens.shape[1]
    routed = seq_count * tok_rows // ROUTE
    part_width, head_cols = heavy_input.shape[1:]
    out_cols = heavy_output.shape[1]
    light_cols = light_input.shape[2]
    per = seq_count // head_count
    pair, across = ([(i, i ^ j) for i in range(head_count)] for j in (1, 2))

    def swap(x):
        return lax.all_to_all(
            x,
            "seq",
            split_axis=0,
            concat_axis=0,
            tiled=True,
            axis_index_groups=[listed(seq_count)],
        )

    routes = (routed, seq_count * slots)
    keep, send, mine_map, query_map, own_map, gate_map = on_chip(
        pick_kernel,
        [((slots, own_width), BF)] * 2
        + [(routes, BF)] * 2
        + [((tok_rows, slots), BF), ((slots, HD), F32)],
        hbm=(tokens, query_tokens, context_tokens, query_gate),
        scratch=[
            pltpu.VMEM(tokens.shape, BF),
            pltpu.VMEM(query_tokens.shape, jnp.int32),
            pltpu.VMEM(context_tokens.shape, jnp.int32),
            pltpu.VMEM(query_gate.shape, F32),
            pltpu.SemaphoreType.DMA((4,)),
        ],
    )
    got = lax.ppermute(send, "head", pair)
    spread = on_chip(spread_kernel, [((seq_count, slots, part_width), BF)], keep, got)
    token_far = lax.ppermute(tokens, "head", across)
    token_pair = lax.ppermute(tokens, "head", pair)
    spread, tokens, token_pair = lax.optimization_barrier((spread, tokens, token_pair))
    light_sum = light_call(
        (0, 1),
        False,
        [((3, tok_rows, light_cols), F32)],
        (tokens, token_pair),
        light_input,
    )
    spread = swap(spread)
    spread, token_far, light_sum = lax.optimization_barrier((spread, token_far, light_sum))
    token_last = lax.ppermute(token_far, "head", pair)
    mine = on_chip(compact_kernel, [((routed, part_width), BF)], spread, mine_map, moved=20 << 20)
    half = seq_count * 2 // head_count
    holds = [
        (s * head_count + h, s * head_count + (h ^ 2))
        for s in range(seq_count)
        for h in range(head_count)
        if s // half == h // 2
    ]
    crossed = lax.ppermute(mine, ("seq", "head"), holds)
    mine = on_chip(choose_kernel, [((routed, part_width), BF)], mine, crossed)
    other = lax.ppermute(mine, "head", pair)
    parts = on_chip(
        project_kernel, [((seq_count, 3, routed, HD), BF)], mine, other, heavy_input
    )

    parts, light_sum, token_far, token_last = lax.optimization_barrier(
        (parts, light_sum, token_far, token_last)
    )
    light_heads, light_give = light_call(
        (2, 3),
        True,
        [((tok_rows, light_cols), BF), ((2, tok_rows, own_width), BF)],
        (token_far, token_last),
        light_input,
        light_sum,
        light_output,
        scratch=[
            pltpu.VMEM((3, tok_rows, light_cols), F32),
            pltpu.VMEM((2, light_cols, own_width), BF),
        ],
    )
    parts = swap(parts)
    parts, light_heads, light_give = lax.optimization_barrier((parts, light_heads, light_give))
    light_got = lax.ppermute(light_give, "head", pair)
    heads = on_chip(heavy_attend_kernel, [((seq_count, routed, HD), BF)], parts)
    light_own, light_far = on_chip(
        light_own_kernel,
        [((tok_rows, own_width), F32), ((tok_rows, own_width), BF)],
        light_got,
        light_heads,
        hbm=(light_output,),
        scratch=[pltpu.VMEM((2, light_cols, own_width), BF), pltpu.SemaphoreType.DMA((2,))],
        flops=4 * tok_rows * light_cols * own_width,
        off=True,
    )
    heads = swap(heads)
    heads, light_own, light_far = lax.optimization_barrier((heads, light_own, light_far))
    light_far = lax.ppermute(light_far, "head", across)

    half_cols = out_cols // 2
    keep, give = on_chip(
        heavy_output_kernel,
        [((routed, half_cols), F32), ((routed, half_cols), BF)],
        heads,
        heavy_output,
    )
    got = lax.ppermute(give, "head", pair)
    pairs = head_count // 2
    back = on_chip(
        return_kernel, [((seq_count, pairs, slots, half_cols), BF)], keep, got, query_map
    )
    groups = [
        [s * head_count + 2 * k + c for s in listed(seq_count) for k in range(pairs)]
        for c in range(2)
    ]
    back = lax.all_to_all(
        back.reshape(-1, slots, half_cols),
        ("seq", "head"),
        split_axis=0,
        concat_axis=0,
        tiled=True,
        axis_index_groups=groups,
    ).reshape(back.shape)
    back, light_far = lax.optimization_barrier((back, light_far))
    give = on_chip(give_kernel, [((per, slots, half_cols), BF)], back)
    give, light_own, light_far = lax.optimization_barrier((give, light_own, light_far))
    got = lax.ppermute(give, "head", pair)
    light = on_chip(
        merge_kernel,
        [((tok_rows, own_width), F32)],
        hbm=(light_own, light_far),
        scratch=[pltpu.VMEM((tok_rows, own_width), BF), pltpu.SemaphoreType.DMA((2,))],
    )
    return on_chip(
        finish_kernel,
        [((tok_rows, own_width), BF)],
        light,
        back,
        got,
        own_map,
        gate_map,
        off=True,
    )


def solution(mesh):
    placed = (
        P("seq", "head"),
        P(None, None, "head"),
        P("head", None),
        P(None, "seq", "head"),
        P("head", "seq"),
        P(),
        P(),
        P("seq", None),
    )

    def per_device(*args):
        seq_count, head_count = mesh.shape["seq"], mesh.shape["head"]
        local_heads = args[3].shape[2] // HD
        fits = head_count // 2 == 2 and seq_count % head_count == 0 and local_heads == seq_count
        return (one_head_a_device if fits else general)(*args)

    return jax.shard_map(
        per_device, mesh=mesh, in_specs=placed, out_specs=P("seq", "head"), check_vma=False
    )
```

```python
import functools
import math

import jax
import jax.numpy as jnp
from jax import lax
from jax.experimental import pallas as pl
from jax.experimental.pallas import tpu as pltpu
from jax.sharding import PartitionSpec as P

HD = 128
LB = 128
ROUTE = 32
BF = jnp.bfloat16
F32 = jnp.float32
VMEM = pl.BlockSpec(memory_space=pltpu.VMEM)
FIRST = (((0,), (0,)), ((), ()))
LAST = (((1,), (1,)), ((), ()))


def attend(queries, key_rows, value_rows):
    scores = jnp.einsum(
        "bqhe,bkhe->bhqk", queries, key_rows, preferred_element_type=jnp.float32
    ) / math.sqrt(queries.shape[-1])
    highest = jnp.max(scores, axis=-1, keepdims=True)
    expanded = jnp.exp(scores - highest)
    totals = jnp.sum(expanded, axis=-1)
    weighted = jnp.einsum(
        "bhqk,bkhe->bqhe",
        expanded.astype(jnp.bfloat16),
        value_rows,
        preferred_element_type=jnp.float32,
    )
    return (weighted / jnp.transpose(totals, (0, 2, 1))[..., None]).astype(jnp.bfloat16)


def routed_map(table, routed):
    counts = jnp.sum((table >= 0).astype(jnp.int32), axis=1)
    shard = jnp.arange(table.shape[0], dtype=jnp.int32)
    upper_end = jnp.sum(jnp.where(shard[None, :] <= shard[:, None], counts[None, :], 0), axis=1)
    lower_end = upper_end - counts
    compact_rows = jnp.arange(routed, dtype=jnp.int32)
    source_shard = jnp.sum((upper_end[None, :] <= compact_rows[:, None]).astype(jnp.int32), axis=1)
    onehot_shard = (
        source_shard[:, None] == jnp.arange(table.shape[0], dtype=jnp.int32)[None, :]
    ).astype(jnp.int32)
    within = compact_rows - jnp.sum(onehot_shard * lower_end[None, :], axis=1)
    return (source_shard * table.shape[1] + within, lower_end)


def project(query_part, source_part, weights):
    stacked = jnp.stack((query_part, source_part, source_part))
    return jnp.einsum("cmd,cdw->mcw", stacked, weights, preferred_element_type=jnp.float32)


def pick_rows(gathered, own_list):
    chosen = jnp.take(gathered, jnp.maximum(own_list, 0), axis=0)
    return jnp.where((own_list >= 0)[:, None], chosen, jnp.zeros_like(chosen))


def general(
    tokens,
    light_input,
    light_output,
    heavy_input,
    heavy_output,
    query_tokens,
    context_tokens,
    query_gate,
):
    gathered = lax.all_gather(tokens, "head", axis=1, tiled=True)
    tok_rows = gathered.shape[0]
    light_mapped = jnp.einsum(
        "td,cdw->ctw", gathered, light_input, preferred_element_type=jnp.float32
    ).astype(jnp.bfloat16)
    light_blocks = light_mapped.reshape(3, tok_rows // LB, LB, -1, HD)
    light_heads = attend(light_blocks[0], light_blocks[1], light_blocks[2]).reshape(tok_rows, -1)
    light_part = jnp.dot(light_heads, light_output, preferred_element_type=jnp.float32)
    seq_count = lax.axis_size("seq")
    routed = seq_count * tok_rows // ROUTE
    slot_count = query_tokens.shape[1]
    seq_index = lax.axis_index("seq")
    own_queries = lax.dynamic_index_in_dim(query_tokens, seq_index, 0, keepdims=False)
    own_sources = lax.dynamic_index_in_dim(context_tokens, seq_index, 0, keepdims=False)
    query_cols, source_cols = (
        lax.all_to_all(
            pick_rows(gathered, own_queries), "seq", split_axis=1, concat_axis=0, tiled=True
        ),
        lax.all_to_all(
            pick_rows(gathered, own_sources), "seq", split_axis=1, concat_axis=0, tiled=True
        ),
    )
    query_index, query_lower = routed_map(query_tokens, routed)
    source_index = routed_map(context_tokens, routed)[0]
    query_rows = jnp.take(query_cols, query_index, axis=0)
    source_rows = jnp.take(source_cols, source_index, axis=0)
    summed = lax.psum(project(query_rows, source_rows, heavy_input), "seq").astype(jnp.bfloat16)
    heavy_heads = attend(
        summed[:, 0].reshape(1, routed, -1, HD),
        summed[:, 1].reshape(1, routed, -1, HD),
        summed[:, 2].reshape(1, routed, -1, HD),
    ).reshape(routed, -1)
    heavy_part = jnp.dot(heavy_heads, heavy_output, preferred_element_type=jnp.float32)
    slot_live = query_tokens >= 0
    compact = query_lower[:, None] + jnp.arange(slot_count, dtype=jnp.int32)[None, :]
    outgoing = jnp.take(heavy_part, jnp.where(slot_live, compact, 0).reshape(-1), axis=0)
    outgoing = jnp.where(slot_live.reshape(-1)[:, None], outgoing, jnp.zeros_like(outgoing))
    returned = lax.all_to_all(
        outgoing.astype(jnp.bfloat16), "seq", split_axis=0, concat_axis=1, tiled=True
    ).astype(outgoing.dtype)
    scaled = returned * query_gate[0][:, None]
    targets = jnp.where(own_queries >= 0, own_queries, tok_rows)
    combined = light_part.at[targets].add(scaled, mode="drop")
    return lax.psum_scatter(combined.astype(jnp.bfloat16), "head", scatter_dimension=1, tiled=True)


def in_vmem(*arrays):
    return tuple(pltpu.with_memory_space_constraint(a, pltpu.VMEM) for a in arrays)


def on_chip(kernel, outs, *arrays, hbm=(), scratch=(), flops=0, moved=0, off=False, kept=()):
    made = [
        (jax.ShapeDtypeStruct if off and i not in kept else pltpu.VMEM)(*o)
        for i, o in enumerate(outs)
    ]
    result = pl.pallas_call(
        kernel,
        in_specs=[pl.BlockSpec(memory_space=pl.ANY)] * len(hbm) + [VMEM] * len(arrays),
        scratch_shapes=list(scratch),
        out_specs=[VMEM] * len(made),
        out_shape=made,
        compiler_params=pltpu.CompilerParams(vmem_limit_bytes=(60 if hbm else 8) << 20),
        cost_estimate=pl.CostEstimate(
            flops=int(flops), bytes_accessed=int(moved), transcendentals=0
        ),
    )(*hbm, *in_vmem(*arrays))
    return result if len(outs) > 1 else result[0]


def listed(count):
    inner = sorted(range(count), key=lambda i: 2 * abs(2 * i + 1 - count) // count)
    return [i ^ 1 for i in inner]


def spots(count):
    order = listed(count)
    return [order.index(i) for i in range(count)]


def look_up(values, index):
    found = jnp.int32(values[0])
    for i, value in enumerate(values[1:], 1):
        found = jnp.where(index == i, value, found)
    return found


def own_row(table, index):
    rows = lax.broadcasted_iota(jnp.int32, table.shape, 0)
    return jnp.sum(jnp.where(rows == index, table, 0), axis=0, keepdims=True)


def onehot(flags):
    return flags.astype(F32).astype(BF)


def compact_onehot(table, out_ref):
    shards, slots = table.shape
    spot = spots(shards)
    live = (table >= 0).astype(jnp.int32)
    counts = jnp.sum(live, axis=1, keepdims=True)
    row = lax.broadcasted_iota(jnp.int32, (out_ref.shape[0], slots), 0)
    place = lax.broadcasted_iota(jnp.int32, (1, slots), 1)
    for s in range(shards):
        here = (row == place) & (table[s : s + 1] >= 0)
        out_ref[:, spot[s] * slots : (spot[s] + 1) * slots] = onehot(here)
        place = place + counts[s : s + 1]


def pick_kernel(
    tok_hbm,
    query_hbm,
    source_hbm,
    gate_hbm,
    keep_ref,
    send_ref,
    mine_ref,
    query_map_ref,
    own_map_ref,
    gate_map_ref,
    tok_ref,
    query_ref,
    source_ref,
    gate_ref,
    sems,
):
    ends = (
        (query_hbm, query_ref),
        (source_hbm, source_ref),
        (gate_hbm, gate_ref),
        (tok_hbm, tok_ref),
    )
    copies = [pltpu.make_async_copy(*e, sems.at[i]) for i, e in enumerate(ends)]
    for copy in copies:
        copy.start()
    odd = lax.axis_index("head") % 2
    for copy in copies[:3]:
        copy.wait()
    query, source = query_ref[...], source_ref[...]
    own_q = own_row(query, lax.axis_index("seq"))
    own_s = own_row(source, lax.axis_index("seq"))
    spot = lax.broadcasted_iota(jnp.int32, own_map_ref.shape, 0)
    chosen = [onehot(spot == jnp.where(odd == k, own_q, own_s)) for k in range(2)]
    own_map_ref[...] = onehot(spot == own_q)
    compact_onehot(query, query_map_ref)
    compact_onehot(jnp.where(odd == 0, query, source), mine_ref)
    slots = own_q.shape[1]
    diagonal = lax.broadcasted_iota(jnp.int32, (slots, slots), 0) == lax.broadcasted_iota(
        jnp.int32, (slots, slots), 1
    )
    gate = jnp.sum(jnp.where(diagonal, gate_ref[...], 0.0), axis=1, keepdims=True)
    gate_map_ref[...] = jnp.broadcast_to(gate, gate_map_ref.shape)
    copies[3].wait()
    for ref, rows in zip((keep_ref, send_ref), chosen):
        ref[...] = lax.dot_general(rows, tok_ref[...], FIRST, preferred_element_type=F32).astype(
            BF
        )


def spread_kernel(keep_ref, got_ref, out_ref):
    odd = lax.axis_index("head") % 2
    keep, got = keep_ref[...], got_ref[...]
    width = out_ref.shape[2]
    per = keep.shape[1] // width
    spot = spots(out_ref.shape[0])
    for part, block in enumerate((jnp.where(odd == 0, keep, got), jnp.where(odd == 0, got, keep))):
        for i in range(per):
            for at in range(part * per + i, out_ref.shape[0], 2 * per):
                out_ref[spot[at]] = block[:, i * width : (i + 1) * width]


def compact_kernel(slots_ref, chosen_ref, out_ref):
    rows = slots_ref[...].reshape(-1, slots_ref.shape[2])
    out_ref[...] = jnp.dot(chosen_ref[...], rows, preferred_element_type=F32).astype(BF)


def choose_kernel(mine_ref, crossed_ref, out_ref):
    pairs = lax.axis_size("head") // 2
    holder = lax.axis_index("seq") * pairs // lax.axis_size("seq")
    out_ref[...] = jnp.where(holder == lax.axis_index("head") // 2, mine_ref[...], crossed_ref[...])


def project_kernel(mine_ref, other_ref, weight_ref, out_ref):
    odd = lax.axis_index("head") % 2
    mine, other = mine_ref[...], other_ref[...]
    query = jnp.where(odd == 0, mine, other)
    source = jnp.where(odd == 0, other, mine)
    spot = spots(out_ref.shape[0])
    for c, rows in enumerate((query, source, source)):
        part = jnp.dot(rows, weight_ref[c], preferred_element_type=F32).astype(BF)
        for g in range(out_ref.shape[0]):
            out_ref[spot[g], c] = part[:, g * HD : (g + 1) * HD]


def one_head(query, key, value):
    scores = lax.dot_general(query, key, LAST, preferred_element_type=F32) / math.sqrt(HD)
    expanded = jnp.exp(scores - jnp.max(scores, axis=-1, keepdims=True))
    totals = jnp.sum(expanded, axis=-1, keepdims=True)
    weighted = jnp.dot(expanded.astype(BF), value, preferred_element_type=F32)
    return (weighted / totals).astype(BF)


def heavy_attend_kernel(parts_ref, out_ref):
    total = parts_ref[0].astype(F32)
    for s in range(1, parts_ref.shape[0]):
        total = total + parts_ref[s].astype(F32)
    total = total.astype(BF)
    result = one_head(total[0], total[1], total[2])
    for s in range(out_ref.shape[0]):
        out_ref[s] = result


def heavy_output_kernel(heads_ref, weight_ref, chosen_ref, out_ref):
    rows = jnp.concatenate([heads_ref[i] for i in spots(heads_ref.shape[0])], axis=1)
    part = jnp.dot(rows, weight_ref[...], preferred_element_type=F32).astype(BF)
    spread = lax.dot_general(chosen_ref[...], part, FIRST, preferred_element_type=F32).astype(BF)
    out_ref[...] = spread.reshape(out_ref.shape)


def block_of(back_ref, head, per, i):
    spot = spots(back_ref.shape[0])
    return back_ref[look_up(spot[i::per], head)]


def give_kernel(back_ref, out_ref):
    head = lax.axis_index("head")
    per = out_ref.shape[1]
    for k, j in enumerate((1, 3)):
        for i in range(per):
            out_ref[k, i] = block_of(back_ref, head ^ j, per, i)


def far_kernel(back_ref, got_ref, out_ref):
    per = out_ref.shape[0]
    head = lax.axis_index("head")
    for i in range(per):
        mine = block_of(back_ref, head ^ 2, per, i).astype(F32)
        out_ref[i] = (mine + got_ref[1, i].astype(F32)).astype(BF)


def finish_kernel(
    light_ref, light_far_ref, back_ref, got_ref, last_ref, own_map_ref, gate_ref, out_ref
):
    head = lax.axis_index("head")
    per = last_ref.shape[0]
    chosen, gate = own_map_ref[...], gate_ref[:, :1]
    width = last_ref.shape[2]
    for j in range(per):
        mine = block_of(back_ref, head, per, j).astype(F32)
        scaled = (mine + got_ref[0, j].astype(F32) + last_ref[j].astype(F32)) * gate
        coarse = scaled.astype(BF)
        fine = (scaled - coarse.astype(F32)).astype(BF)
        added = jnp.dot(chosen, coarse, preferred_element_type=F32) + jnp.dot(
            chosen, fine, preferred_element_type=F32
        )
        cols = slice(j * width, (j + 1) * width)
        light = light_ref[:, cols] + light_far_ref[:, cols].astype(F32)
        out_ref[:, cols] = (light + added).astype(BF)


def light_kernel(flips, last, *refs):
    count = len(flips)
    pieces, (w_in, *refs) = refs[:count], refs[count:]
    if last:
        before, w_out, heads_ref, give_ref, before_ref, out_ref, *refs = refs
    else:
        sum_ref, *refs = refs
    tok_ref, in_ref, sems = refs[:3]
    head = lax.axis_index("head")
    depth = pieces[0].shape[1]
    copies = []
    for i, (j, piece) in enumerate(zip(flips, pieces)):
        rows = pl.ds(pl.multiple_of((head ^ j) * depth, depth), depth)
        copies.append(pltpu.make_async_copy(piece, tok_ref.at[i], sems.at[0, i]))
        for c in range(3):
            copies.append(
                pltpu.make_async_copy(w_in.at[c, rows, :], in_ref.at[c, i], sems.at[1 + c, i])
            )
    late = []
    if last:
        late_sems = refs[3]
        width = give_ref.shape[2]
        late.append(pltpu.make_async_copy(before, before_ref, late_sems.at[2]))
        for i, j in enumerate((1, 3)):
            cols = pl.ds(pl.multiple_of((head ^ j) * width, width), width)
            late.append(pltpu.make_async_copy(w_out.at[:, cols], out_ref.at[i], late_sems.at[i]))
    for copy in copies + late:
        copy.start()
    total = [None] * 3
    for i in range(count):
        copies[4 * i].wait()
        for c in range(3):
            copies[4 * i + 1 + c].wait()
            part = jnp.dot(tok_ref[i], in_ref[c, i], preferred_element_type=F32)
            total[c] = part if i == 0 else total[c] + part
    if not last:
        for c in range(3):
            sum_ref[c] = total[c]
        return
    late[0].wait()
    mapped = [(before_ref[c] + total[c]).astype(BF) for c in range(3)]
    for b in range(heads_ref.shape[0] // LB):
        for g in range(heads_ref.shape[1] // HD):
            at = (slice(b * LB, (b + 1) * LB), slice(g * HD, (g + 1) * HD))
            heads_ref[at] = one_head(*(m[at] for m in mapped))
    for i in range(2):
        late[1 + i].wait()
        give_ref[i] = jnp.dot(heads_ref[...], out_ref[i], preferred_element_type=F32).astype(BF)


def light_own_kernel(w_out, got_ref, heads_ref, own_ref, far_ref, out_ref, sems):
    head = lax.axis_index("head")
    width = own_ref.shape[1]
    copies = []
    for i, j in enumerate((0, 2)):
        cols = pl.ds(pl.multiple_of((head ^ j) * width, width), width)
        copies.append(pltpu.make_async_copy(w_out.at[:, cols], out_ref.at[i], sems.at[i]))
    for copy in copies:
        copy.start()
    for i, ref in enumerate((own_ref, far_ref)):
        copies[i].wait()
        block = jnp.dot(heads_ref[...], out_ref[i], preferred_element_type=F32)
        ref[...] = (block + got_ref[i].astype(F32)).astype(ref.dtype)


def light_call(flips, last, outs, pieces, *arrays, scratch=()):
    count = len(flips)
    rows, width = pieces[0].shape
    return on_chip(
        functools.partial(light_kernel, flips, last),
        outs,
        hbm=(*pieces, *arrays),
        scratch=[
            *scratch,
            pltpu.VMEM((count, rows, width), BF),
            pltpu.VMEM((3, count, width, arrays[0].shape[2]), BF),
            pltpu.SemaphoreType.DMA((4, count)),
            pltpu.SemaphoreType.DMA((3,)),
        ],
        flops=6 * count * rows * width * arrays[0].shape[2],
        off=True,
        kept=(0,) if last else (),
    )


def one_head_a_device(
    tokens,
    light_input,
    light_output,
    heavy_input,
    heavy_output,
    query_tokens,
    context_tokens,
    query_gate,
):
    seq_count, head_count = lax.axis_size("seq"), lax.axis_size("head")
    tok_rows, own_width = tokens.shape
    slots = query_tokens.shape[1]
    routed = seq_count * tok_rows // ROUTE
    part_width, head_cols = heavy_input.shape[1:]
    out_cols = heavy_output.shape[1]
    light_cols = light_input.shape[2]
    per = seq_count // head_count
    pair, across = ([(i, i ^ j) for i in range(head_count)] for j in (1, 2))

    def swap(x):
        return lax.all_to_all(
            x,
            "seq",
            split_axis=0,
            concat_axis=0,
            tiled=True,
            axis_index_groups=[listed(seq_count)],
        )

    routes = (routed, seq_count * slots)
    keep, send, mine_map, query_map, own_map, gate_map = on_chip(
        pick_kernel,
        [((slots, own_width), BF)] * 2
        + [(routes, BF)] * 2
        + [((tok_rows, slots), BF), ((slots, HD), F32)],
        hbm=(tokens, query_tokens, context_tokens, query_gate),
        scratch=[
            pltpu.VMEM(tokens.shape, BF),
            pltpu.VMEM(query_tokens.shape, jnp.int32),
            pltpu.VMEM(context_tokens.shape, jnp.int32),
            pltpu.VMEM(query_gate.shape, F32),
            pltpu.SemaphoreType.DMA((4,)),
        ],
    )
    got = lax.ppermute(send, "head", pair)
    spread = on_chip(spread_kernel, [((seq_count, slots, part_width), BF)], keep, got)
    token_far = lax.ppermute(tokens, "head", across)
    token_pair = lax.ppermute(tokens, "head", pair)
    spread, tokens, token_pair = lax.optimization_barrier((spread, tokens, token_pair))
    light_sum = light_call(
        (0, 1),
        False,
        [((3, tok_rows, light_cols), F32)],
        (tokens, token_pair),
        light_input,
    )
    spread = swap(spread)
    spread, token_far, light_sum = lax.optimization_barrier((spread, token_far, light_sum))
    token_last = lax.ppermute(token_far, "head", pair)
    mine = on_chip(compact_kernel, [((routed, part_width), BF)], spread, mine_map, moved=20 << 20)
    half = seq_count * 2 // head_count
    holds = [
        (s * head_count + h, s * head_count + (h ^ 2))
        for s in range(seq_count)
        for h in range(head_count)
        if s // half == h // 2
    ]
    crossed = lax.ppermute(mine, ("seq", "head"), holds)
    mine = on_chip(choose_kernel, [((routed, part_width), BF)], mine, crossed)
    other = lax.ppermute(mine, "head", pair)
    parts = on_chip(
        project_kernel, [((seq_count, 3, routed, HD), BF)], mine, other, heavy_input
    )

    parts, light_sum, token_far, token_last = lax.optimization_barrier(
        (parts, light_sum, token_far, token_last)
    )
    light_heads, light_give = light_call(
        (2, 3),
        True,
        [((tok_rows, light_cols), BF), ((2, tok_rows, own_width), BF)],
        (token_far, token_last),
        light_input,
        light_sum,
        light_output,
        scratch=[
            pltpu.VMEM((3, tok_rows, light_cols), F32),
            pltpu.VMEM((2, light_cols, own_width), BF),
        ],
    )
    parts = swap(parts)
    parts, light_heads, light_give = lax.optimization_barrier((parts, light_heads, light_give))
    light_got = lax.ppermute(light_give, "head", pair)
    heads = on_chip(heavy_attend_kernel, [((seq_count, routed, HD), BF)], parts)
    light_own, light_far = on_chip(
        light_own_kernel,
        [((tok_rows, own_width), F32), ((tok_rows, own_width), BF)],
        light_got,
        light_heads,
        hbm=(light_output,),
        scratch=[pltpu.VMEM((2, light_cols, own_width), BF), pltpu.SemaphoreType.DMA((2,))],
        flops=4 * tok_rows * light_cols * own_width,
        off=True,
    )
    heads = swap(heads)
    far_sent = lax.ppermute(light_far, "head", across)
    heads, light_own, light_far = lax.optimization_barrier((heads, light_own, light_far))
    light_far = far_sent

    back = on_chip(
        heavy_output_kernel,
        [((seq_count, slots, out_cols), BF)],
        heads,
        heavy_output,
        query_map,
    )
    back = swap(back)
    back, light_far = lax.optimization_barrier((back, light_far))
    give = on_chip(give_kernel, [((2, per, slots, out_cols), BF)], back)
    got = lax.ppermute(give, "head", pair)
    far = on_chip(far_kernel, [((per, slots, out_cols), BF)], back, got)
    last = lax.ppermute(far, "head", across)
    return on_chip(
        finish_kernel,
        [((tok_rows, own_width), BF)],
        light_own,
        light_far,
        back,
        got,
        last,
        own_map,
        gate_map,
        off=True,
    )


def solution(mesh):
    placed = (
        P("seq", "head"),
        P(None, None, "head"),
        P("head", None),
        P(None, "seq", "head"),
        P("head", "seq"),
        P(),
        P(),
        P("seq", None),
    )

    def per_device(*args):
        seq_count, head_count = mesh.shape["seq"], mesh.shape["head"]
        local_heads = args[3].shape[2] // HD
        fits = head_count // 2 == 2 and seq_count % head_count == 0 and local_heads == seq_count
        return (one_head_a_device if fits else general)(*args)

    return jax.shard_map(
        per_device, mesh=mesh, in_specs=placed, out_specs=P("seq", "head"), check_vma=False
    )
```

```python
import functools
import math

import jax
import jax.numpy as jnp
from jax import lax
from jax.experimental import pallas as pl
from jax.experimental.pallas import tpu as pltpu
from jax.sharding import PartitionSpec as P

HD = 128
LB = 128
ROUTE = 32
BF = jnp.bfloat16
F32 = jnp.float32
VMEM = pl.BlockSpec(memory_space=pltpu.VMEM)
FIRST = (((0,), (0,)), ((), ()))
LAST = (((1,), (1,)), ((), ()))


def attend(queries, key_rows, value_rows):
    scores = jnp.einsum(
        "bqhe,bkhe->bhqk", queries, key_rows, preferred_element_type=jnp.float32
    ) / math.sqrt(queries.shape[-1])
    highest = jnp.max(scores, axis=-1, keepdims=True)
    expanded = jnp.exp(scores - highest)
    totals = jnp.sum(expanded, axis=-1)
    weighted = jnp.einsum(
        "bhqk,bkhe->bqhe",
        expanded.astype(jnp.bfloat16),
        value_rows,
        preferred_element_type=jnp.float32,
    )
    return (weighted / jnp.transpose(totals, (0, 2, 1))[..., None]).astype(jnp.bfloat16)


def routed_map(table, routed):
    counts = jnp.sum((table >= 0).astype(jnp.int32), axis=1)
    shard = jnp.arange(table.shape[0], dtype=jnp.int32)
    upper_end = jnp.sum(jnp.where(shard[None, :] <= shard[:, None], counts[None, :], 0), axis=1)
    lower_end = upper_end - counts
    compact_rows = jnp.arange(routed, dtype=jnp.int32)
    source_shard = jnp.sum((upper_end[None, :] <= compact_rows[:, None]).astype(jnp.int32), axis=1)
    onehot_shard = (
        source_shard[:, None] == jnp.arange(table.shape[0], dtype=jnp.int32)[None, :]
    ).astype(jnp.int32)
    within = compact_rows - jnp.sum(onehot_shard * lower_end[None, :], axis=1)
    return (source_shard * table.shape[1] + within, lower_end)


def project(query_part, source_part, weights):
    stacked = jnp.stack((query_part, source_part, source_part))
    return jnp.einsum("cmd,cdw->mcw", stacked, weights, preferred_element_type=jnp.float32)


def pick_rows(gathered, own_list):
    chosen = jnp.take(gathered, jnp.maximum(own_list, 0), axis=0)
    return jnp.where((own_list >= 0)[:, None], chosen, jnp.zeros_like(chosen))


def general(
    tokens,
    light_input,
    light_output,
    heavy_input,
    heavy_output,
    query_tokens,
    context_tokens,
    query_gate,
):
    gathered = lax.all_gather(tokens, "head", axis=1, tiled=True)
    tok_rows = gathered.shape[0]
    light_mapped = jnp.einsum(
        "td,cdw->ctw", gathered, light_input, preferred_element_type=jnp.float32
    ).astype(jnp.bfloat16)
    light_blocks = light_mapped.reshape(3, tok_rows // LB, LB, -1, HD)
    light_heads = attend(light_blocks[0], light_blocks[1], light_blocks[2]).reshape(tok_rows, -1)
    light_part = jnp.dot(light_heads, light_output, preferred_element_type=jnp.float32)
    seq_count = lax.axis_size("seq")
    routed = seq_count * tok_rows // ROUTE
    slot_count = query_tokens.shape[1]
    seq_index = lax.axis_index("seq")
    own_queries = lax.dynamic_index_in_dim(query_tokens, seq_index, 0, keepdims=False)
    own_sources = lax.dynamic_index_in_dim(context_tokens, seq_index, 0, keepdims=False)
    query_cols, source_cols = (
        lax.all_to_all(
            pick_rows(gathered, own_queries), "seq", split_axis=1, concat_axis=0, tiled=True
        ),
        lax.all_to_all(
            pick_rows(gathered, own_sources), "seq", split_axis=1, concat_axis=0, tiled=True
        ),
    )
    query_index, query_lower = routed_map(query_tokens, routed)
    source_index = routed_map(context_tokens, routed)[0]
    query_rows = jnp.take(query_cols, query_index, axis=0)
    source_rows = jnp.take(source_cols, source_index, axis=0)
    summed = lax.psum(project(query_rows, source_rows, heavy_input), "seq").astype(jnp.bfloat16)
    heavy_heads = attend(
        summed[:, 0].reshape(1, routed, -1, HD),
        summed[:, 1].reshape(1, routed, -1, HD),
        summed[:, 2].reshape(1, routed, -1, HD),
    ).reshape(routed, -1)
    heavy_part = jnp.dot(heavy_heads, heavy_output, preferred_element_type=jnp.float32)
    slot_live = query_tokens >= 0
    compact = query_lower[:, None] + jnp.arange(slot_count, dtype=jnp.int32)[None, :]
    outgoing = jnp.take(heavy_part, jnp.where(slot_live, compact, 0).reshape(-1), axis=0)
    outgoing = jnp.where(slot_live.reshape(-1)[:, None], outgoing, jnp.zeros_like(outgoing))
    returned = lax.all_to_all(
        outgoing.astype(jnp.bfloat16), "seq", split_axis=0, concat_axis=1, tiled=True
    ).astype(outgoing.dtype)
    scaled = returned * query_gate[0][:, None]
    targets = jnp.where(own_queries >= 0, own_queries, tok_rows)
    combined = light_part.at[targets].add(scaled, mode="drop")
    return lax.psum_scatter(combined.astype(jnp.bfloat16), "head", scatter_dimension=1, tiled=True)


def in_vmem(*arrays):
    return tuple(pltpu.with_memory_space_constraint(a, pltpu.VMEM) for a in arrays)


def on_chip(kernel, outs, *arrays, hbm=(), scratch=(), flops=0, moved=0, off=False, kept=()):
    made = [
        (jax.ShapeDtypeStruct if off and i not in kept else pltpu.VMEM)(*o)
        for i, o in enumerate(outs)
    ]
    result = pl.pallas_call(
        kernel,
        in_specs=[pl.BlockSpec(memory_space=pl.ANY)] * len(hbm) + [VMEM] * len(arrays),
        scratch_shapes=list(scratch),
        out_specs=[VMEM] * len(made),
        out_shape=made,
        compiler_params=pltpu.CompilerParams(vmem_limit_bytes=(60 if hbm else 8) << 20),
        cost_estimate=pl.CostEstimate(
            flops=int(flops), bytes_accessed=int(moved), transcendentals=0
        ),
    )(*hbm, *in_vmem(*arrays))
    return result if len(outs) > 1 else result[0]


def listed(count):
    inner = sorted(range(count), key=lambda i: 2 * abs(2 * i + 1 - count) // count)
    return [i ^ 1 for i in inner]


def spots(count):
    order = listed(count)
    return [order.index(i) for i in range(count)]


def look_up(values, index):
    found = jnp.int32(values[0])
    for i, value in enumerate(values[1:], 1):
        found = jnp.where(index == i, value, found)
    return found


def own_row(table, index):
    rows = lax.broadcasted_iota(jnp.int32, table.shape, 0)
    return jnp.sum(jnp.where(rows == index, table, 0), axis=0, keepdims=True)


def onehot(flags):
    return flags.astype(F32).astype(BF)


def compact_onehot(table, out_ref):
    shards, slots = table.shape
    spot = spots(shards)
    live = (table >= 0).astype(jnp.int32)
    counts = jnp.sum(live, axis=1, keepdims=True)
    row = lax.broadcasted_iota(jnp.int32, (out_ref.shape[0], slots), 0)
    place = lax.broadcasted_iota(jnp.int32, (1, slots), 1)
    for s in range(shards):
        here = (row == place) & (table[s : s + 1] >= 0)
        out_ref[:, spot[s] * slots : (spot[s] + 1) * slots] = onehot(here)
        place = place + counts[s : s + 1]


def pick_kernel(
    tok_hbm,
    query_hbm,
    source_hbm,
    gate_hbm,
    keep_ref,
    send_ref,
    mine_ref,
    query_map_ref,
    own_map_ref,
    gate_map_ref,
    tok_ref,
    query_ref,
    source_ref,
    gate_ref,
    sems,
):
    ends = (
        (query_hbm, query_ref),
        (source_hbm, source_ref),
        (gate_hbm, gate_ref),
        (tok_hbm, tok_ref),
    )
    copies = [pltpu.make_async_copy(*e, sems.at[i]) for i, e in enumerate(ends)]
    for copy in copies:
        copy.start()
    odd = lax.axis_index("head") % 2
    for copy in copies[:3]:
        copy.wait()
    query, source = query_ref[...], source_ref[...]
    own_q = own_row(query, lax.axis_index("seq"))
    own_s = own_row(source, lax.axis_index("seq"))
    spot = lax.broadcasted_iota(jnp.int32, own_map_ref.shape, 0)
    chosen = [onehot(spot == jnp.where(odd == k, own_q, own_s)) for k in range(2)]
    own_map_ref[...] = onehot(spot == own_q)
    compact_onehot(query, query_map_ref)
    compact_onehot(jnp.where(odd == 0, query, source), mine_ref)
    slots = own_q.shape[1]
    diagonal = lax.broadcasted_iota(jnp.int32, (slots, slots), 0) == lax.broadcasted_iota(
        jnp.int32, (slots, slots), 1
    )
    gate = jnp.sum(jnp.where(diagonal, gate_ref[...], 0.0), axis=1, keepdims=True)
    gate_map_ref[...] = jnp.broadcast_to(gate, gate_map_ref.shape)
    copies[3].wait()
    for ref, rows in zip((keep_ref, send_ref), chosen):
        ref[...] = lax.dot_general(rows, tok_ref[...], FIRST, preferred_element_type=F32).astype(
            BF
        )


def spread_kernel(keep_ref, got_ref, out_ref):
    odd = lax.axis_index("head") % 2
    keep, got = keep_ref[...], got_ref[...]
    width = out_ref.shape[2]
    per = keep.shape[1] // width
    spot = spots(out_ref.shape[0])
    for part, block in enumerate((jnp.where(odd == 0, keep, got), jnp.where(odd == 0, got, keep))):
        for i in range(per):
            for at in range(part * per + i, out_ref.shape[0], 2 * per):
                out_ref[spot[at]] = block[:, i * width : (i + 1) * width]


def compact_kernel(slots_ref, chosen_ref, out_ref):
    rows = slots_ref[...].reshape(-1, slots_ref.shape[2])
    out_ref[...] = jnp.dot(chosen_ref[...], rows, preferred_element_type=F32).astype(BF)


def project_kernel(mine_ref, pair_ref, across_ref, last_ref, weight_ref, out_ref):
    pairs = lax.axis_size("head") // 2
    holder = lax.axis_index("seq") * pairs // lax.axis_size("seq")
    holds = holder == lax.axis_index("head") // 2
    mine = jnp.where(holds, mine_ref[...], across_ref[...])
    other = jnp.where(holds, pair_ref[...], last_ref[...])
    odd = lax.axis_index("head") % 2
    query = jnp.where(odd == 0, mine, other)
    source = jnp.where(odd == 0, other, mine)
    spot = spots(out_ref.shape[0])
    for c, rows in enumerate((query, source, source)):
        part = jnp.dot(rows, weight_ref[c], preferred_element_type=F32).astype(BF)
        for g in range(out_ref.shape[0]):
            out_ref[spot[g], c] = part[:, g * HD : (g + 1) * HD]


def one_head(query, key, value):
    scores = lax.dot_general(query, key, LAST, preferred_element_type=F32) / math.sqrt(HD)
    expanded = jnp.exp(scores - jnp.max(scores, axis=-1, keepdims=True))
    totals = jnp.sum(expanded, axis=-1, keepdims=True)
    weighted = jnp.dot(expanded.astype(BF), value, preferred_element_type=F32)
    return (weighted / totals).astype(BF)


def heavy_attend_kernel(parts_ref, out_ref):
    total = parts_ref[0].astype(F32)
    for s in range(1, parts_ref.shape[0]):
        total = total + parts_ref[s].astype(F32)
    total = total.astype(BF)
    result = one_head(total[0], total[1], total[2])
    for s in range(out_ref.shape[0]):
        out_ref[s] = result


def heavy_output_kernel(heads_ref, weight_ref, chosen_ref, out_ref):
    rows = jnp.concatenate([heads_ref[i] for i in spots(heads_ref.shape[0])], axis=1)
    part = jnp.dot(rows, weight_ref[...], preferred_element_type=F32).astype(BF)
    spread = lax.dot_general(chosen_ref[...], part, FIRST, preferred_element_type=F32).astype(BF)
    out_ref[...] = spread.reshape(out_ref.shape)


def block_of(back_ref, head, per, i):
    spot = spots(back_ref.shape[0])
    return back_ref[look_up(spot[i::per], head)]


def give_kernel(back_ref, out_ref):
    head = lax.axis_index("head")
    per = out_ref.shape[1]
    for k, j in enumerate((1, 3)):
        for i in range(per):
            out_ref[k, i] = block_of(back_ref, head ^ j, per, i)


def far_kernel(back_ref, got_ref, out_ref):
    per = out_ref.shape[0]
    head = lax.axis_index("head")
    for i in range(per):
        mine = block_of(back_ref, head ^ 2, per, i).astype(F32)
        out_ref[i] = (mine + got_ref[1, i].astype(F32)).astype(BF)


def finish_kernel(
    light_ref, light_far_ref, back_ref, got_ref, last_ref, own_map_ref, gate_ref, out_ref
):
    head = lax.axis_index("head")
    per = last_ref.shape[0]
    chosen, gate = own_map_ref[...], gate_ref[:, :1]
    width = last_ref.shape[2]
    for j in range(per):
        mine = block_of(back_ref, head, per, j).astype(F32)
        scaled = (mine + got_ref[0, j].astype(F32) + last_ref[j].astype(F32)) * gate
        coarse = scaled.astype(BF)
        fine = (scaled - coarse.astype(F32)).astype(BF)
        added = jnp.dot(chosen, coarse, preferred_element_type=F32) + jnp.dot(
            chosen, fine, preferred_element_type=F32
        )
        cols = slice(j * width, (j + 1) * width)
        light = light_ref[:, cols] + light_far_ref[:, cols].astype(F32)
        out_ref[:, cols] = (light + added).astype(BF)


def light_kernel(flips, last, *refs):
    count = len(flips)
    pieces, (w_in, *refs) = refs[:count], refs[count:]
    if last:
        before, w_out, heads_ref, give_ref, before_ref, out_ref, *refs = refs
    else:
        sum_ref, *refs = refs
    tok_ref, in_ref, sems = refs[:3]
    head = lax.axis_index("head")
    depth = pieces[0].shape[1]
    copies = []
    for i, (j, piece) in enumerate(zip(flips, pieces)):
        rows = pl.ds(pl.multiple_of((head ^ j) * depth, depth), depth)
        copies.append(pltpu.make_async_copy(piece, tok_ref.at[i], sems.at[0, i]))
        for c in range(3):
            copies.append(
                pltpu.make_async_copy(w_in.at[c, rows, :], in_ref.at[c, i], sems.at[1 + c, i])
            )
    late = []
    if last:
        late_sems = refs[3]
        width = give_ref.shape[2]
        late.append(pltpu.make_async_copy(before, before_ref, late_sems.at[2]))
        for i, j in enumerate((1, 3)):
            cols = pl.ds(pl.multiple_of((head ^ j) * width, width), width)
            late.append(pltpu.make_async_copy(w_out.at[:, cols], out_ref.at[i], late_sems.at[i]))
    for copy in copies + late:
        copy.start()
    total = [None] * 3
    for i in range(count):
        copies[4 * i].wait()
        for c in range(3):
            copies[4 * i + 1 + c].wait()
            part = jnp.dot(tok_ref[i], in_ref[c, i], preferred_element_type=F32)
            total[c] = part if i == 0 else total[c] + part
    if not last:
        for c in range(3):
            sum_ref[c] = total[c]
        return
    late[0].wait()
    mapped = [(before_ref[c] + total[c]).astype(BF) for c in range(3)]
    for b in range(heads_ref.shape[0] // LB):
        for g in range(heads_ref.shape[1] // HD):
            at = (slice(b * LB, (b + 1) * LB), slice(g * HD, (g + 1) * HD))
            heads_ref[at] = one_head(*(m[at] for m in mapped))
    for i in range(2):
        late[1 + i].wait()
        give_ref[i] = jnp.dot(heads_ref[...], out_ref[i], preferred_element_type=F32).astype(BF)


def light_own_kernel(w_out, got_ref, heads_ref, own_ref, far_ref, out_ref, sems):
    head = lax.axis_index("head")
    width = own_ref.shape[1]
    copies = []
    for i, j in enumerate((0, 2)):
        cols = pl.ds(pl.multiple_of((head ^ j) * width, width), width)
        copies.append(pltpu.make_async_copy(w_out.at[:, cols], out_ref.at[i], sems.at[i]))
    for copy in copies:
        copy.start()
    for i, ref in enumerate((own_ref, far_ref)):
        copies[i].wait()
        block = jnp.dot(heads_ref[...], out_ref[i], preferred_element_type=F32)
        ref[...] = (block + got_ref[i].astype(F32)).astype(ref.dtype)


def light_call(flips, last, outs, pieces, *arrays, scratch=()):
    count = len(flips)
    rows, width = pieces[0].shape
    return on_chip(
        functools.partial(light_kernel, flips, last),
        outs,
        hbm=(*pieces, *arrays),
        scratch=[
            *scratch,
            pltpu.VMEM((count, rows, width), BF),
            pltpu.VMEM((3, count, width, arrays[0].shape[2]), BF),
            pltpu.SemaphoreType.DMA((4, count)),
            pltpu.SemaphoreType.DMA((3,)),
        ],
        flops=6 * count * rows * width * arrays[0].shape[2],
        off=True,
        kept=(0,) if last else (),
    )


def one_head_a_device(
    tokens,
    light_input,
    light_output,
    heavy_input,
    heavy_output,
    query_tokens,
    context_tokens,
    query_gate,
):
    seq_count, head_count = lax.axis_size("seq"), lax.axis_size("head")
    tok_rows, own_width = tokens.shape
    slots = query_tokens.shape[1]
    routed = seq_count * tok_rows // ROUTE
    part_width, head_cols = heavy_input.shape[1:]
    out_cols = heavy_output.shape[1]
    light_cols = light_input.shape[2]
    per = seq_count // head_count
    pair, across = ([(i, i ^ j) for i in range(head_count)] for j in (1, 2))

    def swap(x):
        return lax.all_to_all(
            x,
            "seq",
            split_axis=0,
            concat_axis=0,
            tiled=True,
            axis_index_groups=[listed(seq_count)],
        )

    routes = (routed, seq_count * slots)
    keep, send, mine_map, query_map, own_map, gate_map = on_chip(
        pick_kernel,
        [((slots, own_width), BF)] * 2
        + [(routes, BF)] * 2
        + [((tok_rows, slots), BF), ((slots, HD), F32)],
        hbm=(tokens, query_tokens, context_tokens, query_gate),
        scratch=[
            pltpu.VMEM(tokens.shape, BF),
            pltpu.VMEM(query_tokens.shape, jnp.int32),
            pltpu.VMEM(context_tokens.shape, jnp.int32),
            pltpu.VMEM(query_gate.shape, F32),
            pltpu.SemaphoreType.DMA((4,)),
        ],
    )
    got = lax.ppermute(send, "head", pair)
    spread = on_chip(spread_kernel, [((seq_count, slots, part_width), BF)], keep, got)
    token_far = lax.ppermute(tokens, "head", across)
    token_pair = lax.ppermute(tokens, "head", pair)
    spread, tokens, token_pair = lax.optimization_barrier((spread, tokens, token_pair))
    light_sum = light_call(
        (0, 1),
        False,
        [((3, tok_rows, light_cols), F32)],
        (tokens, token_pair),
        light_input,
    )
    spread = swap(spread)
    spread, token_far, light_sum = lax.optimization_barrier((spread, token_far, light_sum))
    token_last = lax.ppermute(token_far, "head", pair)
    mine = on_chip(compact_kernel, [((routed, part_width), BF)], spread, mine_map, moved=20 << 20)
    diagonal = [(i, i ^ 3) for i in range(head_count)]
    rows = [mine, *(lax.ppermute(mine, "head", p) for p in (pair, across, diagonal))]
    parts = on_chip(
        project_kernel, [((seq_count, 3, routed, HD), BF)], *rows, heavy_input
    )

    parts, light_sum, token_far, token_last = lax.optimization_barrier(
        (parts, light_sum, token_far, token_last)
    )
    light_heads, light_give = light_call(
        (2, 3),
        True,
        [((tok_rows, light_cols), BF), ((2, tok_rows, own_width), BF)],
        (token_far, token_last),
        light_input,
        light_sum,
        light_output,
        scratch=[
            pltpu.VMEM((3, tok_rows, light_cols), F32),
            pltpu.VMEM((2, light_cols, own_width), BF),
        ],
    )
    parts = swap(parts)
    parts, light_heads, light_give = lax.optimization_barrier((parts, light_heads, light_give))
    light_got = lax.ppermute(light_give, "head", pair)
    heads = on_chip(heavy_attend_kernel, [((seq_count, routed, HD), BF)], parts)
    light_own, light_far = on_chip(
        light_own_kernel,
        [((tok_rows, own_width), F32), ((tok_rows, own_width), BF)],
        light_got,
        light_heads,
        hbm=(light_output,),
        scratch=[pltpu.VMEM((2, light_cols, own_width), BF), pltpu.SemaphoreType.DMA((2,))],
        flops=4 * tok_rows * light_cols * own_width,
        off=True,
    )
    heads = swap(heads)
    far_sent = lax.ppermute(light_far, "head", across)
    heads, light_own, light_far = lax.optimization_barrier((heads, light_own, light_far))
    light_far = far_sent

    back = on_chip(
        heavy_output_kernel,
        [((seq_count, slots, out_cols), BF)],
        heads,
        heavy_output,
        query_map,
    )
    back = swap(back)
    back, light_far = lax.optimization_barrier((back, light_far))
    give = on_chip(give_kernel, [((2, per, slots, out_cols), BF)], back)
    got = lax.ppermute(give, "head", pair)
    far = on_chip(far_kernel, [((per, slots, out_cols), BF)], back, got)
    last = lax.ppermute(far, "head", across)
    return on_chip(
        finish_kernel,
        [((tok_rows, own_width), BF)],
        light_own,
        light_far,
        back,
        got,
        last,
        own_map,
        gate_map,
        off=True,
    )


def solution(mesh):
    placed = (
        P("seq", "head"),
        P(None, None, "head"),
        P("head", None),
        P(None, "seq", "head"),
        P("head", "seq"),
        P(),
        P(),
        P("seq", None),
    )

    def per_device(*args):
        seq_count, head_count = mesh.shape["seq"], mesh.shape["head"]
        local_heads = args[3].shape[2] // HD
        fits = head_count // 2 == 2 and seq_count % head_count == 0 and local_heads == seq_count
        return (one_head_a_device if fits else general)(*args)

    return jax.shard_map(
        per_device, mesh=mesh, in_specs=placed, out_specs=P("seq", "head"), check_vma=False
    )
```

```python
import functools
import math

import jax
import jax.numpy as jnp
from jax import lax
from jax.experimental import pallas as pl
from jax.experimental.pallas import tpu as pltpu
from jax.sharding import PartitionSpec as P

HD = 128
LB = 128
ROUTE = 32
BF = jnp.bfloat16
F32 = jnp.float32
VMEM = pl.BlockSpec(memory_space=pltpu.VMEM)
FIRST = (((0,), (0,)), ((), ()))
LAST = (((1,), (1,)), ((), ()))


def attend(queries, key_rows, value_rows):
    scores = jnp.einsum(
        "bqhe,bkhe->bhqk", queries, key_rows, preferred_element_type=jnp.float32
    ) / math.sqrt(queries.shape[-1])
    highest = jnp.max(scores, axis=-1, keepdims=True)
    expanded = jnp.exp(scores - highest)
    totals = jnp.sum(expanded, axis=-1)
    weighted = jnp.einsum(
        "bhqk,bkhe->bqhe",
        expanded.astype(jnp.bfloat16),
        value_rows,
        preferred_element_type=jnp.float32,
    )
    return (weighted / jnp.transpose(totals, (0, 2, 1))[..., None]).astype(jnp.bfloat16)


def routed_map(table, routed):
    counts = jnp.sum((table >= 0).astype(jnp.int32), axis=1)
    shard = jnp.arange(table.shape[0], dtype=jnp.int32)
    upper_end = jnp.sum(jnp.where(shard[None, :] <= shard[:, None], counts[None, :], 0), axis=1)
    lower_end = upper_end - counts
    compact_rows = jnp.arange(routed, dtype=jnp.int32)
    source_shard = jnp.sum((upper_end[None, :] <= compact_rows[:, None]).astype(jnp.int32), axis=1)
    onehot_shard = (
        source_shard[:, None] == jnp.arange(table.shape[0], dtype=jnp.int32)[None, :]
    ).astype(jnp.int32)
    within = compact_rows - jnp.sum(onehot_shard * lower_end[None, :], axis=1)
    return (source_shard * table.shape[1] + within, lower_end)


def project(query_part, source_part, weights):
    stacked = jnp.stack((query_part, source_part, source_part))
    return jnp.einsum("cmd,cdw->mcw", stacked, weights, preferred_element_type=jnp.float32)


def pick_rows(gathered, own_list):
    chosen = jnp.take(gathered, jnp.maximum(own_list, 0), axis=0)
    return jnp.where((own_list >= 0)[:, None], chosen, jnp.zeros_like(chosen))


def general(
    tokens,
    light_input,
    light_output,
    heavy_input,
    heavy_output,
    query_tokens,
    context_tokens,
    query_gate,
):
    gathered = lax.all_gather(tokens, "head", axis=1, tiled=True)
    tok_rows = gathered.shape[0]
    light_mapped = jnp.einsum(
        "td,cdw->ctw", gathered, light_input, preferred_element_type=jnp.float32
    ).astype(jnp.bfloat16)
    light_blocks = light_mapped.reshape(3, tok_rows // LB, LB, -1, HD)
    light_heads = attend(light_blocks[0], light_blocks[1], light_blocks[2]).reshape(tok_rows, -1)
    light_part = jnp.dot(light_heads, light_output, preferred_element_type=jnp.float32)
    seq_count = lax.axis_size("seq")
    routed = seq_count * tok_rows // ROUTE
    slot_count = query_tokens.shape[1]
    seq_index = lax.axis_index("seq")
    own_queries = lax.dynamic_index_in_dim(query_tokens, seq_index, 0, keepdims=False)
    own_sources = lax.dynamic_index_in_dim(context_tokens, seq_index, 0, keepdims=False)
    query_cols, source_cols = (
        lax.all_to_all(
            pick_rows(gathered, own_queries), "seq", split_axis=1, concat_axis=0, tiled=True
        ),
        lax.all_to_all(
            pick_rows(gathered, own_sources), "seq", split_axis=1, concat_axis=0, tiled=True
        ),
    )
    query_index, query_lower = routed_map(query_tokens, routed)
    source_index = routed_map(context_tokens, routed)[0]
    query_rows = jnp.take(query_cols, query_index, axis=0)
    source_rows = jnp.take(source_cols, source_index, axis=0)
    summed = lax.psum(project(query_rows, source_rows, heavy_input), "seq").astype(jnp.bfloat16)
    heavy_heads = attend(
        summed[:, 0].reshape(1, routed, -1, HD),
        summed[:, 1].reshape(1, routed, -1, HD),
        summed[:, 2].reshape(1, routed, -1, HD),
    ).reshape(routed, -1)
    heavy_part = jnp.dot(heavy_heads, heavy_output, preferred_element_type=jnp.float32)
    slot_live = query_tokens >= 0
    compact = query_lower[:, None] + jnp.arange(slot_count, dtype=jnp.int32)[None, :]
    outgoing = jnp.take(heavy_part, jnp.where(slot_live, compact, 0).reshape(-1), axis=0)
    outgoing = jnp.where(slot_live.reshape(-1)[:, None], outgoing, jnp.zeros_like(outgoing))
    returned = lax.all_to_all(
        outgoing.astype(jnp.bfloat16), "seq", split_axis=0, concat_axis=1, tiled=True
    ).astype(outgoing.dtype)
    scaled = returned * query_gate[0][:, None]
    targets = jnp.where(own_queries >= 0, own_queries, tok_rows)
    combined = light_part.at[targets].add(scaled, mode="drop")
    return lax.psum_scatter(combined.astype(jnp.bfloat16), "head", scatter_dimension=1, tiled=True)


def in_vmem(*arrays):
    return tuple(pltpu.with_memory_space_constraint(a, pltpu.VMEM) for a in arrays)


def on_chip(kernel, outs, *arrays, hbm=(), scratch=(), flops=0, moved=0, off=False, kept=()):
    made = [
        (jax.ShapeDtypeStruct if off and i not in kept else pltpu.VMEM)(*o)
        for i, o in enumerate(outs)
    ]
    result = pl.pallas_call(
        kernel,
        in_specs=[pl.BlockSpec(memory_space=pl.ANY)] * len(hbm) + [VMEM] * len(arrays),
        scratch_shapes=list(scratch),
        out_specs=[VMEM] * len(made),
        out_shape=made,
        compiler_params=pltpu.CompilerParams(vmem_limit_bytes=(60 if hbm else 8) << 20),
        cost_estimate=pl.CostEstimate(
            flops=int(flops), bytes_accessed=int(moved), transcendentals=0
        ),
    )(*hbm, *in_vmem(*arrays))
    return result if len(outs) > 1 else result[0]


def listed(count):
    inner = range(count // 4, count - count // 4)
    order = sorted(inner, key=lambda i: (abs(2 * i + 1 - count), -i))
    return order + [i for i in reversed(range(count)) if i not in inner]


def spots(count):
    order = listed(count)
    return [order.index(i) for i in range(count)]


def look_up(values, index):
    found = jnp.int32(values[0])
    for i, value in enumerate(values[1:], 1):
        found = jnp.where(index == i, value, found)
    return found


def own_row(table, index):
    rows = lax.broadcasted_iota(jnp.int32, table.shape, 0)
    return jnp.sum(jnp.where(rows == index, table, 0), axis=0, keepdims=True)


def onehot(flags):
    return flags.astype(F32).astype(BF)


def compact_onehot(table, out_ref):
    shards, slots = table.shape
    spot = spots(shards)
    live = (table >= 0).astype(jnp.int32)
    counts = jnp.sum(live, axis=1, keepdims=True)
    row = lax.broadcasted_iota(jnp.int32, (out_ref.shape[0], slots), 0)
    place = lax.broadcasted_iota(jnp.int32, (1, slots), 1)
    for s in range(shards):
        here = (row == place) & (table[s : s + 1] >= 0)
        out_ref[:, spot[s] * slots : (spot[s] + 1) * slots] = onehot(here)
        place = place + counts[s : s + 1]


def pick_kernel(
    tok_hbm,
    query_hbm,
    source_hbm,
    gate_hbm,
    keep_ref,
    send_ref,
    mine_ref,
    query_map_ref,
    own_map_ref,
    gate_map_ref,
    tok_ref,
    query_ref,
    source_ref,
    gate_ref,
    sems,
):
    ends = (
        (query_hbm, query_ref),
        (source_hbm, source_ref),
        (gate_hbm, gate_ref),
        (tok_hbm, tok_ref),
    )
    copies = [pltpu.make_async_copy(*e, sems.at[i]) for i, e in enumerate(ends)]
    for copy in copies:
        copy.start()
    odd = lax.axis_index("head") % 2
    for copy in copies[:3]:
        copy.wait()
    query, source = query_ref[...], source_ref[...]
    own_q = own_row(query, lax.axis_index("seq"))
    own_s = own_row(source, lax.axis_index("seq"))
    spot = lax.broadcasted_iota(jnp.int32, own_map_ref.shape, 0)
    chosen = [onehot(spot == jnp.where(odd == k, own_q, own_s)) for k in range(2)]
    own_map_ref[...] = onehot(spot == own_q)
    compact_onehot(query, query_map_ref)
    compact_onehot(jnp.where(odd == 0, query, source), mine_ref)
    slots = own_q.shape[1]
    diagonal = lax.broadcasted_iota(jnp.int32, (slots, slots), 0) == lax.broadcasted_iota(
        jnp.int32, (slots, slots), 1
    )
    gate = jnp.sum(jnp.where(diagonal, gate_ref[...], 0.0), axis=1, keepdims=True)
    gate_map_ref[...] = jnp.broadcast_to(gate, gate_map_ref.shape)
    copies[3].wait()
    for ref, rows in zip((keep_ref, send_ref), chosen):
        ref[...] = lax.dot_general(rows, tok_ref[...], FIRST, preferred_element_type=F32).astype(
            BF
        )


def spread_kernel(keep_ref, got_ref, out_ref):
    odd = lax.axis_index("head") % 2
    keep, got = keep_ref[...], got_ref[...]
    width = out_ref.shape[2]
    per = keep.shape[1] // width
    spot = spots(out_ref.shape[0])
    for part, block in enumerate((jnp.where(odd == 0, keep, got), jnp.where(odd == 0, got, keep))):
        for i in range(per):
            for at in range(part * per + i, out_ref.shape[0], 2 * per):
                out_ref[spot[at]] = block[:, i * width : (i + 1) * width]


def compact_kernel(slots_ref, chosen_ref, out_ref):
    rows = slots_ref[...].reshape(-1, slots_ref.shape[2])
    out_ref[...] = jnp.dot(chosen_ref[...], rows, preferred_element_type=F32).astype(BF)


def project_kernel(mine_ref, pair_ref, across_ref, last_ref, weight_ref, out_ref):
    pairs = lax.axis_size("head") // 2
    holder = lax.axis_index("seq") * pairs // lax.axis_size("seq")
    holds = holder == lax.axis_index("head") // 2
    mine = jnp.where(holds, mine_ref[...], across_ref[...])
    other = jnp.where(holds, pair_ref[...], last_ref[...])
    odd = lax.axis_index("head") % 2
    query = jnp.where(odd == 0, mine, other)
    source = jnp.where(odd == 0, other, mine)
    spot = spots(out_ref.shape[0])
    for c, rows in enumerate((query, source, source)):
        part = jnp.dot(rows, weight_ref[c], preferred_element_type=F32).astype(BF)
        for g in range(out_ref.shape[0]):
            out_ref[spot[g], c] = part[:, g * HD : (g + 1) * HD]


def one_head(query, key, value):
    scores = lax.dot_general(query, key, LAST, preferred_element_type=F32) / math.sqrt(HD)
    expanded = jnp.exp(scores - jnp.max(scores, axis=-1, keepdims=True))
    totals = jnp.sum(expanded, axis=-1, keepdims=True)
    weighted = jnp.dot(expanded.astype(BF), value, preferred_element_type=F32)
    return (weighted / totals).astype(BF)


def heavy_attend_kernel(parts_ref, out_ref):
    total = parts_ref[0].astype(F32)
    for s in range(1, parts_ref.shape[0]):
        total = total + parts_ref[s].astype(F32)
    total = total.astype(BF)
    result = one_head(total[0], total[1], total[2])
    for s in range(out_ref.shape[0]):
        out_ref[s] = result


def heavy_output_kernel(heads_ref, weight_ref, chosen_ref, out_ref):
    rows = jnp.concatenate([heads_ref[i] for i in spots(heads_ref.shape[0])], axis=1)
    part = jnp.dot(rows, weight_ref[...], preferred_element_type=F32).astype(BF)
    spread = lax.dot_general(chosen_ref[...], part, FIRST, preferred_element_type=F32).astype(BF)
    out_ref[...] = spread.reshape(out_ref.shape)


def block_of(back_ref, head, per, i):
    spot = spots(back_ref.shape[0])
    return back_ref[look_up(spot[i::per], head)]


def give_kernel(back_ref, out_ref):
    head = lax.axis_index("head")
    per = out_ref.shape[1]
    for k, j in enumerate((1, 3)):
        for i in range(per):
            out_ref[k, i] = block_of(back_ref, head ^ j, per, i)


def far_kernel(back_ref, got_ref, out_ref):
    per = out_ref.shape[0]
    head = lax.axis_index("head")
    for i in range(per):
        mine = block_of(back_ref, head ^ 2, per, i).astype(F32)
        out_ref[i] = (mine + got_ref[1, i].astype(F32)).astype(BF)


def finish_kernel(
    light_ref, light_far_ref, back_ref, got_ref, last_ref, own_map_ref, gate_ref, out_ref
):
    head = lax.axis_index("head")
    per = last_ref.shape[0]
    chosen, gate = own_map_ref[...], gate_ref[:, :1]
    width = last_ref.shape[2]
    for j in range(per):
        mine = block_of(back_ref, head, per, j).astype(F32)
        scaled = (mine + got_ref[0, j].astype(F32) + last_ref[j].astype(F32)) * gate
        coarse = scaled.astype(BF)
        fine = (scaled - coarse.astype(F32)).astype(BF)
        added = jnp.dot(chosen, coarse, preferred_element_type=F32) + jnp.dot(
            chosen, fine, preferred_element_type=F32
        )
        cols = slice(j * width, (j + 1) * width)
        light = light_ref[:, cols] + light_far_ref[:, cols].astype(F32)
        out_ref[:, cols] = (light + added).astype(BF)


def light_kernel(flips, last, *refs):
    count = len(flips)
    pieces, (w_in, *refs) = refs[:count], refs[count:]
    if last:
        before, w_out, heads_ref, give_ref, before_ref, out_ref, *refs = refs
    else:
        sum_ref, *refs = refs
    tok_ref, in_ref, sems = refs[:3]
    head = lax.axis_index("head")
    depth = pieces[0].shape[1]
    copies = []
    for i, (j, piece) in enumerate(zip(flips, pieces)):
        rows = pl.ds(pl.multiple_of((head ^ j) * depth, depth), depth)
        copies.append(pltpu.make_async_copy(piece, tok_ref.at[i], sems.at[0, i]))
        for c in range(3):
            copies.append(
                pltpu.make_async_copy(w_in.at[c, rows, :], in_ref.at[c, i], sems.at[1 + c, i])
            )
    late = []
    if last:
        late_sems = refs[3]
        width = give_ref.shape[2]
        late.append(pltpu.make_async_copy(before, before_ref, late_sems.at[2]))
        for i, j in enumerate((1, 3)):
            cols = pl.ds(pl.multiple_of((head ^ j) * width, width), width)
            late.append(pltpu.make_async_copy(w_out.at[:, cols], out_ref.at[i], late_sems.at[i]))
    for copy in copies + late:
        copy.start()
    total = [None] * 3
    for i in range(count):
        copies[4 * i].wait()
        for c in range(3):
            copies[4 * i + 1 + c].wait()
            part = jnp.dot(tok_ref[i], in_ref[c, i], preferred_element_type=F32)
            total[c] = part if i == 0 else total[c] + part
    if not last:
        for c in range(3):
            sum_ref[c] = total[c]
        return
    late[0].wait()
    mapped = [(before_ref[c] + total[c]).astype(BF) for c in range(3)]
    for b in range(heads_ref.shape[0] // LB):
        for g in range(heads_ref.shape[1] // HD):
            at = (slice(b * LB, (b + 1) * LB), slice(g * HD, (g + 1) * HD))
            heads_ref[at] = one_head(*(m[at] for m in mapped))
    for i in range(2):
        late[1 + i].wait()
        give_ref[i] = jnp.dot(heads_ref[...], out_ref[i], preferred_element_type=F32).astype(BF)


def light_own_kernel(w_out, got_ref, heads_ref, own_ref, far_ref, out_ref, sems):
    head = lax.axis_index("head")
    width = own_ref.shape[1]
    copies = []
    for i, j in enumerate((0, 2)):
        cols = pl.ds(pl.multiple_of((head ^ j) * width, width), width)
        copies.append(pltpu.make_async_copy(w_out.at[:, cols], out_ref.at[i], sems.at[i]))
    for copy in copies:
        copy.start()
    for i, ref in enumerate((own_ref, far_ref)):
        copies[i].wait()
        block = jnp.dot(heads_ref[...], out_ref[i], preferred_element_type=F32)
        ref[...] = (block + got_ref[i].astype(F32)).astype(ref.dtype)


def light_call(flips, last, outs, pieces, *arrays, scratch=()):
    count = len(flips)
    rows, width = pieces[0].shape
    return on_chip(
        functools.partial(light_kernel, flips, last),
        outs,
        hbm=(*pieces, *arrays),
        scratch=[
            *scratch,
            pltpu.VMEM((count, rows, width), BF),
            pltpu.VMEM((3, count, width, arrays[0].shape[2]), BF),
            pltpu.SemaphoreType.DMA((4, count)),
            pltpu.SemaphoreType.DMA((3,)),
        ],
        flops=6 * count * rows * width * arrays[0].shape[2],
        off=True,
        kept=(0,) if last else (),
    )


def one_head_a_device(
    tokens,
    light_input,
    light_output,
    heavy_input,
    heavy_output,
    query_tokens,
    context_tokens,
    query_gate,
):
    seq_count, head_count = lax.axis_size("seq"), lax.axis_size("head")
    tok_rows, own_width = tokens.shape
    slots = query_tokens.shape[1]
    routed = seq_count * tok_rows // ROUTE
    part_width, head_cols = heavy_input.shape[1:]
    out_cols = heavy_output.shape[1]
    light_cols = light_input.shape[2]
    per = seq_count // head_count
    pair, across = ([(i, i ^ j) for i in range(head_count)] for j in (1, 2))

    def swap(x):
        return lax.all_to_all(
            x,
            "seq",
            split_axis=0,
            concat_axis=0,
            tiled=True,
            axis_index_groups=[listed(seq_count)],
        )

    routes = (routed, seq_count * slots)
    keep, send, mine_map, query_map, own_map, gate_map = on_chip(
        pick_kernel,
        [((slots, own_width), BF)] * 2
        + [(routes, BF)] * 2
        + [((tok_rows, slots), BF), ((slots, HD), F32)],
        hbm=(tokens, query_tokens, context_tokens, query_gate),
        scratch=[
            pltpu.VMEM(tokens.shape, BF),
            pltpu.VMEM(query_tokens.shape, jnp.int32),
            pltpu.VMEM(context_tokens.shape, jnp.int32),
            pltpu.VMEM(query_gate.shape, F32),
            pltpu.SemaphoreType.DMA((4,)),
        ],
    )
    got = lax.ppermute(send, "head", pair)
    spread = on_chip(spread_kernel, [((seq_count, slots, part_width), BF)], keep, got)
    token_far = lax.ppermute(tokens, "head", across)
    token_pair = lax.ppermute(tokens, "head", pair)
    spread, tokens, token_pair = lax.optimization_barrier((spread, tokens, token_pair))
    light_sum = light_call(
        (0, 1),
        False,
        [((3, tok_rows, light_cols), F32)],
        (tokens, token_pair),
        light_input,
    )
    spread = swap(spread)
    spread, token_far, light_sum = lax.optimization_barrier((spread, token_far, light_sum))
    token_last = lax.ppermute(token_far, "head", pair)
    mine = on_chip(compact_kernel, [((routed, part_width), BF)], spread, mine_map, moved=20 << 20)
    diagonal = [(i, i ^ 3) for i in range(head_count)]
    rows = [mine, *(lax.ppermute(mine, "head", p) for p in (pair, across, diagonal))]
    parts = on_chip(
        project_kernel, [((seq_count, 3, routed, HD), BF)], *rows, heavy_input
    )

    parts, light_sum, token_far, token_last = lax.optimization_barrier(
        (parts, light_sum, token_far, token_last)
    )
    light_heads, light_give = light_call(
        (2, 3),
        True,
        [((tok_rows, light_cols), BF), ((2, tok_rows, own_width), BF)],
        (token_far, token_last),
        light_input,
        light_sum,
        light_output,
        scratch=[
            pltpu.VMEM((3, tok_rows, light_cols), F32),
            pltpu.VMEM((2, light_cols, own_width), BF),
        ],
    )
    parts = swap(parts)
    parts, light_heads, light_give = lax.optimization_barrier((parts, light_heads, light_give))
    light_got = lax.ppermute(light_give, "head", pair)
    heads = on_chip(heavy_attend_kernel, [((seq_count, routed, HD), BF)], parts)
    light_own, light_far = on_chip(
        light_own_kernel,
        [((tok_rows, own_width), F32), ((tok_rows, own_width), BF)],
        light_got,
        light_heads,
        hbm=(light_output,),
        scratch=[pltpu.VMEM((2, light_cols, own_width), BF), pltpu.SemaphoreType.DMA((2,))],
        flops=4 * tok_rows * light_cols * own_width,
        off=True,
    )
    heads = swap(heads)
    far_sent = lax.ppermute(light_far, "head", across)
    heads, light_own, light_far = lax.optimization_barrier((heads, light_own, light_far))
    light_far = far_sent

    back = on_chip(
        heavy_output_kernel,
        [((seq_count, slots, out_cols), BF)],
        heads,
        heavy_output,
        query_map,
    )
    back = swap(back)
    back, light_far = lax.optimization_barrier((back, light_far))
    give = on_chip(give_kernel, [((2, per, slots, out_cols), BF)], back)
    got = lax.ppermute(give, "head", pair)
    far = on_chip(far_kernel, [((per, slots, out_cols), BF)], back, got)
    last = lax.ppermute(far, "head", across)
    return on_chip(
        finish_kernel,
        [((tok_rows, own_width), BF)],
        light_own,
        light_far,
        back,
        got,
        last,
        own_map,
        gate_map,
        off=True,
    )


def solution(mesh):
    placed = (
        P("seq", "head"),
        P(None, None, "head"),
        P("head", None),
        P(None, "seq", "head"),
        P("head", "seq"),
        P(),
        P(),
        P("seq", None),
    )

    def per_device(*args):
        seq_count, head_count = mesh.shape["seq"], mesh.shape["head"]
        local_heads = args[3].shape[2] // HD
        fits = head_count // 2 == 2 and seq_count % head_count == 0 and local_heads == seq_count
        return (one_head_a_device if fits else general)(*args)

    return jax.shard_map(
        per_device, mesh=mesh, in_specs=placed, out_specs=P("seq", "head"), check_vma=False
    )
```

```python
import functools
import math

import jax
import jax.numpy as jnp
from jax import lax
from jax.experimental import pallas as pl
from jax.experimental.pallas import tpu as pltpu
from jax.sharding import PartitionSpec as P

HD = 128
LB = 128
ROUTE = 32
BF = jnp.bfloat16
F32 = jnp.float32
VMEM = pl.BlockSpec(memory_space=pltpu.VMEM)
FIRST = (((0,), (0,)), ((), ()))
LAST = (((1,), (1,)), ((), ()))


def attend(queries, key_rows, value_rows):
    scores = jnp.einsum(
        "bqhe,bkhe->bhqk", queries, key_rows, preferred_element_type=jnp.float32
    ) / math.sqrt(queries.shape[-1])
    highest = jnp.max(scores, axis=-1, keepdims=True)
    expanded = jnp.exp(scores - highest)
    totals = jnp.sum(expanded, axis=-1)
    weighted = jnp.einsum(
        "bhqk,bkhe->bqhe",
        expanded.astype(jnp.bfloat16),
        value_rows,
        preferred_element_type=jnp.float32,
    )
    return (weighted / jnp.transpose(totals, (0, 2, 1))[..., None]).astype(jnp.bfloat16)


def routed_map(table, routed):
    counts = jnp.sum((table >= 0).astype(jnp.int32), axis=1)
    shard = jnp.arange(table.shape[0], dtype=jnp.int32)
    upper_end = jnp.sum(jnp.where(shard[None, :] <= shard[:, None], counts[None, :], 0), axis=1)
    lower_end = upper_end - counts
    compact_rows = jnp.arange(routed, dtype=jnp.int32)
    source_shard = jnp.sum((upper_end[None, :] <= compact_rows[:, None]).astype(jnp.int32), axis=1)
    onehot_shard = (
        source_shard[:, None] == jnp.arange(table.shape[0], dtype=jnp.int32)[None, :]
    ).astype(jnp.int32)
    within = compact_rows - jnp.sum(onehot_shard * lower_end[None, :], axis=1)
    return (source_shard * table.shape[1] + within, lower_end)


def project(query_part, source_part, weights):
    stacked = jnp.stack((query_part, source_part, source_part))
    return jnp.einsum("cmd,cdw->mcw", stacked, weights, preferred_element_type=jnp.float32)


def pick_rows(gathered, own_list):
    chosen = jnp.take(gathered, jnp.maximum(own_list, 0), axis=0)
    return jnp.where((own_list >= 0)[:, None], chosen, jnp.zeros_like(chosen))


def general(
    tokens,
    light_input,
    light_output,
    heavy_input,
    heavy_output,
    query_tokens,
    context_tokens,
    query_gate,
):
    gathered = lax.all_gather(tokens, "head", axis=1, tiled=True)
    tok_rows = gathered.shape[0]
    light_mapped = jnp.einsum(
        "td,cdw->ctw", gathered, light_input, preferred_element_type=jnp.float32
    ).astype(jnp.bfloat16)
    light_blocks = light_mapped.reshape(3, tok_rows // LB, LB, -1, HD)
    light_heads = attend(light_blocks[0], light_blocks[1], light_blocks[2]).reshape(tok_rows, -1)
    light_part = jnp.dot(light_heads, light_output, preferred_element_type=jnp.float32)
    seq_count = lax.axis_size("seq")
    routed = seq_count * tok_rows // ROUTE
    slot_count = query_tokens.shape[1]
    seq_index = lax.axis_index("seq")
    own_queries = lax.dynamic_index_in_dim(query_tokens, seq_index, 0, keepdims=False)
    own_sources = lax.dynamic_index_in_dim(context_tokens, seq_index, 0, keepdims=False)
    query_cols, source_cols = (
        lax.all_to_all(
            pick_rows(gathered, own_queries), "seq", split_axis=1, concat_axis=0, tiled=True
        ),
        lax.all_to_all(
            pick_rows(gathered, own_sources), "seq", split_axis=1, concat_axis=0, tiled=True
        ),
    )
    query_index, query_lower = routed_map(query_tokens, routed)
    source_index = routed_map(context_tokens, routed)[0]
    query_rows = jnp.take(query_cols, query_index, axis=0)
    source_rows = jnp.take(source_cols, source_index, axis=0)
    summed = lax.psum(project(query_rows, source_rows, heavy_input), "seq").astype(jnp.bfloat16)
    heavy_heads = attend(
        summed[:, 0].reshape(1, routed, -1, HD),
        summed[:, 1].reshape(1, routed, -1, HD),
        summed[:, 2].reshape(1, routed, -1, HD),
    ).reshape(routed, -1)
    heavy_part = jnp.dot(heavy_heads, heavy_output, preferred_element_type=jnp.float32)
    slot_live = query_tokens >= 0
    compact = query_lower[:, None] + jnp.arange(slot_count, dtype=jnp.int32)[None, :]
    outgoing = jnp.take(heavy_part, jnp.where(slot_live, compact, 0).reshape(-1), axis=0)
    outgoing = jnp.where(slot_live.reshape(-1)[:, None], outgoing, jnp.zeros_like(outgoing))
    returned = lax.all_to_all(
        outgoing.astype(jnp.bfloat16), "seq", split_axis=0, concat_axis=1, tiled=True
    ).astype(outgoing.dtype)
    scaled = returned * query_gate[0][:, None]
    targets = jnp.where(own_queries >= 0, own_queries, tok_rows)
    combined = light_part.at[targets].add(scaled, mode="drop")
    return lax.psum_scatter(combined.astype(jnp.bfloat16), "head", scatter_dimension=1, tiled=True)


def in_vmem(*arrays):
    return tuple(pltpu.with_memory_space_constraint(a, pltpu.VMEM) for a in arrays)


def on_chip(kernel, outs, *arrays, hbm=(), scratch=(), flops=0, moved=0, off=False, kept=()):
    made = [
        (jax.ShapeDtypeStruct if off and i not in kept else pltpu.VMEM)(*o)
        for i, o in enumerate(outs)
    ]
    result = pl.pallas_call(
        kernel,
        in_specs=[pl.BlockSpec(memory_space=pl.ANY)] * len(hbm) + [VMEM] * len(arrays),
        scratch_shapes=list(scratch),
        out_specs=[VMEM] * len(made),
        out_shape=made,
        compiler_params=pltpu.CompilerParams(vmem_limit_bytes=(60 if hbm else 8) << 20),
        cost_estimate=pl.CostEstimate(
            flops=int(flops), bytes_accessed=int(moved), transcendentals=0
        ),
    )(*hbm, *in_vmem(*arrays))
    return result if len(outs) > 1 else result[0]


def listed(count):
    inner = range(count // 4, count - count // 4)
    order = sorted(inner, key=lambda i: (abs(2 * i + 1 - count), -i))
    return order + [i for i in reversed(range(count)) if i not in inner]


def spots(count):
    order = listed(count)
    return [order.index(i) for i in range(count)]


def look_up(values, index):
    found = jnp.int32(values[0])
    for i, value in enumerate(values[1:], 1):
        found = jnp.where(index == i, value, found)
    return found


def own_row(table, index):
    rows = lax.broadcasted_iota(jnp.int32, table.shape, 0)
    return jnp.sum(jnp.where(rows == index, table, 0), axis=0, keepdims=True)


def onehot(flags):
    return flags.astype(F32).astype(BF)


def compact_onehot(table, out_ref):
    shards, slots = table.shape
    spot = spots(shards)
    live = (table >= 0).astype(jnp.int32)
    counts = jnp.sum(live, axis=1, keepdims=True)
    row = lax.broadcasted_iota(jnp.int32, (out_ref.shape[0], slots), 0)
    place = lax.broadcasted_iota(jnp.int32, (1, slots), 1)
    for s in range(shards):
        here = (row == place) & (table[s : s + 1] >= 0)
        out_ref[:, spot[s] * slots : (spot[s] + 1) * slots] = onehot(here)
        place = place + counts[s : s + 1]


def pick_kernel(
    tok_hbm,
    query_hbm,
    source_hbm,
    gate_hbm,
    keep_ref,
    send_ref,
    mine_ref,
    query_map_ref,
    own_map_ref,
    gate_map_ref,
    tok_ref,
    query_ref,
    source_ref,
    gate_ref,
    sems,
):
    ends = (
        (query_hbm, query_ref),
        (source_hbm, source_ref),
        (gate_hbm, gate_ref),
        (tok_hbm, tok_ref),
    )
    copies = [pltpu.make_async_copy(*e, sems.at[i]) for i, e in enumerate(ends)]
    for copy in copies:
        copy.start()
    odd = lax.axis_index("head") % 2
    for copy in copies[:3]:
        copy.wait()
    query, source = query_ref[...], source_ref[...]
    own_q = own_row(query, lax.axis_index("seq"))
    own_s = own_row(source, lax.axis_index("seq"))
    spot = lax.broadcasted_iota(jnp.int32, own_map_ref.shape, 0)
    chosen = [onehot(spot == jnp.where(odd == k, own_q, own_s)) for k in range(2)]
    own_map_ref[...] = onehot(spot == own_q)
    compact_onehot(query, query_map_ref)
    compact_onehot(jnp.where(odd == 0, query, source), mine_ref)
    slots = own_q.shape[1]
    diagonal = lax.broadcasted_iota(jnp.int32, (slots, slots), 0) == lax.broadcasted_iota(
        jnp.int32, (slots, slots), 1
    )
    gate = jnp.sum(jnp.where(diagonal, gate_ref[...], 0.0), axis=1, keepdims=True)
    gate_map_ref[...] = jnp.broadcast_to(gate, gate_map_ref.shape)
    copies[3].wait()
    for ref, rows in zip((keep_ref, send_ref), chosen):
        ref[...] = lax.dot_general(rows, tok_ref[...], FIRST, preferred_element_type=F32).astype(
            BF
        )


def spread_kernel(keep_ref, got_ref, out_ref):
    odd = lax.axis_index("head") % 2
    keep, got = keep_ref[...], got_ref[...]
    width = out_ref.shape[2]
    per = keep.shape[1] // width
    spot = spots(out_ref.shape[0])
    for part, block in enumerate((jnp.where(odd == 0, keep, got), jnp.where(odd == 0, got, keep))):
        for i in range(per):
            for at in range(part * per + i, out_ref.shape[0], 2 * per):
                out_ref[spot[at]] = block[:, i * width : (i + 1) * width]


def compact_kernel(slots_ref, chosen_ref, out_ref):
    rows = slots_ref[...].reshape(-1, slots_ref.shape[2])
    out_ref[...] = jnp.dot(chosen_ref[...], rows, preferred_element_type=F32).astype(BF)


def project_kernel(mine_ref, pair_ref, across_ref, last_ref, weight_ref, out_ref):
    pairs = lax.axis_size("head") // 2
    holder = lax.axis_index("seq") * pairs // lax.axis_size("seq")
    holds = holder == lax.axis_index("head") // 2
    mine = jnp.where(holds, mine_ref[...], across_ref[...])
    other = jnp.where(holds, pair_ref[...], last_ref[...])
    odd = lax.axis_index("head") % 2
    query = jnp.where(odd == 0, mine, other)
    source = jnp.where(odd == 0, other, mine)
    spot = spots(out_ref.shape[0])
    for c, rows in enumerate((query, source, source)):
        part = jnp.dot(rows, weight_ref[c], preferred_element_type=F32).astype(BF)
        for g in range(out_ref.shape[0]):
            out_ref[spot[g], c] = part[:, g * HD : (g + 1) * HD]


def one_head(query, key, value):
    scores = lax.dot_general(query, key, LAST, preferred_element_type=F32) / math.sqrt(HD)
    expanded = jnp.exp(scores - jnp.max(scores, axis=-1, keepdims=True))
    totals = jnp.sum(expanded, axis=-1, keepdims=True)
    weighted = jnp.dot(expanded.astype(BF), value, preferred_element_type=F32)
    return (weighted / totals).astype(BF)


def heavy_attend_kernel(parts_ref, out_ref):
    total = parts_ref[0].astype(F32)
    for s in range(1, parts_ref.shape[0]):
        total = total + parts_ref[s].astype(F32)
    total = total.astype(BF)
    result = one_head(total[0], total[1], total[2])
    for s in range(out_ref.shape[0]):
        out_ref[s] = result


def heavy_output_kernel(heads_ref, weight_ref, chosen_ref, out_ref):
    rows = jnp.concatenate([heads_ref[i] for i in spots(heads_ref.shape[0])], axis=1)
    part = jnp.dot(rows, weight_ref[...], preferred_element_type=F32).astype(BF)
    spread = lax.dot_general(chosen_ref[...], part, FIRST, preferred_element_type=F32).astype(BF)
    out_ref[...] = spread.reshape(out_ref.shape)


def block_of(back_ref, head, per, i):
    spot = spots(back_ref.shape[0])
    return back_ref[look_up(spot[i::per], head)]


def give_kernel(back_ref, out_ref):
    head = lax.axis_index("head")
    per = out_ref.shape[1]
    for k, j in enumerate((1, 3)):
        for i in range(per):
            out_ref[k, i] = block_of(back_ref, head ^ j, per, i)


def far_kernel(back_ref, got_ref, out_ref):
    per = out_ref.shape[0]
    head = lax.axis_index("head")
    for i in range(per):
        mine = block_of(back_ref, head ^ 2, per, i).astype(F32)
        out_ref[i] = (mine + got_ref[1, i].astype(F32)).astype(BF)


def merge_kernel(own, far, out_ref, far_ref, sems):
    copies = [
        pltpu.make_async_copy(own, out_ref, sems.at[0]),
        pltpu.make_async_copy(far, far_ref, sems.at[1]),
    ]
    for copy in copies:
        copy.start()
    for copy in copies:
        copy.wait()
    out_ref[...] = out_ref[...] + far_ref[...].astype(F32)


def finish_kernel(
    light_ref, back_ref, got_ref, last_ref, own_map_ref, gate_ref, out_ref
):
    head = lax.axis_index("head")
    per = last_ref.shape[0]
    chosen, gate = own_map_ref[...], gate_ref[:, :1]
    width = last_ref.shape[2]
    for j in range(per):
        mine = block_of(back_ref, head, per, j).astype(F32)
        scaled = (mine + got_ref[0, j].astype(F32) + last_ref[j].astype(F32)) * gate
        coarse = scaled.astype(BF)
        fine = (scaled - coarse.astype(F32)).astype(BF)
        added = jnp.dot(chosen, coarse, preferred_element_type=F32) + jnp.dot(
            chosen, fine, preferred_element_type=F32
        )
        cols = slice(j * width, (j + 1) * width)
        out_ref[:, cols] = (light_ref[:, cols] + added).astype(BF)


def light_kernel(flips, last, *refs):
    count = len(flips)
    pieces, (w_in, *refs) = refs[:count], refs[count:]
    if last:
        before, w_out, heads_ref, give_ref, before_ref, out_ref, *refs = refs
    else:
        sum_ref, *refs = refs
    tok_ref, in_ref, sems = refs[:3]
    head = lax.axis_index("head")
    depth = pieces[0].shape[1]
    copies = []
    for i, (j, piece) in enumerate(zip(flips, pieces)):
        rows = pl.ds(pl.multiple_of((head ^ j) * depth, depth), depth)
        copies.append(pltpu.make_async_copy(piece, tok_ref.at[i], sems.at[0, i]))
        for c in range(3):
            copies.append(
                pltpu.make_async_copy(w_in.at[c, rows, :], in_ref.at[c, i], sems.at[1 + c, i])
            )
    late = []
    if last:
        late_sems = refs[3]
        width = give_ref.shape[2]
        late.append(pltpu.make_async_copy(before, before_ref, late_sems.at[2]))
        for i, j in enumerate((1, 3)):
            cols = pl.ds(pl.multiple_of((head ^ j) * width, width), width)
            late.append(pltpu.make_async_copy(w_out.at[:, cols], out_ref.at[i], late_sems.at[i]))
    for copy in copies + late:
        copy.start()
    total = [None] * 3
    for i in range(count):
        copies[4 * i].wait()
        for c in range(3):
            copies[4 * i + 1 + c].wait()
            part = jnp.dot(tok_ref[i], in_ref[c, i], preferred_element_type=F32)
            total[c] = part if i == 0 else total[c] + part
    if not last:
        for c in range(3):
            sum_ref[c] = total[c]
        return
    late[0].wait()
    mapped = [(before_ref[c] + total[c]).astype(BF) for c in range(3)]
    for b in range(heads_ref.shape[0] // LB):
        for g in range(heads_ref.shape[1] // HD):
            at = (slice(b * LB, (b + 1) * LB), slice(g * HD, (g + 1) * HD))
            heads_ref[at] = one_head(*(m[at] for m in mapped))
    for i in range(2):
        late[1 + i].wait()
        give_ref[i] = jnp.dot(heads_ref[...], out_ref[i], preferred_element_type=F32).astype(BF)


def light_own_kernel(w_out, got_ref, heads_ref, own_ref, far_ref, out_ref, sems):
    head = lax.axis_index("head")
    width = own_ref.shape[1]
    copies = []
    for i, j in enumerate((0, 2)):
        cols = pl.ds(pl.multiple_of((head ^ j) * width, width), width)
        copies.append(pltpu.make_async_copy(w_out.at[:, cols], out_ref.at[i], sems.at[i]))
    for copy in copies:
        copy.start()
    for i, ref in enumerate((own_ref, far_ref)):
        copies[i].wait()
        block = jnp.dot(heads_ref[...], out_ref[i], preferred_element_type=F32)
        ref[...] = (block + got_ref[i].astype(F32)).astype(ref.dtype)


def light_call(flips, last, outs, pieces, *arrays, scratch=()):
    count = len(flips)
    rows, width = pieces[0].shape
    return on_chip(
        functools.partial(light_kernel, flips, last),
        outs,
        hbm=(*pieces, *arrays),
        scratch=[
            *scratch,
            pltpu.VMEM((count, rows, width), BF),
            pltpu.VMEM((3, count, width, arrays[0].shape[2]), BF),
            pltpu.SemaphoreType.DMA((4, count)),
            pltpu.SemaphoreType.DMA((3,)),
        ],
        flops=6 * count * rows * width * arrays[0].shape[2],
        off=True,
        kept=(0,) if last else (),
    )


def one_head_a_device(
    tokens,
    light_input,
    light_output,
    heavy_input,
    heavy_output,
    query_tokens,
    context_tokens,
    query_gate,
):
    seq_count, head_count = lax.axis_size("seq"), lax.axis_size("head")
    tok_rows, own_width = tokens.shape
    slots = query_tokens.shape[1]
    routed = seq_count * tok_rows // ROUTE
    part_width, head_cols = heavy_input.shape[1:]
    out_cols = heavy_output.shape[1]
    light_cols = light_input.shape[2]
    per = seq_count // head_count
    pair, across = ([(i, i ^ j) for i in range(head_count)] for j in (1, 2))

    def swap(x):
        return lax.all_to_all(
            x,
            "seq",
            split_axis=0,
            concat_axis=0,
            tiled=True,
            axis_index_groups=[listed(seq_count)],
        )

    routes = (routed, seq_count * slots)
    keep, send, mine_map, query_map, own_map, gate_map = on_chip(
        pick_kernel,
        [((slots, own_width), BF)] * 2
        + [(routes, BF)] * 2
        + [((tok_rows, slots), BF), ((slots, HD), F32)],
        hbm=(tokens, query_tokens, context_tokens, query_gate),
        scratch=[
            pltpu.VMEM(tokens.shape, BF),
            pltpu.VMEM(query_tokens.shape, jnp.int32),
            pltpu.VMEM(context_tokens.shape, jnp.int32),
            pltpu.VMEM(query_gate.shape, F32),
            pltpu.SemaphoreType.DMA((4,)),
        ],
    )
    got = lax.ppermute(send, "head", pair)
    spread = on_chip(spread_kernel, [((seq_count, slots, part_width), BF)], keep, got)
    token_far = lax.ppermute(tokens, "head", across)
    token_pair = lax.ppermute(tokens, "head", pair)
    spread, tokens, token_pair = lax.optimization_barrier((spread, tokens, token_pair))
    light_sum = light_call(
        (0, 1),
        False,
        [((3, tok_rows, light_cols), F32)],
        (tokens, token_pair),
        light_input,
    )
    spread = swap(spread)
    spread, token_far, light_sum = lax.optimization_barrier((spread, token_far, light_sum))
    token_last = lax.ppermute(token_far, "head", pair)
    mine = on_chip(compact_kernel, [((routed, part_width), BF)], spread, mine_map, moved=20 << 20)
    diagonal = [(i, i ^ 3) for i in range(head_count)]
    rows = [mine, *(lax.ppermute(mine, "head", p) for p in (pair, across, diagonal))]
    parts = on_chip(
        project_kernel, [((seq_count, 3, routed, HD), BF)], *rows, heavy_input
    )

    parts, light_sum, token_far, token_last = lax.optimization_barrier(
        (parts, light_sum, token_far, token_last)
    )
    light_heads, light_give = light_call(
        (2, 3),
        True,
        [((tok_rows, light_cols), BF), ((2, tok_rows, own_width), BF)],
        (token_far, token_last),
        light_input,
        light_sum,
        light_output,
        scratch=[
            pltpu.VMEM((3, tok_rows, light_cols), F32),
            pltpu.VMEM((2, light_cols, own_width), BF),
        ],
    )
    parts = swap(parts)
    parts, light_heads, light_give = lax.optimization_barrier((parts, light_heads, light_give))
    light_got = lax.ppermute(light_give, "head", pair)
    heads = on_chip(heavy_attend_kernel, [((seq_count, routed, HD), BF)], parts)
    light_own, light_far = on_chip(
        light_own_kernel,
        [((tok_rows, own_width), F32), ((tok_rows, own_width), BF)],
        light_got,
        light_heads,
        hbm=(light_output,),
        scratch=[pltpu.VMEM((2, light_cols, own_width), BF), pltpu.SemaphoreType.DMA((2,))],
        flops=4 * tok_rows * light_cols * own_width,
        off=True,
    )
    heads = swap(heads)
    far_sent = lax.ppermute(light_far, "head", across)
    heads, light_own, light_far = lax.optimization_barrier((heads, light_own, light_far))
    light_far = far_sent

    back = on_chip(
        heavy_output_kernel,
        [((seq_count, slots, out_cols), BF)],
        heads,
        heavy_output,
        query_map,
    )
    back = swap(back)
    back, light_far = lax.optimization_barrier((back, light_far))
    give = on_chip(give_kernel, [((2, per, slots, out_cols), BF)], back)
    give, light_own, light_far = lax.optimization_barrier((give, light_own, light_far))
    light = on_chip(
        merge_kernel,
        [((tok_rows, own_width), F32)],
        hbm=(light_own, light_far),
        scratch=[pltpu.VMEM((tok_rows, own_width), BF), pltpu.SemaphoreType.DMA((2,))],
    )
    got = lax.ppermute(give, "head", pair)
    far = on_chip(far_kernel, [((per, slots, out_cols), BF)], back, got)
    last = lax.ppermute(far, "head", across)
    return on_chip(
        finish_kernel,
        [((tok_rows, own_width), BF)],
        light,
        back,
        got,
        last,
        own_map,
        gate_map,
        off=True,
    )


def solution(mesh):
    placed = (
        P("seq", "head"),
        P(None, None, "head"),
        P("head", None),
        P(None, "seq", "head"),
        P("head", "seq"),
        P(),
        P(),
        P("seq", None),
    )

    def per_device(*args):
        seq_count, head_count = mesh.shape["seq"], mesh.shape["head"]
        local_heads = args[3].shape[2] // HD
        fits = head_count // 2 == 2 and seq_count % head_count == 0 and local_heads == seq_count
        return (one_head_a_device if fits else general)(*args)

    return jax.shard_map(
        per_device, mesh=mesh, in_specs=placed, out_specs=P("seq", "head"), check_vma=False
    )
```
